256 devices in a mesh: seq: 64 (over z, y, core), mp: 4 (over x).
Axes of the slice: x: 4, y: 4, z: 8, core: 2. Of those that a mesh axis runs over, the one named last changes fastest.
Arguments:
- latents: bfloat16 [16384, 1536], P('seq'), may hold values from -6 to 6
- w_query: bfloat16 [1536, 1536], P(None, 'mp'), may hold values from -0.15625 to 0.15625
- w_key: bfloat16 [1536, 1536], P(None, 'mp'), may hold values from -0.15625 to 0.15625
- w_value: bfloat16 [1536, 1536], P(None, 'mp'), may hold values from -0.15625 to 0.15625
- w_out: bfloat16 [1536, 1536], P('mp'), may hold values from -0.15625 to 0.15625
- head_gain: float32 [1536], P('mp'), may hold values from 0.25 to 1.75
- grad_out: bfloat16 [16384, 1536], P('seq', 'mp'), may hold values from -6 to 6
Outputs:
- branch: bfloat16 [16384, 1536], P('seq', 'mp')
- d_latents: bfloat16 [16384, 1536], P('seq', 'mp')
The draws below stay inside these ranges and needn't reach their ends.
All inputs are finite; a program needn't handle non-finite values.
Results may differ from the reference program's by a relative error of at most 0.013.
Values may be sent and summed in bfloat16 or wider, within the bound.
No kernel may reach another device: no remote copies, remote signals or barrier semaphores. Data moves between devices by JAX's collectives and lax.ppermute only.
A program may use at most 64 MiB of HBM per device.

```python
import jax
import jax.numpy as jnp
from jax import lax

D = 1536
HEADS = 24
HD = 64
LENGTH = 16384
N_MP = 4


def shard_levels(stream_key, dims, shards, least, high):
    level, own = 1.0, jax.random.fold_in(stream_key, 6)
    for position, shards_of in shards:
        heights = jnp.exp(jax.random.uniform(jax.random.fold_in(own, position), (shards_of,), jnp.float32, least / len(shards), high / len(shards)))
        level = level * jnp.repeat(heights, dims[position] // shards_of).reshape([-1 if axis == position else 1 for axis in range(len(dims))])
    return level


def gaussian(key, dims, scale, most, split=(), kind=jnp.bfloat16):
    values = scale * jax.random.normal(key, dims, jnp.float32)
    if split:
        values = values * shard_levels(key, dims, split, -0.22, 0.18)
    return jnp.clip(values, -most, most).astype(kind)


def setup_inputs(seed: int = 0) -> dict:
    key_of = jax.random.split(jax.random.key(seed), 8)
    latents = gaussian(key_of[0], (LENGTH, D), 1.0, 6.0, ((0, 64),))
    w_query = gaussian(key_of[1], (D, D), D ** -0.5, 0.15625, ((1, 4),))
    w_key = gaussian(key_of[2], (D, D), D ** -0.5, 0.15625, ((1, 4),))
    w_value = gaussian(key_of[3], (D, D), D ** -0.5, 0.15625, ((1, 4),))
    w_out = gaussian(key_of[4], (D, D), D ** -0.5, 0.15625, ((0, 4),))
    head_gain = jnp.clip(1.0 + 0.15 * jax.random.normal(key_of[5], (D,), jnp.float32), 0.25, 1.75)
    grad_out = gaussian(key_of[6], (LENGTH, D), 1.0, 6.0, ((0, 64), (1, 4)))
    return dict(latents=latents, w_query=w_query, w_key=w_key, w_value=w_value, w_out=w_out, head_gain=head_gain, grad_out=grad_out)


highest_precision = lax.Precision.HIGHEST
epsilon = 1e-06

def feature_map(inputs):
    return jnp.where(inputs > 0, inputs + 1.0, jnp.exp(jnp.minimum(inputs, 0.0)))

def feature_slope(inputs):
    return jnp.where(inputs > 0, jnp.ones_like(inputs), jnp.exp(jnp.minimum(inputs, 0.0)))

def causal_table(block_rows):
    return (jnp.arange(block_rows)[:, None] >= jnp.arange(block_rows)[None, :]).astype(jnp.float32)

def reference(latents, w_query, w_key, w_value, w_out, head_gain, grad_out):
    total_rows = latents.shape[0]
    query_raw = jnp.dot(latents, w_query, preferred_element_type=jnp.float32).reshape(total_rows, HEADS, HD)
    key_raw = jnp.dot(latents, w_key, preferred_element_type=jnp.float32).reshape(total_rows, HEADS, HD)
    value_matrix = jnp.dot(latents, w_value, preferred_element_type=jnp.float32).reshape(total_rows, HEADS, HD)
    mapped_query = feature_map(query_raw)
    mapped_key = feature_map(key_raw)
    block_rows = min(512, total_rows)
    block_count = total_rows // block_rows
    causal_mask = causal_table(block_rows)

    def blocked(array):
        return array.reshape(block_count, block_rows, HEADS, HD)

    def forward_step(running_state, inputs):
        mapped_query_block, mapped_key_block, value_block = inputs
        score_matrix = jnp.einsum('thk,shk->hts', mapped_query_block, mapped_key_block, precision=highest_precision) * causal_mask
        unnormed_block = jnp.einsum('hts,shv->thv', score_matrix, value_block, precision=highest_precision)
        unnormed_block = unnormed_block + jnp.einsum('lsd,sdq->lsq', mapped_query_block, running_state, precision=highest_precision)
        updated_state = running_state + jnp.einsum('omw,omd->mwd', mapped_key_block, value_block, precision=highest_precision)
        return (updated_state, (unnormed_block, running_state))
    initial = jnp.zeros((HEADS, HD, HD), jnp.float32)
    _, (raw_blocks, befores) = lax.scan(forward_step, initial, (blocked(mapped_query), blocked(mapped_key), blocked(value_matrix)))
    raw = raw_blocks.reshape(total_rows, HEADS, HD)
    inv_scale = lax.rsqrt(lax.optimization_barrier(jnp.mean(raw * raw, axis=-1, keepdims=True)) + epsilon)
    gain_rows = head_gain.reshape(HEADS, HD)
    attn = (raw * inv_scale * gain_rows).astype(jnp.bfloat16).reshape(total_rows, D)
    group_width = D // N_MP
    summed = jnp.zeros((total_rows, D), jnp.float32)
    for group in range(N_MP):
        lower = group * group_width
        partial_out = jnp.dot(attn[:, lower:lower + group_width], w_out[lower:lower + group_width], preferred_element_type=jnp.float32)
        summed = summed + lax.optimization_barrier(partial_out.astype(jnp.bfloat16)).astype(jnp.float32)
    branch = summed.astype(jnp.bfloat16)
    contract = (((1,), (1,)), ((), ()))
    d_attn = lax.dot_general(grad_out, w_out, contract, preferred_element_type=jnp.float32).reshape(total_rows, HEADS, HD)
    upstream = d_attn * gain_rows
    row_stat = lax.optimization_barrier(jnp.mean(raw * upstream, axis=-1, keepdims=True))
    unnormed_gradient = inv_scale * upstream - inv_scale * inv_scale * inv_scale * raw * row_stat

    def backward_step(running_state, inputs):
        mapped_query_block, mapped_key_block, value_block, unnormed_block_gradient, prior_state_sum = inputs
        score_matrix = jnp.einsum('thk,shk->hts', mapped_query_block, mapped_key_block, precision=highest_precision) * causal_mask
        mixed_output = jnp.einsum('thv,shv->hts', unnormed_block_gradient, value_block, precision=highest_precision) * causal_mask
        feature_query_gradient = jnp.einsum('fui,ifc->ufc', mixed_output, mapped_key_block, precision=highest_precision) + jnp.einsum('pue,ure->pur', unnormed_block_gradient, prior_state_sum, precision=highest_precision)
        feature_key_gradient = jnp.einsum('xbc,bxj->cxj', mixed_output, mapped_query_block, precision=highest_precision) + jnp.einsum('wqj,qtj->wqt', value_block, running_state, precision=highest_precision)
        value_gradient = jnp.einsum('fud,ufx->dfx', score_matrix, unnormed_block_gradient, precision=highest_precision) + jnp.einsum('eul,ulw->euw', mapped_key_block, running_state, precision=highest_precision)
        updated_state = running_state + jnp.einsum('wei,wej->eij', mapped_query_block, unnormed_block_gradient, precision=highest_precision)
        return (updated_state, (feature_query_gradient, feature_key_gradient, value_gradient))
    _, (feature_query_gradient, feature_key_gradient, value_gradient) = lax.scan(backward_step, initial, (blocked(mapped_query), blocked(mapped_key), blocked(value_matrix), blocked(unnormed_gradient), befores), reverse=True)
    d_query = (feature_query_gradient.reshape(total_rows, HEADS, HD) * feature_slope(query_raw)).astype(jnp.bfloat16).reshape(total_rows, D)
    d_key = (feature_key_gradient.reshape(total_rows, HEADS, HD) * feature_slope(key_raw)).astype(jnp.bfloat16).reshape(total_rows, D)
    d_value = value_gradient.reshape(total_rows, D).astype(jnp.bfloat16)
    summed_in = jnp.zeros((total_rows, D), jnp.float32)
    for group in range(N_MP):
        lower = group * group_width
        upper = lower + group_width
        partial_in = lax.dot_general(d_query[:, lower:upper], w_query[:, lower:upper], contract, preferred_element_type=jnp.float32)
        partial_in = partial_in + lax.dot_general(d_key[:, lower:upper], w_key[:, lower:upper], contract, preferred_element_type=jnp.float32)
        partial_in = partial_in + lax.dot_general(d_value[:, lower:upper], w_value[:, lower:upper], contract, preferred_element_type=jnp.float32)
        summed_in = summed_in + lax.optimization_barrier(partial_in.astype(jnp.bfloat16)).astype(jnp.float32)
    d_latents = summed_in.astype(jnp.bfloat16)
    return (branch, d_latents)
```

```python
import jax
import jax.numpy as jnp
from jax import lax
from jax.sharding import Mesh
from jax.sharding import PartitionSpec as P

HD = 64
SEQ = ("seq_0", "seq_1", "seq_2")


epsilon = 1e-06


def shifts(count, step):
    return [(i, (i + step) % count) for i in range(count)]


SWAP = [(0, 1), (1, 0)]


def seq_before(state, later):
    z, y, c = (lax.axis_index(a) for a in SEQ)
    if later:
        z, y, c = (7 - z, 3 - y, 1 - c)
    side = lax.axis_index("seq_2")
    half = state.shape[0] // 2
    low, high = (state[:half], state[half:])
    own = jnp.where(side == 0, low, high)
    other = jnp.where(side == 0, high, low)
    pair = lax.ppermute(other.astype(jnp.bfloat16), "seq_2", SWAP).astype(jnp.float32)
    chip = own + pair
    chip16 = chip.astype(jnp.bfloat16)
    plane, inside = (chip, jnp.zeros_like(chip))
    for k in (1, 2, 3):
        step = -k if later else k
        got = lax.ppermute(chip16, "seq_1", shifts(4, step)).astype(jnp.float32)
        plane = plane + got
        inside = inside + jnp.where(y >= k, got, 0.0)
    planes = lax.all_to_all(
        jnp.broadcast_to(plane.astype(jnp.bfloat16)[None], (8, *plane.shape)), "seq_0", 0, 0, tiled=True
    ).astype(jnp.float32)
    order = jnp.arange(8)
    order = 7 - order if later else order
    inside = inside + jnp.sum(jnp.where((order < z)[:, None, None], planes, 0.0), axis=0)
    send = inside + jnp.where(c == 0, own, 0.0)
    got = lax.ppermute(send.astype(jnp.bfloat16), "seq_2", SWAP).astype(jnp.float32)
    mine = inside + jnp.where(c == 1, pair, 0.0)
    first, second = (jnp.where(side == 0, mine, got), jnp.where(side == 0, got, mine))
    return jnp.concatenate([first, second], axis=0)


def packed_scan(state, later):
    heads = state.shape[0]
    flat = state.reshape(heads * HD * HD // 128, 128)
    return seq_before(flat, later).reshape(state.shape)


def split_up(x, dim, devices):
    before, after = (x.shape[:dim], x.shape[dim + 1 :])
    return jnp.moveaxis(x.reshape(*before, devices, -1, *after), dim, 0)


def sum_at_owner(x, axis, dim):
    devices = lax.axis_size(axis)
    parts = lax.all_to_all(split_up(x, dim, devices), axis, 0, 0, tiled=True)
    return jnp.sum(parts.astype(jnp.float32), axis=0)


def copy_for_each(x, axis):
    devices = lax.axis_size(axis)
    return lax.all_to_all(jnp.broadcast_to(x[None], (devices, *x.shape)), axis, 0, 0, tiled=True)


def in_order(parts, dim):
    parts = jnp.moveaxis(parts, 0, dim)
    dims = parts.shape
    return parts.reshape(*dims[:dim], dims[dim] * dims[dim + 1], *dims[dim + 2 :])


def gathered_copies(x, axis, dim):
    parts = copy_for_each(x, axis)
    return in_order(parts, dim)


def feature_map(inputs):
    return jnp.where(inputs > 0, inputs + 1.0, jnp.exp(jnp.minimum(inputs, 0.0)))


def feature_slope(inputs):
    return jnp.where(inputs > 0, jnp.ones_like(inputs), jnp.exp(jnp.minimum(inputs, 0.0)))


def causal_table(block_rows):
    return (jnp.arange(block_rows)[:, None] >= jnp.arange(block_rows)[None, :]).astype(jnp.float32)


def per_device(latents, w_query, w_key, w_value, w_out, head_gain, grad_out):
    row_count = latents.shape[0]
    local_width = w_query.shape[1]
    local_heads = local_width // HD
    query_raw = jnp.dot(latents, w_query, preferred_element_type=jnp.float32).reshape(
        row_count, local_heads, HD
    )
    key_raw = jnp.dot(latents, w_key, preferred_element_type=jnp.float32).reshape(
        row_count, local_heads, HD
    )
    value_matrix = jnp.dot(latents, w_value, preferred_element_type=jnp.float32).reshape(
        row_count, local_heads, HD
    )
    mapped_query = feature_map(query_raw)
    mapped_key = feature_map(key_raw)
    forward_state_local = jnp.einsum("omw,omd->mwd", mapped_key, value_matrix)
    prefix_state = packed_scan(forward_state_local, False)
    block_rows = min(512, row_count)
    block_count = row_count // block_rows
    causal_mask = causal_table(block_rows)

    def blocked(array):
        return array.reshape(block_count, block_rows, local_heads, HD)

    def forward_step(running_state, inputs):
        mapped_query_block, mapped_key_block, value_block = inputs
        score_matrix = (
            jnp.einsum("thk,shk->hts", mapped_query_block, mapped_key_block) * causal_mask
        )
        unnormed_block = jnp.einsum("hts,shv->thv", score_matrix, value_block)
        unnormed_block = unnormed_block + jnp.einsum(
            "lsd,sdq->lsq", mapped_query_block, running_state
        )
        updated_state = running_state + jnp.einsum("omw,omd->mwd", mapped_key_block, value_block)
        return (updated_state, (unnormed_block, running_state))

    _, forward_out = lax.scan(
        forward_step,
        prefix_state,
        (blocked(mapped_query), blocked(mapped_key), blocked(value_matrix)),
    )
    raw = forward_out[0].reshape(row_count, local_heads, HD)
    befores = forward_out[1]
    inv_scale = lax.rsqrt(jnp.mean(raw * raw, axis=-1, keepdims=True) + epsilon)
    gain_rows = head_gain.reshape(local_heads, HD)
    attn = (raw * inv_scale * gain_rows).astype(jnp.bfloat16).reshape(row_count, local_width)
    partial_out = jnp.dot(attn, w_out, preferred_element_type=jnp.float32)
    branch = sum_at_owner(partial_out.astype(jnp.bfloat16), "mp", 1).astype(jnp.bfloat16)
    contract = (((1,), (1,)), ((), ()))
    d_attn = lax.dot_general(
        gathered_copies(grad_out, "mp", 1), w_out, contract, preferred_element_type=jnp.float32
    )
    upstream = d_attn.reshape(row_count, local_heads, HD) * gain_rows
    row_stat = jnp.mean(raw * upstream, axis=-1, keepdims=True)
    unnormed_gradient = inv_scale * upstream - inv_scale * inv_scale * inv_scale * raw * row_stat
    reverse_state_local = jnp.einsum("wei,wej->eij", mapped_query, unnormed_gradient)
    suffix_state = packed_scan(reverse_state_local, True)

    def backward_step(running_state, inputs):
        (
            mapped_query_block,
            mapped_key_block,
            value_block,
            unnormed_block_gradient,
            prior_state_sum,
        ) = inputs
        score_matrix = (
            jnp.einsum("thk,shk->hts", mapped_query_block, mapped_key_block) * causal_mask
        )
        mixed_output = (
            jnp.einsum("thv,shv->hts", unnormed_block_gradient, value_block) * causal_mask
        )
        feature_query_gradient = jnp.einsum(
            "fui,ifc->ufc", mixed_output, mapped_key_block
        ) + jnp.einsum("pue,ure->pur", unnormed_block_gradient, prior_state_sum)
        feature_key_gradient = jnp.einsum(
            "xbc,bxj->cxj", mixed_output, mapped_query_block
        ) + jnp.einsum("wqj,qtj->wqt", value_block, running_state)
        value_gradient = jnp.einsum(
            "fud,ufx->dfx", score_matrix, unnormed_block_gradient
        ) + jnp.einsum("eul,ulw->euw", mapped_key_block, running_state)
        updated_state = running_state + jnp.einsum(
            "wei,wej->eij", mapped_query_block, unnormed_block_gradient
        )
        return (updated_state, (feature_query_gradient, feature_key_gradient, value_gradient))

    backward_in = (
        blocked(mapped_query),
        blocked(mapped_key),
        blocked(value_matrix),
        blocked(unnormed_gradient),
        befores,
    )
    _, (feature_query_gradient, feature_key_gradient, value_gradient) = lax.scan(
        backward_step, suffix_state, backward_in, reverse=True
    )
    d_query = (
        (feature_query_gradient.reshape(row_count, local_heads, HD) * feature_slope(query_raw))
        .astype(jnp.bfloat16)
        .reshape(row_count, local_width)
    )
    d_key = (
        (feature_key_gradient.reshape(row_count, local_heads, HD) * feature_slope(key_raw))
        .astype(jnp.bfloat16)
        .reshape(row_count, local_width)
    )
    d_value = value_gradient.reshape(row_count, local_width).astype(jnp.bfloat16)
    partial_in = lax.dot_general(d_query, w_query, contract, preferred_element_type=jnp.float32)
    partial_in = partial_in + lax.dot_general(
        d_key, w_key, contract, preferred_element_type=jnp.float32
    )
    partial_in = partial_in + lax.dot_general(
        d_value, w_value, contract, preferred_element_type=jnp.float32
    )
    d_latents = sum_at_owner(partial_in.astype(jnp.bfloat16), "mp", 1).astype(jnp.bfloat16)
    return (branch, d_latents)


def solution(mesh):
    split = Mesh(mesh.devices.reshape(8, 4, 2, mesh.shape["mp"]), ("seq_0", "seq_1", "seq_2", "mp"))
    in_specs = (
        P(SEQ, None),
        P(None, "mp"),
        P(None, "mp"),
        P(None, "mp"),
        P("mp", None),
        P("mp"),
        P(SEQ, "mp"),
    )
    out_specs = (P(SEQ, "mp"), P(SEQ, "mp"))
    return jax.shard_map(
        per_device, mesh=split, in_specs=in_specs, out_specs=out_specs, check_vma=False
    )
```

```python
import functools

import jax
import jax.numpy as jnp
from jax import lax
from jax.experimental import pallas as pl
from jax.experimental.pallas import tpu as pltpu
from jax.sharding import Mesh
from jax.sharding import PartitionSpec as P

HD = 64
LANES = 128
SEQ = ("seq_0", "seq_1", "seq_2")
SWAP = [(0, 1), (1, 0)]
epsilon = 1e-06
f32, bf16 = (jnp.float32, jnp.bfloat16)
NT = (((1,), (1,)), ((), ()))
TN = (((0,), (0,)), ((), ()))
VMEM = pl.BlockSpec(memory_space=pltpu.VMEM)


def shifts(count, step):
    return [(i, (i + step) % count) for i in range(count)]


def mm(a, b, contract=(((1,), (0,)), ((), ()))):
    return lax.dot_general(a, b, contract, preferred_element_type=f32)


def call(body, outs, flops, moved, **extra):
    return pl.pallas_call(
        body,
        out_shape=[jax.ShapeDtypeStruct(s, d) for s, d in outs],
        cost_estimate=pl.CostEstimate(flops=flops, bytes_accessed=moved, transcendentals=0),
        compiler_params=pltpu.CompilerParams(vmem_limit_bytes=20 * 1024 * 1024),
        **extra,
    )


def plain(body, outs, flops, moved, *args):
    return call(
        body, outs, flops, moved, in_specs=[VMEM] * len(args), out_specs=[VMEM] * len(outs)
    )(*args)


def feature_map(u):
    return jnp.where(u > 0, u + 1.0, jnp.exp(jnp.minimum(u, 0.0)))


def low_lanes(shape):
    return lax.broadcasted_iota(jnp.int32, shape, len(shape) - 1) < HD


def one_head(x, head):
    low = low_lanes(x.shape)
    keep = low if head == 0 else jnp.logical_not(low)
    return jnp.where(keep, x, jnp.zeros_like(x))


def pack(full):
    return jnp.where(low_lanes((HD, LANES)), full[:HD], full[HD:])


def unpack(rows):
    low = low_lanes((HD, LANES))
    zero = jnp.zeros_like(rows)
    return jnp.concatenate([jnp.where(low, rows, zero), jnp.where(low, zero, rows)], axis=0)


def head_ones():
    r = lax.broadcasted_iota(jnp.int32, (LANES, LANES), 0) < HD
    c = lax.broadcasted_iota(jnp.int32, (LANES, LANES), 1) < HD
    return jnp.where(r == c, 1.0, 0.0).astype(bf16)


def split_state(state_ref, own_ref, other_ref):
    half = own_ref.shape[0]
    side = lax.axis_index("seq_2")
    own_ref[...] = state_ref[pl.ds(pl.multiple_of(side * half, 16), half), :]
    other_ref[...] = state_ref[pl.ds(pl.multiple_of((1 - side) * half, 16), half), :].astype(bf16)


def whole_state(later, inside_ref, pair_ref, got_ref, state_ref):
    half = inside_ref.shape[0]
    side = lax.axis_index("seq_2")
    last = side == (0 if later else 1)
    mine = inside_ref[...] + jnp.where(last, pair_ref[...].astype(f32), 0.0)
    state_ref[pl.ds(pl.multiple_of(side * half, 16), half), :] = mine
    state_ref[pl.ds(pl.multiple_of((1 - side) * half, 16), half), :] = got_ref[...].astype(f32)


def seq_before(later, own, other):
    half = own.shape[0]
    pair = lax.ppermute(other, "seq_2", SWAP)

    def add_pair(own_ref, pair_ref, chip_ref):
        chip_ref[...] = (own_ref[...] + pair_ref[...].astype(f32)).astype(bf16)

    (chip,) = plain(add_pair, [((half, LANES), bf16)], 1, half * 1024, own, pair)
    got = [lax.ppermute(chip, "seq_1", shifts(4, -k if later else k)) for k in (1, 2, 3)]

    def add_plane(own_ref, pair_ref, g1, g2, g3, inside_ref, planes_ref):
        y = lax.axis_index("seq_1")
        y = 3 - y if later else y
        total = own_ref[...] + pair_ref[...].astype(f32)
        inside = jnp.zeros_like(total)
        for k, ref in ((1, g1), (2, g2), (3, g3)):
            piece = ref[...].astype(f32)
            total = total + piece
            inside = inside + jnp.where(y >= k, piece, 0.0)
        inside_ref[...] = inside
        planes_ref[...] = jnp.broadcast_to(total.astype(bf16)[None], planes_ref.shape)

    in_plane, planes = plain(
        add_plane,
        [((half, LANES), f32), ((8, half, LANES), bf16)],
        1,
        half * 4096,
        own,
        pair,
        *got,
    )
    planes = lax.all_to_all(planes, "seq_0", 0, 0, tiled=True)

    def add_planes(inside_ref, own_ref, planes_ref, out_ref, send_ref):
        z = lax.axis_index("seq_0")
        first = lax.axis_index("seq_2") == (1 if later else 0)
        total = inside_ref[...]
        for k in range(8):
            take = (k > z) if later else (k < z)
            total = total + jnp.where(take, planes_ref[k].astype(f32), 0.0)
        out_ref[...] = total
        send_ref[...] = (total + jnp.where(first, own_ref[...], 0.0)).astype(bf16)

    inside, send = plain(
        add_planes,
        [((half, LANES), f32), ((half, LANES), bf16)],
        1,
        half * 4096,
        in_plane,
        own,
        planes,
    )
    return inside, pair, lax.ppermute(send, "seq_2", SWAP), in_plane, chip


def key_value(latents, w_key, w_value):
    rows, width = (latents.shape[0], w_key.shape[1])
    half = width * HD // LANES // 2
    steps = 3
    depth = latents.shape[1] // steps

    def body(x_ref, wk_ref, wv_ref, fk_ref, v_ref, own_ref, other_ref, k_acc, v_acc, state):
        step = pl.program_id(0)

        @pl.when(step == 0)
        def _():
            k_acc[...] = jnp.zeros_like(k_acc)
            v_acc[...] = jnp.zeros_like(v_acc)

        x = x_ref[...]
        k_acc[...] += mm(x, wk_ref[...])
        v_acc[...] += mm(x, wv_ref[...])

        @pl.when(step == steps - 1)
        def _():
            fk_ref[...] = feature_map(k_acc[...]).astype(bf16)
            v_ref[...] = v_acc[...].astype(bf16)
            for p in range(width // LANES):
                cols = slice(p * LANES, (p + 1) * LANES)
                state[p * HD : (p + 1) * HD, :] = pack(mm(fk_ref[:, cols], v_ref[:, cols], TN))
            split_state(state, own_ref, other_ref)

    fixed = lambda i: (0, 0)
    return call(
        body,
        [((rows, width), bf16), ((rows, width), bf16), ((half, LANES), f32), ((half, LANES), bf16)],
        4 * rows * width * latents.shape[1],
        3 * 1024 * 1024,
        grid=(steps,),
        in_specs=[
            pl.BlockSpec((rows, depth), lambda i: (0, i)),
            pl.BlockSpec((depth, width), lambda i: (i, 0)),
            pl.BlockSpec((depth, width), lambda i: (i, 0)),
        ],
        out_specs=[
            pl.BlockSpec((rows, width), fixed),
            pl.BlockSpec((rows, width), fixed),
            pl.BlockSpec((half, LANES), fixed),
            pl.BlockSpec((half, LANES), fixed),
        ],
        scratch_shapes=[
            pltpu.VMEM((rows, width), f32),
            pltpu.VMEM((rows, width), f32),
            pltpu.VMEM((2 * half, LANES), f32),
        ],
    )(latents, w_key, w_value)


def tri(rows, upper):
    t = lax.broadcasted_iota(jnp.int32, (rows, rows), 0)
    s = lax.broadcasted_iota(jnp.int32, (rows, rows), 1)
    return (t <= s) if upper else (t >= s)


def masked(scores, keep):
    return jnp.where(keep, scores, 0.0).astype(bf16)


def query_local(latents, w_query, fk, v):
    rows, width = fk.shape

    def body(x_ref, wq_ref, fk_ref, v_ref, fq_ref, raw_ref):
        fq_ref[...] = feature_map(mm(x_ref[...], wq_ref[...])).astype(bf16)
        keep = tri(rows, False)
        for p in range(width // LANES):
            cols = slice(p * LANES, (p + 1) * LANES)
            q, k, val = (fq_ref[:, cols], fk_ref[:, cols], v_ref[:, cols])
            total = None
            for h in (0, 1):
                score = masked(mm(q, one_head(k, h), NT), keep)
                part = mm(score, one_head(val, h))
                total = part if total is None else total + part
            raw_ref[:, cols] = total

    return plain(
        body,
        [((rows, width), bf16), ((rows, width), f32)],
        2 * rows * width * (latents.shape[1] + 4 * rows),
        3 * 1024 * 1024,
        latents,
        w_query,
        fk,
        v,
    )


def upstream_of(grads, w_out, gain):
    rows, width = grads[0].shape

    def body(g0, g1, g2, g3, w_ref, gain_ref, up_ref):
        m = lax.axis_index("mp")
        total = jnp.zeros((rows, width), f32)
        for k, ref in enumerate((g0, g1, g2, g3)):
            at = lax.rem(m + 4 - k, 4) * width
            total = total + mm(ref[...], w_ref[:, pl.ds(pl.multiple_of(at, LANES), width)], NT)
        up_ref[...] = total * gain_ref[...]

    return plain(
        body,
        [((rows, width), f32)],
        8 * rows * width * width,
        3 * 1024 * 1024,
        *grads,
        w_out,
        gain,
    )[0]


def normed(inside, pair, got, fq, raw_local, up, gain):
    rows, width = fq.shape
    half = inside.shape[0]

    def body(
        inside_ref,
        pair_ref,
        got_ref,
        fq_ref,
        raw_ref,
        up_ref,
        gain_ref,
        attn_ref,
        draw_ref,
        before_ref,
        own_ref,
        other_ref,
        state,
    ):
        whole_state(False, inside_ref, pair_ref, got_ref, state)
        before_ref[...] = state[...].astype(bf16)
        ones = head_ones()
        for p in range(width // LANES):
            cols = slice(p * LANES, (p + 1) * LANES)
            q = fq_ref[:, cols]
            raw = raw_ref[:, cols] + mm(q, unpack(before_ref[p * HD : (p + 1) * HD, :]))
            upstream = up_ref[:, cols]
            square = mm((raw * raw).astype(bf16), ones) * (1.0 / HD)
            cross = mm((raw * upstream).astype(bf16), ones) * (1.0 / HD)
            inv = lax.rsqrt(square + epsilon)
            unit = raw * inv
            attn_ref[:, cols] = (unit * gain_ref[:, cols]).astype(bf16)
            draw = (inv * upstream - inv * inv * unit * cross).astype(bf16)
            draw_ref[:, cols] = draw
            state[p * HD : (p + 1) * HD, :] = pack(mm(q, draw, TN))
        split_state(state, own_ref, other_ref)

    return call(
        body,
        [
            ((rows, width), bf16),
            ((rows, width), bf16),
            ((2 * half, LANES), bf16),
            ((half, LANES), f32),
            ((half, LANES), bf16),
        ],
        8 * rows * width * LANES,
        2 * 1024 * 1024,
        in_specs=[VMEM] * 7,
        out_specs=[VMEM] * 5,
        scratch_shapes=[pltpu.VMEM((2 * half, LANES), f32)],
    )(inside, pair, got, fq, raw_local, up, gain)


def branch_parts(attn, w_out):
    rows, width = attn.shape

    def body(attn_ref, w_ref, *outs):
        m = lax.axis_index("mp")
        for k, ref in zip((2, 1, 3, 0), outs):
            at = lax.rem(m + k, 4) * width
            ref[...] = mm(
                attn_ref[...], w_ref[:, pl.ds(pl.multiple_of(at, LANES), width)]
            ).astype(bf16)

    return plain(
        body,
        [((rows, width), bf16)] * 4,
        8 * rows * width * width,
        2 * 1024 * 1024,
        attn,
        w_out,
    )


def local_grads(fq, fk, v, draw, before):
    rows, width = fq.shape

    def body(fq_ref, fk_ref, v_ref, draw_ref, before_ref, dq_ref, dk_ref, dv_ref):
        lower, upper = (tri(rows, False), tri(rows, True))
        for p in range(width // LANES):
            cols = slice(p * LANES, (p + 1) * LANES)
            q, k, val, dr = (fq_ref[:, cols], fk_ref[:, cols], v_ref[:, cols], draw_ref[:, cols])
            dq = mm(dr, unpack(before_ref[p * HD : (p + 1) * HD, :]), NT)
            dk, dv = (None, None)
            for h in (0, 1):
                val_h, k_h, q_h, dr_h = (one_head(a, h) for a in (val, k, q, dr))
                dq = dq + mm(masked(mm(dr, val_h, NT), lower), k_h)
                dk_h = mm(masked(mm(val_h, dr, NT), upper), q_h)
                dv_h = mm(masked(mm(k_h, q, NT), upper), dr_h)
                dk = dk_h if dk is None else dk + dk_h
                dv = dv_h if dv is None else dv + dv_h
            dq_ref[:, cols] = (dq * jnp.minimum(q.astype(f32), 1.0)).astype(bf16)
            dk_ref[:, cols] = dk
            dv_ref[:, cols] = dv

    return plain(
        body,
        [((rows, width), bf16), ((rows, width), f32), ((rows, width), f32)],
        24 * rows * rows * width,
        3 * 1024 * 1024,
        fq,
        fk,
        v,
        draw,
        before,
    )


def latent_part(m, k, width, triples):
    rows = pl.ds(pl.multiple_of(lax.rem(m + k, 4) * width, LANES), width)
    total = None
    for grad_ref, w_ref in triples:
        part = mm(grad_ref[...], w_ref[rows, :], NT)
        total = part if total is None else total + part
    return total.astype(bf16)


def first_part(inside, pair, got, fk, v, dq, dk, dv, w_query, w_key, w_value):
    rows, width = fk.shape
    half = inside.shape[0]

    def body(
        inside_ref,
        pair_ref,
        got_ref,
        fk_ref,
        v_ref,
        dq_ref,
        dkl_ref,
        dvl_ref,
        wq_ref,
        wk_ref,
        wv_ref,
        dk_ref,
        dv_ref,
        part_ref,
        state,
    ):
        whole_state(True, inside_ref, pair_ref, got_ref, state)
        for p in range(width // LANES):
            cols = slice(p * LANES, (p + 1) * LANES)
            after = unpack(state[p * HD : (p + 1) * HD, :].astype(bf16))
            k = fk_ref[:, cols]
            dk = dkl_ref[:, cols] + mm(v_ref[:, cols], after, NT)
            dk_ref[:, cols] = (dk * jnp.minimum(k.astype(f32), 1.0)).astype(bf16)
            dv_ref[:, cols] = (dvl_ref[:, cols] + mm(k, after)).astype(bf16)
        m = lax.axis_index("mp")
        part_ref[...] = latent_part(
            m, 2, width, ((dq_ref, wq_ref), (dk_ref, wk_ref), (dv_ref, wv_ref))
        )

    return call(
        body,
        [((rows, width), bf16)] * 3,
        6 * rows * width * width,
        5 * 1024 * 1024,
        in_specs=[VMEM] * 11,
        out_specs=[VMEM] * 3,
        scratch_shapes=[pltpu.VMEM((2 * half, LANES), f32)],
    )(inside, pair, got, fk, v, dq, dk, dv, w_query, w_key, w_value)


def other_parts(which, dq, dk, dv, w_query, w_key, w_value):
    rows, width = dq.shape

    def body(dq_ref, dk_ref, dv_ref, wq_ref, wk_ref, wv_ref, *outs):
        m = lax.axis_index("mp")
        for k, ref in zip(which, outs):
            ref[...] = latent_part(
                m, k, width, ((dq_ref, wq_ref), (dk_ref, wk_ref), (dv_ref, wv_ref))
            )

    return plain(
        body,
        [((rows, width), bf16)] * len(which),
        6 * rows * width * width * len(which),
        5 * 1024 * 1024,
        dq,
        dk,
        dv,
        w_query,
        w_key,
        w_value,
    )


def add_up(parts):
    total = parts[0].astype(f32)
    for part in parts[1:]:
        total = total + part.astype(f32)
    return total.astype(bf16)


def to_owner(part, k):
    return lax.ppermute(part, "mp", shifts(4, k))


def per_device(latents, w_query, w_key, w_value, w_out, head_gain, grad_out):
    gain = head_gain.reshape(1, -1)
    fk, v, own, other = key_value(latents, w_key, w_value)
    inside, pair, got, in_plane, chip = seq_before(False, own, other)
    grad_held, _ = lax.optimization_barrier((grad_out, chip))
    grads = [grad_out] + [to_owner(grad_held, k) for k in (1, 2, 3)]
    latents_held, _ = lax.optimization_barrier((latents, in_plane))
    fq, raw_local = query_local(latents_held, w_query, fk, v)
    up = upstream_of(grads, w_out, gain)
    attn, draw, before, own_r, other_r = normed(inside, pair, got, fq, raw_local, up, gain)
    inside_r, pair_r, got_r, in_plane_r, chip_r = seq_before(True, own_r, other_r)
    attn_held, _ = lax.optimization_barrier((attn, chip_r))
    b2, b1, b3, b0 = branch_parts(attn_held, w_out)
    branch = add_up([b0, to_owner(b2, 2), to_owner(b1, 1), to_owner(b3, 3)])
    draw_held, _ = lax.optimization_barrier((draw, in_plane_r))
    dq, dk_local, dv_local = local_grads(fq, fk, v, draw_held, before)
    dk, dv, l2 = first_part(
        inside_r, pair_r, got_r, fk, v, dq, dk_local, dv_local, w_query, w_key, w_value
    )
    l1, l3 = other_parts((1, 3), dq, dk, dv, w_query, w_key, w_value)
    (l0,) = other_parts((0,), dq, dk, dv, w_query, w_key, w_value)
    d_latents = add_up([l0, to_owner(l2, 2), to_owner(l1, 1), to_owner(l3, 3)])
    return (branch, d_latents)


def solution(mesh):
    split = Mesh(mesh.devices.reshape(8, 4, 2, mesh.shape["mp"]), (*SEQ, "mp"))
    in_specs = (
        P(SEQ, None),
        P(None, "mp"),
        P(None, "mp"),
        P(None, "mp"),
        P("mp", None),
        P("mp"),
        P(SEQ, "mp"),
    )
    out_specs = (P(SEQ, "mp"), P(SEQ, "mp"))
    return jax.shard_map(
        per_device, mesh=split, in_specs=in_specs, out_specs=out_specs, check_vma=False
    )
```

```python
import jax
import jax.numpy as jnp
from jax import lax
from jax.experimental import pallas as pl
from jax.experimental.pallas import tpu as pltpu
from jax.sharding import Mesh
from jax.sharding import PartitionSpec as P


HD = 64
LANES = 128
SEQ = ("seq_0", "seq_1", "seq_2")
SWAP = [(0, 1), (1, 0)]
epsilon = 1e-06
f32, bf16 = (jnp.float32, jnp.bfloat16)
NT = (((1,), (1,)), ((), ()))
TN = (((0,), (0,)), ((), ()))
VMEM = pl.BlockSpec(memory_space=pltpu.VMEM)


def shifts(count, step):
    return [(i, (i + step) % count) for i in range(count)]


def mm(a, b, contract=(((1,), (0,)), ((), ()))):
    return lax.dot_general(a, b, contract, preferred_element_type=f32)


def relay(near, *args):
    def body(*refs):
        sources, targets, sem = (refs[: len(args)], refs[len(args) : -1], refs[-1])
        copies = [
            pltpu.make_async_copy(a, b, sem.at[i]) for i, (a, b) in enumerate(zip(sources, targets))
        ]
        for copy in copies:
            copy.start()
        for copy in copies:
            copy.wait()

    hbm = pl.BlockSpec(memory_space=pltpu.HBM)
    make = pltpu.VMEM if near else pltpu.HBM
    return pl.pallas_call(
        body,
        out_shape=[make(a.shape, a.dtype) for a in args],
        in_specs=[hbm if near else VMEM] * len(args),
        out_specs=[VMEM if near else hbm] * len(args),
        scratch_shapes=[pltpu.SemaphoreType.DMA((len(args),))],
        cost_estimate=pl.CostEstimate(flops=1, bytes_accessed=1024 * 1024, transcendentals=0),
    )(*(pltpu.with_memory_space_constraint(a, pltpu.HBM if near else pltpu.VMEM) for a in args))


def in_hbm(x):
    return pltpu.with_memory_space_constraint(x, pltpu.HBM)


def shape_of(shape, kind, far=False):
    return pltpu.HBM(shape, kind) if far else jax.ShapeDtypeStruct(shape, kind)


def call(body, outs, flops, moved, **extra):
    return pl.pallas_call(
        body,
        out_shape=[shape_of(*out) for out in outs],
        cost_estimate=pl.CostEstimate(flops=flops, bytes_accessed=moved, transcendentals=0),
        compiler_params=pltpu.CompilerParams(vmem_limit_bytes=20 * 1024 * 1024),
        **extra,
    )


def plain(body, outs, flops, moved, *args):
    return call(
        body, outs, flops, moved, in_specs=[VMEM] * len(args), out_specs=[VMEM] * len(outs)
    )(*args)


def feature_map(u):
    return jnp.where(u > 0, u + 1.0, jnp.exp(jnp.minimum(u, 0.0)))


def low_lanes(shape):
    return lax.broadcasted_iota(jnp.int32, shape, len(shape) - 1) < HD


def one_head(x, head):
    low = low_lanes(x.shape)
    keep = low if head == 0 else jnp.logical_not(low)
    return jnp.where(keep, x, jnp.zeros_like(x))


def pack(full):
    return jnp.where(low_lanes((HD, LANES)), full[:HD], full[HD:])


def unpack(rows):
    low = low_lanes((HD, LANES))
    zero = jnp.zeros_like(rows)
    return jnp.concatenate([jnp.where(low, rows, zero), jnp.where(low, zero, rows)], axis=0)


def head_ones():
    r = lax.broadcasted_iota(jnp.int32, (LANES, LANES), 0) < HD
    c = lax.broadcasted_iota(jnp.int32, (LANES, LANES), 1) < HD
    return jnp.where(r == c, 1.0, 0.0).astype(bf16)


def half_at(other, half):
    side = lax.axis_index("seq_2")
    side = 1 - side if other else side
    return pl.ds(pl.multiple_of(side * half, 16), half)


def whole_state(later, mine_ref, got_ref, pair_ref, state_ref):
    half = mine_ref.shape[0]
    last = lax.axis_index("seq_2") == (0 if later else 1)
    state_ref[half_at(False, half), :] = mine_ref[...].astype(f32)
    state_ref[half_at(True, half), :] = got_ref[...].astype(f32)
    state_ref[...] += jnp.where(last, pair_ref[...].astype(f32), 0.0)


def pair_sum(state, pair):
    half = state.shape[0] // 2

    def body(state_ref, pair_ref, chip_ref):
        own = half_at(False, half)
        chip_ref[...] = (state_ref[own, :].astype(f32) + pair_ref[own, :].astype(f32)).astype(bf16)

    return plain(body, [((half, LANES), bf16)], 1, half * 1024, state, pair)[0]


def plane_sums(later, chip, got, pair):
    half = chip.shape[0]

    def body(chip_ref, g1, g2, g3, pair_ref, planes_ref, kept_ref):
        y = lax.axis_index("seq_1")
        y = 3 - y if later else y
        total = chip_ref[...].astype(f32)
        inside = jnp.zeros_like(total)
        for k, ref in ((1, g1), (2, g2), (3, g3)):
            piece = ref[...].astype(f32)
            total = total + piece
            inside = inside + jnp.where(y >= k, piece, 0.0)
        planes_ref[...] = jnp.broadcast_to(total.astype(bf16)[None], planes_ref.shape)
        planes_ref[pl.ds(lax.axis_index("seq_0"), 1)] = inside.astype(bf16)[None]
        kept_ref[...] = pair_ref[...]

    outs = [((8, half, LANES), bf16, True), ((2 * half, LANES), bf16, True)]
    return plain(body, outs, 1, half * 4096, chip, *got, pair)


def before_chip(later, planes):
    half = planes.shape[1]

    def body(planes_ref, send_ref):
        z = lax.axis_index("seq_0")
        total = jnp.zeros((half, LANES), f32)
        for k in range(8):
            take = (z <= k) if later else (z >= k)
            total = total + jnp.where(take, planes_ref[k].astype(f32), 0.0)
        send_ref[...] = total.astype(bf16)

    return plain(body, [((half, LANES), bf16)], 1, half * 4096, planes)[0]


def plane_exchange(planes):
    return lax.all_to_all(planes, "seq_0", 0, 0, tiled=True)


def swap(x):
    return lax.ppermute(x, "seq_2", SWAP)


def y_gather(later, chip):
    got = []
    for k in (2, 1, 3):
        got.append(lax.ppermute(chip, "seq_1", shifts(4, -k if later else k)))
    return got[1], got[0], got[2]


def key_value(latents, w_key, w_value):
    rows, width = (latents.shape[0], w_key.shape[1])
    steps = 4
    depth = latents.shape[1] // steps

    def body(x_hbm, wk_hbm, wv_hbm, fk_ref, v_ref, state_ref, x_ref, w_ref, sem):
        copies = []
        for i in range(steps):
            span = pl.ds(i * depth, depth)
            copies.append(
                [
                    pltpu.make_async_copy(src, dst, sem.at[3 * i + j])
                    for j, (src, dst) in enumerate(
                        (
                            (x_hbm.at[:, span], x_ref.at[:, span]),
                            (wk_hbm.at[span, :], w_ref.at[span, pl.ds(0, width)]),
                            (wv_hbm.at[span, :], w_ref.at[span, pl.ds(width, width)]),
                        )
                    )
                ]
            )
        for group in copies:
            for copy in group:
                copy.start()
        total = None
        for i, group in enumerate(copies):
            for copy in group:
                copy.wait()
            span = slice(i * depth, (i + 1) * depth)
            part = mm(x_ref[:, span], w_ref[span, :])
            total = part if total is None else total + part
        fk_ref[...] = feature_map(total[:, :width]).astype(bf16)
        v_ref[...] = total[:, width:].astype(bf16)
        for p in range(width // LANES):
            cols = slice(p * LANES, (p + 1) * LANES)
            state_ref[p * HD : (p + 1) * HD, :] = pack(
                mm(fk_ref[:, cols], v_ref[:, cols], TN)
            ).astype(bf16)

    hbm = pl.BlockSpec(memory_space=pltpu.HBM)
    return call(
        body,
        [
            ((rows, width), bf16),
            ((rows, width), bf16),
            ((width * HD // LANES, LANES), bf16),
        ],
        4 * rows * width * latents.shape[1],
        3 * 1024 * 1024,
        in_specs=[hbm] * 3,
        out_specs=[VMEM] * 3,
        scratch_shapes=[
            pltpu.VMEM(latents.shape, bf16),
            pltpu.VMEM((latents.shape[1], 2 * width), bf16),
            pltpu.SemaphoreType.DMA((3 * steps,)),
        ],
    )(in_hbm(latents), in_hbm(w_key), in_hbm(w_value))


def tri(rows, upper):
    t = lax.broadcasted_iota(jnp.int32, (rows, rows), 0)
    s = lax.broadcasted_iota(jnp.int32, (rows, rows), 1)
    return (t <= s) if upper else (t >= s)


def masked(scores, keep):
    return jnp.where(keep, scores, 0.0).astype(bf16)


def query_local(latents, w_query, fk, v):
    rows, width = fk.shape

    def body(x_ref, wq_ref, fk_ref, v_ref, fq_ref, raw_ref):
        fq_ref[...] = feature_map(mm(x_ref[...], wq_ref[...])).astype(bf16)
        keep = tri(rows, False)
        for p in range(width // LANES):
            cols = slice(p * LANES, (p + 1) * LANES)
            q, k, val = (fq_ref[:, cols], fk_ref[:, cols], v_ref[:, cols])
            total = None
            for h in (0, 1):
                score = masked(mm(q, one_head(k, h), NT), keep)
                part = mm(score, one_head(val, h))
                total = part if total is None else total + part
            raw_ref[:, cols] = total.astype(bf16)

    return plain(
        body,
        [((rows, width), bf16, True)] * 2,
        2 * rows * width * (latents.shape[1] + 4 * rows),
        3 * 1024 * 1024,
        latents,
        w_query,
        in_hbm(fk),
        in_hbm(v),
    )


def upstream_of(grads, w_out, gain):
    rows, width = grads[0].shape

    def body(g0, g1, g2, g3, w_ref, gain_ref, up_ref):
        m = lax.axis_index("mp")
        total = jnp.zeros((rows, width), f32)
        for k, ref in enumerate((g0, g1, g2, g3)):
            at = lax.rem(m + 4 - k, 4) * width
            total = total + mm(ref[...], w_ref[:, pl.ds(pl.multiple_of(at, LANES), width)], NT)
        up_ref[...] = (total * gain_ref[...]).astype(bf16)

    return plain(
        body,
        [((rows, width), bf16, True)],
        8 * rows * width * width,
        3 * 1024 * 1024,
        *grads,
        w_out,
        gain,
    )[0]


def normed(mine, got, pair, fq, raw_local, up, gain):
    rows, width = fq.shape
    half = mine.shape[0]

    def body(
        mine_ref,
        got_ref,
        pair_ref,
        fq_ref,
        raw_ref,
        up_ref,
        gain_ref,
        attn_ref,
        draw_ref,
        before_ref,
        after_ref,
        state,
    ):
        whole_state(False, mine_ref, got_ref, pair_ref, state)
        before_ref[...] = state[...].astype(bf16)
        ones = head_ones()
        for p in range(width // LANES):
            cols = slice(p * LANES, (p + 1) * LANES)
            q = fq_ref[:, cols]
            raw = raw_ref[:, cols].astype(f32) + mm(q, unpack(before_ref[p * HD : (p + 1) * HD, :]))
            upstream = up_ref[:, cols].astype(f32)
            square = mm((raw * raw).astype(bf16), ones) * (1.0 / HD)
            cross = mm((raw * upstream).astype(bf16), ones) * (1.0 / HD)
            inv = lax.rsqrt(square + epsilon)
            unit = raw * inv
            attn_ref[:, cols] = (unit * gain_ref[:, cols]).astype(bf16)
            draw = (inv * upstream - inv * inv * unit * cross).astype(bf16)
            draw_ref[:, cols] = draw
            after_ref[p * HD : (p + 1) * HD, :] = pack(mm(q, draw, TN)).astype(bf16)

    return call(
        body,
        [
            ((rows, width), bf16),
            ((rows, width), bf16),
            ((2 * half, LANES), bf16),
            ((2 * half, LANES), bf16),
        ],
        8 * rows * width * LANES,
        2 * 1024 * 1024,
        in_specs=[VMEM] * 7,
        out_specs=[VMEM] * 4,
        scratch_shapes=[pltpu.VMEM((2 * half, LANES), f32)],
    )(mine, got, pair, fq, raw_local, up, gain)


def branch_parts(attn, w_out, draw, before):
    rows, width = attn.shape

    def body(attn_ref, w_ref, draw_ref, before_ref, *refs):
        outs, kept, sem = (refs[:4], refs[4:6], refs[6])
        copies = [
            pltpu.make_async_copy(a, b, sem.at[i])
            for i, (a, b) in enumerate(zip((draw_ref, before_ref), kept))
        ]
        for copy in copies:
            copy.start()
        m = lax.axis_index("mp")
        for k, ref in zip((2, 1, 3, 0), outs):
            at = lax.rem(m + k, 4) * width
            ref[...] = mm(
                attn_ref[...], w_ref[:, pl.ds(pl.multiple_of(at, LANES), width)]
            ).astype(bf16)
        for copy in copies:
            copy.wait()

    return call(
        body,
        [((rows, width), bf16, True)] * 5 + [(before.shape, bf16, True)],
        8 * rows * width * width,
        2 * 1024 * 1024,
        in_specs=[VMEM] * 4,
        out_specs=[VMEM] * 4 + [pl.BlockSpec(memory_space=pltpu.HBM)] * 2,
        scratch_shapes=[pltpu.SemaphoreType.DMA((2,))],
    )(attn, w_out, draw, before)


def local_grads(fq, fk, v, draw, before):
    rows, width = fq.shape

    def body(fq_ref, fk_ref, v_ref, draw_ref, before_ref, dq_ref, dk_ref, dv_ref):
        lower, upper = (tri(rows, False), tri(rows, True))
        for p in range(width // LANES):
            cols = slice(p * LANES, (p + 1) * LANES)
            q, k, val, dr = (fq_ref[:, cols], fk_ref[:, cols], v_ref[:, cols], draw_ref[:, cols])
            dq = mm(dr, unpack(before_ref[p * HD : (p + 1) * HD, :]), NT)
            dk, dv = (None, None)
            for h in (0, 1):
                val_h, k_h, q_h, dr_h = (one_head(a, h) for a in (val, k, q, dr))
                dq = dq + mm(masked(mm(dr, val_h, NT), lower), k_h)
                dk_h = mm(masked(mm(val_h, dr, NT), upper), q_h)
                dv_h = mm(masked(mm(k_h, q, NT), upper), dr_h)
                dk = dk_h if dk is None else dk + dk_h
                dv = dv_h if dv is None else dv + dv_h
            dq_ref[:, cols] = (dq * jnp.minimum(q.astype(f32), 1.0)).astype(bf16)
            dk_ref[:, cols] = dk.astype(bf16)
            dv_ref[:, cols] = dv.astype(bf16)

    return plain(
        body,
        [((rows, width), bf16, True)] * 3,
        400 * rows * rows * width,
        3 * 1024 * 1024,
        *(in_hbm(a) for a in (fq, fk, v, draw, before)),
    )


def latent_part(m, k, width, triples):
    rows = pl.ds(pl.multiple_of(lax.rem(m + k, 4) * width, LANES), width)
    total = None
    for grad_ref, w_ref in triples:
        part = mm(grad_ref[...], w_ref[rows, :], NT)
        total = part if total is None else total + part
    return total.astype(bf16)


def first_part(mine, got, pair, fk, v, dq, dk, dv, w_query, w_key, w_value):
    rows, width = fk.shape
    half = mine.shape[0]

    def body(
        mine_ref,
        got_ref,
        pair_ref,
        fk_ref,
        v_ref,
        dq_ref,
        dkl_ref,
        dvl_ref,
        wq_ref,
        wk_ref,
        wv_ref,
        dk_ref,
        dv_ref,
        part_ref,
        state,
    ):
        whole_state(True, mine_ref, got_ref, pair_ref, state)
        for p in range(width // LANES):
            cols = slice(p * LANES, (p + 1) * LANES)
            after = unpack(state[p * HD : (p + 1) * HD, :].astype(bf16))
            k = fk_ref[:, cols]
            dk = dkl_ref[:, cols].astype(f32) + mm(v_ref[:, cols], after, NT)
            dk_ref[:, cols] = (dk * jnp.minimum(k.astype(f32), 1.0)).astype(bf16)
            dv_ref[:, cols] = (dvl_ref[:, cols].astype(f32) + mm(k, after)).astype(bf16)
        m = lax.axis_index("mp")
        part_ref[...] = latent_part(
            m, 2, width, ((dq_ref, wq_ref), (dk_ref, wk_ref), (dv_ref, wv_ref))
        )

    return call(
        body,
        [((rows, width), bf16)] * 3,
        6 * rows * width * width,
        5 * 1024 * 1024,
        in_specs=[VMEM] * 11,
        out_specs=[VMEM] * 3,
        scratch_shapes=[pltpu.VMEM((2 * half, LANES), f32)],
    )(mine, got, pair, fk, v, dq, dk, dv, w_query, w_key, w_value)


def other_parts(which, dq, dk, dv, w_query, w_key, w_value):
    rows, width = dq.shape

    def body(dq_ref, dk_ref, dv_ref, wq_ref, wk_ref, wv_ref, *outs):
        m = lax.axis_index("mp")
        for k, ref in zip(which, outs):
            ref[...] = latent_part(
                m, k, width, ((dq_ref, wq_ref), (dk_ref, wk_ref), (dv_ref, wv_ref))
            )

    return plain(
        body,
        [((rows, width), bf16)] * len(which),
        6 * rows * width * width * len(which),
        5 * 1024 * 1024,
        dq,
        dk,
        dv,
        w_query,
        w_key,
        w_value,
    )


def add_up(parts):
    total = parts[0].astype(f32)
    for part in parts[1:]:
        total = total + part.astype(f32)
    return total.astype(bf16)


def to_owner(part, k):
    return lax.ppermute(part, "mp", shifts(4, k))


def hold(x, anchor):
    return lax.optimization_barrier((x, anchor))[0]


def per_device(latents, w_query, w_key, w_value, w_out, head_gain, grad_out):
    gain = head_gain.reshape(1, -1)
    fk, v, state = key_value(latents, w_key, w_value)
    pair = swap(state)
    fk, v = relay(False, fk, v)
    chip = pair_sum(state, pair)
    got = y_gather(False, chip)
    grad_held = hold(grad_out, chip)
    grads = [grad_out] + [to_owner(grad_held, k) for k in (1, 2, 3)]
    planes, pair = plane_sums(False, chip, got, pair)
    fq, raw_local = query_local(hold(latents, planes), w_query, fk, v)
    up = upstream_of(grads, w_out, gain)
    planes = plane_exchange(planes)
    mine = before_chip(False, planes)
    got = swap(mine)
    near = relay(True, pair, fq, raw_local, up)
    attn, draw, before, state = normed(mine, got, *near, gain)
    pair = swap(state)
    b2, b1, b3, b0, draw, before = branch_parts(attn, w_out, draw, before)
    chip = pair_sum(state, pair)
    got = y_gather(True, chip)
    b2, b1, b3 = (hold(b, chip) for b in (b2, b1, b3))
    branch = [b0, to_owner(b2, 2), to_owner(b1, 1), to_owner(b3, 3)]
    planes, pair = plane_sums(True, chip, got, pair)
    dq, dk_local, dv_local = local_grads(fq, fk, v, hold(draw, planes), before)
    (w_query,) = relay(True, hold(w_query, dq))
    planes = plane_exchange(planes)
    mine = before_chip(True, planes)
    got = swap(mine)
    near = relay(True, pair, fk, v, dq, dk_local, dv_local)
    dq = near[3]
    weights = (w_query, w_key, w_value)
    dk, dv, l2 = first_part(mine, got, *near, *weights)
    l2 = to_owner(l2, 2)
    l1, l3 = other_parts((1, 3), dq, dk, dv, *weights)
    l1, l3 = (to_owner(l1, 1), to_owner(l3, 3))
    (l0,) = other_parts((0,), dq, dk, dv, *weights)
    return (add_up(branch), add_up([l0, l2, l1, l3]))


def solution(mesh):
    split = Mesh(mesh.devices.reshape(8, 4, 2, mesh.shape["mp"]), (*SEQ, "mp"))
    in_specs = (
        P(SEQ, None),
        P(None, "mp"),
        P(None, "mp"),
        P(None, "mp"),
        P("mp", None),
        P("mp"),
        P(SEQ, "mp"),
    )
    out_specs = (P(SEQ, "mp"), P(SEQ, "mp"))
    return jax.shard_map(
        per_device, mesh=split, in_specs=in_specs, out_specs=out_specs, check_vma=False
    )
```

```python
import jax
import jax.numpy as jnp
from jax import lax
from jax.experimental import pallas as pl
from jax.experimental.pallas import tpu as pltpu
from jax.sharding import Mesh
from jax.sharding import PartitionSpec as P


HD = 64
LANES = 128
SEQ = ("seq_0", "seq_1", "seq_2")
SWAP = [(0, 1), (1, 0)]
epsilon = 1e-06
f32, bf16 = (jnp.float32, jnp.bfloat16)
NT = (((1,), (1,)), ((), ()))
TN = (((0,), (0,)), ((), ()))
VMEM = pl.BlockSpec(memory_space=pltpu.VMEM)


def shifts(count, step):
    return [(i, (i + step) % count) for i in range(count)]


def mm(a, b, contract=(((1,), (0,)), ((), ()))):
    return lax.dot_general(a, b, contract, preferred_element_type=f32)


def in_hbm(x):
    return pltpu.with_memory_space_constraint(x, pltpu.HBM)


def shape_of(shape, kind, where=pltpu.VMEM):
    return where(shape, kind)


def call(body, outs, flops, moved, **extra):
    return pl.pallas_call(
        body,
        out_shape=[shape_of(*out) for out in outs],
        cost_estimate=pl.CostEstimate(flops=flops, bytes_accessed=moved, transcendentals=0),
        compiler_params=pltpu.CompilerParams(vmem_limit_bytes=20 * 1024 * 1024),
        **extra,
    )


def plain(body, outs, flops, moved, *args):
    return call(
        body, outs, flops, moved, in_specs=[VMEM] * len(args), out_specs=[VMEM] * len(outs)
    )(*args)


def feature_map(u):
    return jnp.where(u > 0, u + 1.0, jnp.exp(jnp.minimum(u, 0.0)))


def low_lanes(shape):
    return lax.broadcasted_iota(jnp.int32, shape, len(shape) - 1) < HD


def one_head(x, head):
    low = low_lanes(x.shape)
    keep = low if head == 0 else jnp.logical_not(low)
    return jnp.where(keep, x, jnp.zeros_like(x))


def pack(full):
    return jnp.where(low_lanes((HD, LANES)), full[:HD], full[HD:])


def unpack(rows):
    low = low_lanes((HD, LANES))
    zero = jnp.zeros_like(rows)
    return jnp.concatenate([jnp.where(low, rows, zero), jnp.where(low, zero, rows)], axis=0)


def head_ones():
    r = lax.broadcasted_iota(jnp.int32, (LANES, LANES), 0) < HD
    c = lax.broadcasted_iota(jnp.int32, (LANES, LANES), 1) < HD
    return jnp.where(r == c, 1.0, 0.0).astype(bf16)


def half_at(other, half):
    side = lax.axis_index("seq_2")
    side = 1 - side if other else side
    return pl.ds(pl.multiple_of(side * half, 16), half)


def whole_state(later, mine_ref, got_ref, pair_ref, state_ref):
    half = mine_ref.shape[0]
    last = lax.axis_index("seq_2") == (0 if later else 1)
    state_ref[half_at(False, half), :] = mine_ref[...].astype(f32)
    state_ref[half_at(True, half), :] = got_ref[...].astype(f32)
    state_ref[...] += jnp.where(last, pair_ref[...].astype(f32), 0.0)


def pair_sum(state, pair):
    half = state.shape[0] // 2

    def body(state_ref, pair_ref, chip_ref):
        own = half_at(False, half)
        chip_ref[...] = (state_ref[own, :].astype(f32) + pair_ref[own, :].astype(f32)).astype(bf16)

    return plain(body, [((half, LANES), bf16)], 1, half * 1024, state, pair)[0]


def plane_sums(later, chip, got):
    half = chip.shape[0]

    def body(chip_ref, g1, g2, g3, planes_ref):
        y = lax.axis_index("seq_1")
        y = 3 - y if later else y
        total = chip_ref[...].astype(f32)
        inside = jnp.zeros_like(total)
        for k, ref in ((1, g1), (2, g2), (3, g3)):
            piece = ref[...].astype(f32)
            total = total + piece
            inside = inside + jnp.where(y >= k, piece, 0.0)
        planes_ref[...] = jnp.broadcast_to(total.astype(bf16)[None], planes_ref.shape)
        planes_ref[pl.ds(lax.axis_index("seq_0"), 1)] = inside.astype(bf16)[None]

    outs = [((8, half, LANES), bf16, pltpu.HBM)]
    return plain(body, outs, 1, half * 4096, chip, *got)[0]


def before_chip(later, planes):
    half = planes.shape[1]

    def body(planes_ref, send_ref):
        z = lax.axis_index("seq_0")
        total = jnp.zeros((half, LANES), f32)
        for k in range(8):
            take = (z <= k) if later else (z >= k)
            total = total + jnp.where(take, planes_ref[k].astype(f32), 0.0)
        send_ref[...] = total.astype(bf16)

    return plain(body, [((half, LANES), bf16)], 1, half * 4096, planes)[0]


def plane_exchange(planes):
    return lax.all_to_all(planes, "seq_0", 0, 0, tiled=True)


def swap(x):
    return lax.ppermute(x, "seq_2", SWAP)


def y_gather(later, chip):
    got = []
    for k in (2, 1, 3):
        got.append(lax.ppermute(chip, "seq_1", shifts(4, -k if later else k)))
    return got[1], got[0], got[2]


def key_value(latents, w_key, w_value):
    rows, width = (latents.shape[0], w_key.shape[1])
    steps = 4
    depth = latents.shape[1] // steps

    def body(x_hbm, wk_hbm, wv_hbm, fk_ref, v_ref, state_ref, x_ref, w_ref, sem):
        copies = []
        for i in range(steps):
            span = pl.ds(i * depth, depth)
            copies.append(
                [
                    pltpu.make_async_copy(src, dst, sem.at[3 * i + j])
                    for j, (src, dst) in enumerate(
                        (
                            (x_hbm.at[:, span], x_ref.at[:, span]),
                            (wk_hbm.at[span, :], w_ref.at[span, pl.ds(0, width)]),
                            (wv_hbm.at[span, :], w_ref.at[span, pl.ds(width, width)]),
                        )
                    )
                ]
            )
        for group in copies:
            for copy in group:
                copy.start()
        total = None
        for i, group in enumerate(copies):
            for copy in group:
                copy.wait()
            span = slice(i * depth, (i + 1) * depth)
            part = mm(x_ref[:, span], w_ref[span, :])
            total = part if total is None else total + part
        fk_ref[...] = feature_map(total[:, :width]).astype(bf16)
        v_ref[...] = total[:, width:].astype(bf16)
        for p in range(width // LANES):
            cols = slice(p * LANES, (p + 1) * LANES)
            state_ref[p * HD : (p + 1) * HD, :] = pack(
                mm(fk_ref[:, cols], v_ref[:, cols], TN)
            ).astype(bf16)

    hbm = pl.BlockSpec(memory_space=pltpu.HBM)
    return call(
        body,
        [
            ((rows, width), bf16),
            ((rows, width), bf16),
            ((width * HD // LANES, LANES), bf16),
        ],
        4 * rows * width * latents.shape[1],
        3 * 1024 * 1024,
        in_specs=[hbm] * 3,
        out_specs=[VMEM] * 3,
        scratch_shapes=[
            pltpu.VMEM(latents.shape, bf16),
            pltpu.VMEM((latents.shape[1], 2 * width), bf16),
            pltpu.SemaphoreType.DMA((3 * steps,)),
        ],
    )(in_hbm(latents), in_hbm(w_key), in_hbm(w_value))


def tri(rows, upper):
    t = lax.broadcasted_iota(jnp.int32, (rows, rows), 0)
    s = lax.broadcasted_iota(jnp.int32, (rows, rows), 1)
    return (t <= s) if upper else (t >= s)


def masked(scores, keep):
    return jnp.where(keep, scores, 0.0).astype(bf16)


def query_local(latents, w_query, fk, v):
    rows, width = fk.shape

    def body(x_ref, wq_ref, fk_ref, v_ref, fq_ref, raw_ref):
        fq_ref[...] = feature_map(mm(x_ref[...], wq_ref[...])).astype(bf16)
        keep = tri(rows, False)
        for p in range(width // LANES):
            cols = slice(p * LANES, (p + 1) * LANES)
            q, k, val = (fq_ref[:, cols], fk_ref[:, cols], v_ref[:, cols])
            total = None
            for h in (0, 1):
                score = masked(mm(q, one_head(k, h), NT), keep)
                part = mm(score, one_head(val, h))
                total = part if total is None else total + part
            raw_ref[:, cols] = total.astype(bf16)

    return plain(
        body,
        [((rows, width), bf16)] * 2,
        2 * rows * width * (latents.shape[1] + 4 * rows),
        3 * 1024 * 1024,
        latents,
        w_query,
        fk,
        v,
    )


def upstream_of(grads, w_out, gain):
    rows, width = grads[0].shape

    def body(g0, g1, g2, g3, w_hbm, gain_ref, up_ref, w_ref, sem):
        m = lax.axis_index("mp")
        copies = []
        for k in range(4):
            at = pl.multiple_of(lax.rem(m + 4 - k, 4) * width, LANES)
            copies.append(
                pltpu.make_async_copy(w_hbm.at[:, pl.ds(at, width)], w_ref.at[k], sem.at[k])
            )
        for copy in copies:
            copy.start()
        total = jnp.zeros((rows, width), f32)
        for k, ref in enumerate((g0, g1, g2, g3)):
            copies[k].wait()
            total = total + mm(ref[...], w_ref[k], NT)
        up_ref[...] = (total * gain_ref[...]).astype(bf16)

    return call(
        body,
        [((rows, width), bf16)],
        8 * rows * width * width,
        3 * 1024 * 1024,
        in_specs=[VMEM] * 4 + [pl.BlockSpec(memory_space=pltpu.HBM), VMEM],
        out_specs=[VMEM],
        scratch_shapes=[pltpu.VMEM((4, width, width), bf16), pltpu.SemaphoreType.DMA((4,))],
    )(*grads, in_hbm(w_out), gain)[0]


def normed(mine, got, pair, fq, raw_local, up, gain):
    rows, width = fq.shape
    half = mine.shape[0]

    def body(
        mine_ref,
        got_ref,
        pair_ref,
        fq_ref,
        raw_ref,
        up_ref,
        gain_ref,
        attn_ref,
        draw_ref,
        before_ref,
        after_ref,
        state,
    ):
        whole_state(False, mine_ref, got_ref, pair_ref, state)
        before_ref[...] = state[...].astype(bf16)
        ones = head_ones()
        for p in range(width // LANES):
            cols = slice(p * LANES, (p + 1) * LANES)
            q = fq_ref[:, cols]
            raw = raw_ref[:, cols].astype(f32) + mm(q, unpack(before_ref[p * HD : (p + 1) * HD, :]))
            upstream = up_ref[:, cols].astype(f32)
            square = mm((raw * raw).astype(bf16), ones) * (1.0 / HD)
            cross = mm((raw * upstream).astype(bf16), ones) * (1.0 / HD)
            inv = lax.rsqrt(square + epsilon)
            unit = raw * inv
            attn_ref[:, cols] = (unit * gain_ref[:, cols]).astype(bf16)
            draw = (inv * upstream - inv * inv * unit * cross).astype(bf16)
            draw_ref[:, cols] = draw
            after_ref[p * HD : (p + 1) * HD, :] = pack(mm(q, draw, TN)).astype(bf16)

    return call(
        body,
        [
            ((rows, width), bf16),
            ((rows, width), bf16),
            ((2 * half, LANES), bf16),
            ((2 * half, LANES), bf16),
        ],
        8 * rows * width * LANES,
        2 * 1024 * 1024,
        in_specs=[VMEM] * 7,
        out_specs=[VMEM] * 4,
        scratch_shapes=[pltpu.VMEM((2 * half, LANES), f32)],
    )(mine, got, pair, fq, raw_local, up, gain)


def branch_parts(attn, w_out):
    rows, width = attn.shape

    def body(attn_ref, w_hbm, *refs):
        outs, w_ref, sem = (refs[:4], refs[4], refs[5])
        copies = []
        for i, k in enumerate((2, 1, 3, 0)):
            source = w_hbm.at[:, block_rows(k, width)]
            copies.append(pltpu.make_async_copy(source, w_ref.at[i], sem.at[i]))
        for copy in copies:
            copy.start()
        for i, ref in enumerate(outs):
            copies[i].wait()
            ref[...] = mm(attn_ref[...], w_ref[i]).astype(bf16)

    return call(
        body,
        [((rows, width), bf16, pltpu.HBM)] * 4,
        8 * rows * width * width,
        2 * 1024 * 1024,
        in_specs=[VMEM, pl.BlockSpec(memory_space=pltpu.HBM)],
        out_specs=[VMEM] * 4,
        scratch_shapes=[pltpu.VMEM((4, width, width), bf16), pltpu.SemaphoreType.DMA((4,))],
    )(attn, in_hbm(w_out))


def local_grads(fq, fk, v, draw, before):
    rows, width = fq.shape

    def body(fq_ref, fk_ref, v_ref, draw_ref, before_ref, dq_ref, dk_ref, dv_ref):
        lower, upper = (tri(rows, False), tri(rows, True))
        for p in range(width // LANES):
            cols = slice(p * LANES, (p + 1) * LANES)
            q, k, val, dr = (fq_ref[:, cols], fk_ref[:, cols], v_ref[:, cols], draw_ref[:, cols])
            dq = mm(dr, unpack(before_ref[p * HD : (p + 1) * HD, :]), NT)
            dk, dv = (None, None)
            for h in (0, 1):
                val_h, k_h, q_h, dr_h = (one_head(a, h) for a in (val, k, q, dr))
                dq = dq + mm(masked(mm(dr, val_h, NT), lower), k_h)
                dk_h = mm(masked(mm(val_h, dr, NT), upper), q_h)
                dv_h = mm(masked(mm(k_h, q, NT), upper), dr_h)
                dk = dk_h if dk is None else dk + dk_h
                dv = dv_h if dv is None else dv + dv_h
            dq_ref[:, cols] = (dq * jnp.minimum(q.astype(f32), 1.0)).astype(bf16)
            dk_ref[:, cols] = dk.astype(bf16)
            dv_ref[:, cols] = dv.astype(bf16)

    return plain(
        body,
        [((rows, width), bf16)] * 3,
        24 * rows * rows * width,
        3 * 1024 * 1024,
        fq,
        fk,
        v,
        draw,
        before,
    )


def block_rows(k, width):
    at = lax.rem(lax.axis_index("mp") + k, 4) * width
    return pl.ds(pl.multiple_of(at, LANES), width)


def block_copies(k, sources, targets, sem, first):
    width = sources[0].shape[1]
    return [
        pltpu.make_async_copy(src.at[block_rows(k, width), :], dst, sem.at[first + i])
        for i, (src, dst) in enumerate(zip(sources, targets))
    ]


def weight_blocks(k, weights):
    width = weights[0].shape[1]

    def body(*refs):
        copies = block_copies(k, refs[:3], refs[3:6], refs[6], 0)
        for copy in copies:
            copy.start()
        for copy in copies:
            copy.wait()

    return call(
        body,
        [((width, width), bf16)] * 3,
        1,
        1024 * 1024,
        in_specs=[pl.BlockSpec(memory_space=pltpu.HBM)] * 3,
        out_specs=[VMEM] * 3,
        scratch_shapes=[pltpu.SemaphoreType.DMA((3,))],
    )(*(in_hbm(w) for w in weights))


def first_part(mine, got, pair, fk, v, dq, dk, dv, blocks):
    rows, width = fk.shape
    half = mine.shape[0]

    def body(
        mine_ref,
        got_ref,
        pair_ref,
        fk_ref,
        v_ref,
        dq_ref,
        dkl_ref,
        dvl_ref,
        wq_ref,
        wk_ref,
        wv_ref,
        dk_ref,
        dv_ref,
        part_ref,
        state,
    ):
        whole_state(True, mine_ref, got_ref, pair_ref, state)
        for p in range(width // LANES):
            cols = slice(p * LANES, (p + 1) * LANES)
            after = unpack(state[p * HD : (p + 1) * HD, :].astype(bf16))
            k = fk_ref[:, cols]
            dk = dkl_ref[:, cols].astype(f32) + mm(v_ref[:, cols], after, NT)
            dk_ref[:, cols] = (dk * jnp.minimum(k.astype(f32), 1.0)).astype(bf16)
            dv_ref[:, cols] = (dvl_ref[:, cols].astype(f32) + mm(k, after)).astype(bf16)
        total = mm(dq_ref[...], wq_ref[...], NT)
        total = total + mm(dk_ref[...], wk_ref[...], NT)
        part_ref[...] = (total + mm(dv_ref[...], wv_ref[...], NT)).astype(bf16)

    return call(
        body,
        [((rows, width), bf16)] * 3,
        6 * rows * width * width,
        2 * 1024 * 1024,
        in_specs=[VMEM] * 11,
        out_specs=[VMEM] * 3,
        scratch_shapes=[pltpu.VMEM((2 * half, LANES), f32)],
    )(mine, got, pair, fk, v, dq, dk, dv, *blocks)


def other_parts(which, dq, dk, dv, weights):
    rows, width = dq.shape
    count = len(which)

    def body(dq_ref, dk_ref, dv_ref, wq_hbm, wk_hbm, wv_hbm, *refs):
        outs, blocks, sem = (refs[:count], refs[count], refs[count + 1])
        copies = [
            block_copies(
                k, (wq_hbm, wk_hbm, wv_hbm), [blocks.at[3 * i + j] for j in range(3)], sem, 3 * i
            )
            for i, k in enumerate(which)
        ]
        for group in copies:
            for copy in group:
                copy.start()
        for i, (group, ref) in enumerate(zip(copies, outs)):
            for copy in group:
                copy.wait()
            total = None
            for j, grad_ref in enumerate((dq_ref, dk_ref, dv_ref)):
                part = mm(grad_ref[...], blocks[3 * i + j], NT)
                total = part if total is None else total + part
            ref[...] = total.astype(bf16)

    hbm = pl.BlockSpec(memory_space=pltpu.HBM)
    return call(
        body,
        [((rows, width), bf16)] * count,
        6 * rows * width * width * count,
        1024 * 1024 * count,
        in_specs=[VMEM] * 3 + [hbm] * 3,
        out_specs=[VMEM] * count,
        scratch_shapes=[
            pltpu.VMEM((3 * count, width, width), bf16),
            pltpu.SemaphoreType.DMA((3 * count,)),
        ],
    )(dq, dk, dv, *(in_hbm(w) for w in weights))


def add_up(parts):
    total = parts[0].astype(f32)
    for part in parts[1:]:
        total = total + part.astype(f32)
    return total.astype(bf16)


def to_owner(part, k):
    return lax.ppermute(part, "mp", shifts(4, k))


def hold(x, anchor):
    return lax.optimization_barrier((x, anchor))[0]


def per_device(latents, w_query, w_key, w_value, w_out, head_gain, grad_out):
    gain = head_gain.reshape(1, -1)
    fk, v, state = key_value(latents, w_key, w_value)
    pair = swap(state)
    chip = pair_sum(state, pair)
    got = y_gather(False, chip)
    grad_held = hold(grad_out, chip)
    grads = [grad_out] + [to_owner(grad_held, k) for k in (1, 2, 3)]
    planes = plane_sums(False, chip, got)
    fq, raw_local = query_local(hold(latents, planes), w_query, fk, v)
    up = upstream_of(grads, w_out, gain)
    planes = plane_exchange(planes)
    mine = before_chip(False, planes)
    got = swap(mine)
    attn, draw, before, state = normed(mine, got, pair, fq, raw_local, up, gain)
    pair = swap(state)
    chip = pair_sum(state, pair)
    got = y_gather(True, chip)
    b2, b1, b3, b0 = branch_parts(hold(attn, chip), w_out)
    planes = plane_sums(True, chip, got)
    b2, b1, b3 = (hold(b, planes) for b in (b2, b1, b3))
    branch = [b0, to_owner(b2, 2), to_owner(b1, 1), to_owner(b3, 3)]
    dq, dk_local, dv_local = local_grads(fq, fk, v, hold(draw, planes), before)
    weights = (w_query, w_key, w_value)
    blocks = weight_blocks(2, (hold(w_query, dq), w_key, w_value))
    planes = plane_exchange(planes)
    mine = before_chip(True, planes)
    got = swap(mine)
    dk, dv, l2 = first_part(mine, got, pair, fk, v, dq, dk_local, dv_local, blocks)
    l2 = to_owner(l2, 2)
    l1, l3 = other_parts((1, 3), dq, dk, dv, weights)
    l1, l3 = (to_owner(l1, 1), to_owner(l3, 3))
    (l0,) = other_parts((0,), dq, dk, dv, weights)
    return (add_up(branch), add_up([l0, l2, l1, l3]))


def solution(mesh):
    split = Mesh(mesh.devices.reshape(8, 4, 2, mesh.shape["mp"]), (*SEQ, "mp"))
    in_specs = (
        P(SEQ, None),
        P(None, "mp"),
        P(None, "mp"),
        P(None, "mp"),
        P("mp", None),
        P("mp"),
        P(SEQ, "mp"),
    )
    out_specs = (P(SEQ, "mp"), P(SEQ, "mp"))
    return jax.shard_map(
        per_device, mesh=split, in_specs=in_specs, out_specs=out_specs, check_vma=False
    )
```

```python
import jax
import jax.numpy as jnp
from jax import lax
from jax.experimental import pallas as pl
from jax.experimental.pallas import tpu as pltpu
from jax.sharding import Mesh
from jax.sharding import PartitionSpec as P


HD = 64
LANES = 128
SEQ = ("seq_0", "seq_1", "seq_2")
SWAP = [(0, 1), (1, 0)]
epsilon = 1e-06
f32, bf16 = (jnp.float32, jnp.bfloat16)
NT = (((1,), (1,)), ((), ()))
TN = (((0,), (0,)), ((), ()))
VMEM = pl.BlockSpec(memory_space=pltpu.VMEM)


def shifts(count, step):
    return [(i, (i + step) % count) for i in range(count)]


def mm(a, b, contract=(((1,), (0,)), ((), ()))):
    return lax.dot_general(a, b, contract, preferred_element_type=f32)


def in_hbm(x):
    return pltpu.with_memory_space_constraint(x, pltpu.HBM)


def shape_of(shape, kind, where=pltpu.VMEM):
    return where(shape, kind)


def call(body, outs, flops, moved, **extra):
    return pl.pallas_call(
        body,
        out_shape=[shape_of(*out) for out in outs],
        cost_estimate=pl.CostEstimate(flops=flops, bytes_accessed=moved, transcendentals=0),
        compiler_params=pltpu.CompilerParams(vmem_limit_bytes=20 * 1024 * 1024),
        **extra,
    )


def plain(body, outs, flops, moved, *args):
    return call(
        body, outs, flops, moved, in_specs=[VMEM] * len(args), out_specs=[VMEM] * len(outs)
    )(*args)


def feature_map(u):
    return jnp.where(u > 0, u + 1.0, jnp.exp(jnp.minimum(u, 0.0)))


def low_lanes(shape):
    return lax.broadcasted_iota(jnp.int32, shape, len(shape) - 1) < HD


def one_head(x, head):
    low = low_lanes(x.shape)
    keep = low if head == 0 else jnp.logical_not(low)
    return jnp.where(keep, x, jnp.zeros_like(x))


def pack(full):
    return jnp.where(low_lanes((HD, LANES)), full[:HD], full[HD:])


def unpack(rows):
    low = low_lanes((HD, LANES))
    zero = jnp.zeros_like(rows)
    return jnp.concatenate([jnp.where(low, rows, zero), jnp.where(low, zero, rows)], axis=0)


def head_ones():
    r = lax.broadcasted_iota(jnp.int32, (LANES, LANES), 0) < HD
    c = lax.broadcasted_iota(jnp.int32, (LANES, LANES), 1) < HD
    return jnp.where(r == c, 1.0, 0.0).astype(bf16)


def half_at(other, half):
    side = lax.axis_index("seq_2")
    side = 1 - side if other else side
    return pl.ds(pl.multiple_of(side * half, 16), half)


def whole_state(later, mine_ref, got_ref, pair_ref, state_ref):
    half = mine_ref.shape[0]
    last = lax.axis_index("seq_2") == (0 if later else 1)
    state_ref[half_at(False, half), :] = mine_ref[...].astype(f32)
    state_ref[half_at(True, half), :] = got_ref[...].astype(f32)
    state_ref[...] += jnp.where(last, pair_ref[...].astype(f32), 0.0)


def pair_sum(state, pair):
    half = state.shape[0] // 2

    def body(state_ref, pair_ref, chip_ref):
        own = half_at(False, half)
        chip_ref[...] = (state_ref[own, :].astype(f32) + pair_ref[own, :].astype(f32)).astype(bf16)

    return plain(body, [((half, LANES), bf16)], 1, half * 1024, state, pair)[0]


def plane_sums(later, chip, got):
    half = chip.shape[0]

    def body(chip_ref, g1, g2, g3, planes_ref):
        y = lax.axis_index("seq_1")
        y = 3 - y if later else y
        total = chip_ref[...].astype(f32)
        inside = jnp.zeros_like(total)
        for k, ref in ((1, g1), (2, g2), (3, g3)):
            piece = ref[...].astype(f32)
            total = total + piece
            inside = inside + jnp.where(y >= k, piece, 0.0)
        planes_ref[...] = jnp.broadcast_to(total.astype(bf16)[None], planes_ref.shape)
        planes_ref[pl.ds(lax.axis_index("seq_0"), 1)] = inside.astype(bf16)[None]

    outs = [((8, half, LANES), bf16, pltpu.HBM)]
    return plain(body, outs, 1, half * 4096, chip, *got)[0]


def before_chip(later, planes):
    half = planes.shape[1]

    def body(planes_ref, send_ref):
        z = lax.axis_index("seq_0")
        total = jnp.zeros((half, LANES), f32)
        for k in range(8):
            take = (z <= k) if later else (z >= k)
            total = total + jnp.where(take, planes_ref[k].astype(f32), 0.0)
        send_ref[...] = total.astype(bf16)

    return plain(body, [((half, LANES), bf16)], 1, half * 4096, planes)[0]


def plane_exchange(planes):
    return lax.all_to_all(planes, "seq_0", 0, 0, tiled=True)


def swap(x):
    return lax.ppermute(x, "seq_2", SWAP)


def y_gather(later, chip):
    got = []
    for k in (2, 1, 3):
        got.append(lax.ppermute(chip, "seq_1", shifts(4, -k if later else k)))
    return got[1], got[0], got[2]


def key_value(latents, w_key, w_value):
    rows, width = (latents.shape[0], w_key.shape[1])
    steps = 4
    depth = latents.shape[1] // steps

    def body(x_hbm, wk_hbm, wv_hbm, fk_ref, v_ref, state_ref, x_ref, w_ref, sem):
        copies = []
        for i in range(steps):
            span = pl.ds(i * depth, depth)
            copies.append(
                [
                    pltpu.make_async_copy(src, dst, sem.at[3 * i + j])
                    for j, (src, dst) in enumerate(
                        (
                            (x_hbm.at[:, span], x_ref.at[:, span]),
                            (wk_hbm.at[span, :], w_ref.at[span, pl.ds(0, width)]),
                            (wv_hbm.at[span, :], w_ref.at[span, pl.ds(width, width)]),
                        )
                    )
                ]
            )
        for group in copies:
            for copy in group:
                copy.start()
        total = None
        for i, group in enumerate(copies):
            for copy in group:
                copy.wait()
            span = slice(i * depth, (i + 1) * depth)
            part = mm(x_ref[:, span], w_ref[span, :])
            total = part if total is None else total + part
        fk_ref[...] = feature_map(total[:, :width]).astype(bf16)
        v_ref[...] = total[:, width:].astype(bf16)
        for p in range(width // LANES):
            cols = slice(p * LANES, (p + 1) * LANES)
            state_ref[p * HD : (p + 1) * HD, :] = pack(
                mm(fk_ref[:, cols], v_ref[:, cols], TN)
            ).astype(bf16)

    hbm = pl.BlockSpec(memory_space=pltpu.HBM)
    return call(
        body,
        [
            ((rows, width), bf16),
            ((rows, width), bf16),
            ((width * HD // LANES, LANES), bf16),
        ],
        4 * rows * width * latents.shape[1],
        3 * 1024 * 1024,
        in_specs=[hbm] * 3,
        out_specs=[VMEM] * 3,
        scratch_shapes=[
            pltpu.VMEM(latents.shape, bf16),
            pltpu.VMEM((latents.shape[1], 2 * width), bf16),
            pltpu.SemaphoreType.DMA((3 * steps,)),
        ],
    )(in_hbm(latents), in_hbm(w_key), in_hbm(w_value))


def tri(rows, upper):
    t = lax.broadcasted_iota(jnp.int32, (rows, rows), 0)
    s = lax.broadcasted_iota(jnp.int32, (rows, rows), 1)
    return (t <= s) if upper else (t >= s)


def masked(scores, keep):
    return jnp.where(keep, scores, 0.0).astype(bf16)


def query_local(latents, w_query, fk, v):
    rows, width = fk.shape
    steps = 2
    depth = latents.shape[1] // steps

    def body(x_hbm, wq_ref, fk_ref, v_ref, fq_ref, raw_ref, x_ref, sem):
        spans = [pl.ds(i * depth, depth) for i in range(steps)]
        copies = [
            pltpu.make_async_copy(x_hbm.at[:, span], x_ref.at[:, span], sem.at[i])
            for i, span in enumerate(spans)
        ]
        for copy in copies:
            copy.start()
        total = jnp.zeros((rows, width), f32)
        for copy, span in zip(copies, spans):
            copy.wait()
            total = total + mm(x_ref[:, span], wq_ref[span, :])
        fq_ref[...] = feature_map(total).astype(bf16)
        keep = tri(rows, False)
        for p in range(width // LANES):
            cols = slice(p * LANES, (p + 1) * LANES)
            q, k, val = (fq_ref[:, cols], fk_ref[:, cols], v_ref[:, cols])
            total = None
            for h in (0, 1):
                score = masked(mm(q, one_head(k, h), NT), keep)
                part = mm(score, one_head(val, h))
                total = part if total is None else total + part
            raw_ref[:, cols] = total.astype(bf16)

    return call(
        body,
        [((rows, width), bf16)] * 2,
        2 * rows * width * (latents.shape[1] + 4 * rows),
        3 * 1024 * 1024,
        in_specs=[pl.BlockSpec(memory_space=pltpu.HBM)] + [VMEM] * 3,
        out_specs=[VMEM] * 2,
        scratch_shapes=[pltpu.VMEM(latents.shape, bf16), pltpu.SemaphoreType.DMA((steps,))],
    )(in_hbm(latents), w_query, fk, v)


def upstream_of(grads, w_out, gain):
    rows, width = grads[0].shape

    def body(g0, g1, g2, g3, w_hbm, gain_ref, up_ref, w_ref, sem):
        m = lax.axis_index("mp")
        copies = []
        for k in range(4):
            at = pl.multiple_of(lax.rem(m + 4 - k, 4) * width, LANES)
            copies.append(
                pltpu.make_async_copy(w_hbm.at[:, pl.ds(at, width)], w_ref.at[k], sem.at[k])
            )
        for copy in copies:
            copy.start()
        total = jnp.zeros((rows, width), f32)
        for k, ref in enumerate((g0, g1, g2, g3)):
            copies[k].wait()
            total = total + mm(ref[...], w_ref[k], NT)
        up_ref[...] = (total * gain_ref[...]).astype(bf16)

    return call(
        body,
        [((rows, width), bf16)],
        8 * rows * width * width,
        3 * 1024 * 1024,
        in_specs=[VMEM] * 4 + [pl.BlockSpec(memory_space=pltpu.HBM), VMEM],
        out_specs=[VMEM],
        scratch_shapes=[pltpu.VMEM((4, width, width), bf16), pltpu.SemaphoreType.DMA((4,))],
    )(*grads, in_hbm(w_out), gain)[0]


def normed(mine, got, pair, fq, raw_local, up, gain):
    rows, width = fq.shape
    half = mine.shape[0]

    def body(
        mine_ref,
        got_ref,
        pair_ref,
        fq_ref,
        raw_ref,
        up_ref,
        gain_ref,
        attn_ref,
        draw_ref,
        before_ref,
        after_ref,
        state,
    ):
        whole_state(False, mine_ref, got_ref, pair_ref, state)
        before_ref[...] = state[...].astype(bf16)
        ones = head_ones()
        for p in range(width // LANES):
            cols = slice(p * LANES, (p + 1) * LANES)
            q = fq_ref[:, cols]
            raw = raw_ref[:, cols].astype(f32) + mm(q, unpack(before_ref[p * HD : (p + 1) * HD, :]))
            upstream = up_ref[:, cols].astype(f32)
            square = mm((raw * raw).astype(bf16), ones) * (1.0 / HD)
            cross = mm((raw * upstream).astype(bf16), ones) * (1.0 / HD)
            inv = lax.rsqrt(square + epsilon)
            unit = raw * inv
            attn_ref[:, cols] = (unit * gain_ref[:, cols]).astype(bf16)
            draw = (inv * upstream - inv * inv * unit * cross).astype(bf16)
            draw_ref[:, cols] = draw
            after_ref[p * HD : (p + 1) * HD, :] = pack(mm(q, draw, TN)).astype(bf16)

    return call(
        body,
        [
            ((rows, width), bf16),
            ((rows, width), bf16),
            ((2 * half, LANES), bf16),
            ((2 * half, LANES), bf16),
        ],
        8 * rows * width * LANES,
        2 * 1024 * 1024,
        in_specs=[VMEM] * 7,
        out_specs=[VMEM] * 4,
        scratch_shapes=[pltpu.VMEM((2 * half, LANES), f32)],
    )(mine, got, pair, fq, raw_local, up, gain)


def branch_parts(attn, w_out):
    rows, width = attn.shape

    def body(attn_ref, w_ref, *outs):
        for k, ref in zip((2, 1, 3, 0), outs):
            ref[...] = mm(attn_ref[...], w_ref[:, block_rows(k, width)]).astype(bf16)

    return plain(
        body,
        [((rows, width), bf16, pltpu.HBM)] * 4,
        8 * rows * width * width,
        2 * 1024 * 1024,
        attn,
        w_out,
    )


def local_grads(fq, fk, v, draw, before):
    rows, width = fq.shape

    def body(fq_ref, fk_ref, v_ref, draw_ref, before_ref, dq_ref, dk_ref, dv_ref):
        lower, upper = (tri(rows, False), tri(rows, True))
        for p in range(width // LANES):
            cols = slice(p * LANES, (p + 1) * LANES)
            q, k, val, dr = (fq_ref[:, cols], fk_ref[:, cols], v_ref[:, cols], draw_ref[:, cols])
            dq = mm(dr, unpack(before_ref[p * HD : (p + 1) * HD, :]), NT)
            dk, dv = (None, None)
            for h in (0, 1):
                val_h, k_h, q_h, dr_h = (one_head(a, h) for a in (val, k, q, dr))
                dq = dq + mm(masked(mm(dr, val_h, NT), lower), k_h)
                dk_h = mm(masked(mm(val_h, dr, NT), upper), q_h)
                dv_h = mm(masked(mm(k_h, q, NT), upper), dr_h)
                dk = dk_h if dk is None else dk + dk_h
                dv = dv_h if dv is None else dv + dv_h
            dq_ref[:, cols] = (dq * jnp.minimum(q.astype(f32), 1.0)).astype(bf16)
            dk_ref[:, cols] = dk.astype(bf16)
            dv_ref[:, cols] = dv.astype(bf16)

    return plain(
        body,
        [((rows, width), bf16)] * 3,
        24 * rows * rows * width,
        3 * 1024 * 1024,
        fq,
        fk,
        v,
        draw,
        before,
    )


def block_rows(k, width):
    at = lax.rem(lax.axis_index("mp") + k, 4) * width
    return pl.ds(pl.multiple_of(at, LANES), width)


def block_copies(k, sources, targets, sem, first):
    width = sources[0].shape[1]
    return [
        pltpu.make_async_copy(src.at[block_rows(k, width), :], dst, sem.at[first + i])
        for i, (src, dst) in enumerate(zip(sources, targets))
    ]


def weight_blocks(k, weights):
    width = weights[0].shape[1]

    def body(*refs):
        copies = block_copies(k, refs[:3], refs[3:6], refs[6], 0)
        for copy in copies:
            copy.start()
        for copy in copies:
            copy.wait()

    return call(
        body,
        [((width, width), bf16)] * 3,
        1,
        1024 * 1024,
        in_specs=[pl.BlockSpec(memory_space=pltpu.HBM)] * 3,
        out_specs=[VMEM] * 3,
        scratch_shapes=[pltpu.SemaphoreType.DMA((3,))],
    )(*(in_hbm(w) for w in weights))


def first_part(mine, got, pair, fk, v, dq, dk, dv, blocks):
    rows, width = fk.shape
    half = mine.shape[0]

    def body(
        mine_ref,
        got_ref,
        pair_ref,
        fk_ref,
        v_ref,
        dq_ref,
        dkl_ref,
        dvl_ref,
        wq_ref,
        wk_ref,
        wv_ref,
        dk_ref,
        dv_ref,
        part_ref,
        state,
    ):
        whole_state(True, mine_ref, got_ref, pair_ref, state)
        for p in range(width // LANES):
            cols = slice(p * LANES, (p + 1) * LANES)
            after = unpack(state[p * HD : (p + 1) * HD, :].astype(bf16))
            k = fk_ref[:, cols]
            dk = dkl_ref[:, cols].astype(f32) + mm(v_ref[:, cols], after, NT)
            dk_ref[:, cols] = (dk * jnp.minimum(k.astype(f32), 1.0)).astype(bf16)
            dv_ref[:, cols] = (dvl_ref[:, cols].astype(f32) + mm(k, after)).astype(bf16)
        total = mm(dq_ref[...], wq_ref[...], NT)
        total = total + mm(dk_ref[...], wk_ref[...], NT)
        part_ref[...] = (total + mm(dv_ref[...], wv_ref[...], NT)).astype(bf16)

    return call(
        body,
        [((rows, width), bf16)] * 3,
        6 * rows * width * width,
        2 * 1024 * 1024,
        in_specs=[VMEM] * 11,
        out_specs=[VMEM] * 3,
        scratch_shapes=[pltpu.VMEM((2 * half, LANES), f32)],
    )(mine, got, pair, fk, v, dq, dk, dv, *blocks)


def other_parts(which, dq, dk, dv, weights):
    rows, width = dq.shape
    count = len(which)

    def body(dq_ref, dk_ref, dv_ref, wq_hbm, wk_hbm, wv_hbm, *refs):
        outs, blocks, sem = (refs[:count], refs[count], refs[count + 1])
        copies = [
            block_copies(
                k, (wq_hbm, wk_hbm, wv_hbm), [blocks.at[3 * i + j] for j in range(3)], sem, 3 * i
            )
            for i, k in enumerate(which)
        ]
        for group in copies:
            for copy in group:
                copy.start()
        for i, (group, ref) in enumerate(zip(copies, outs)):
            for copy in group:
                copy.wait()
            total = None
            for j, grad_ref in enumerate((dq_ref, dk_ref, dv_ref)):
                part = mm(grad_ref[...], blocks[3 * i + j], NT)
                total = part if total is None else total + part
            ref[...] = total.astype(bf16)

    hbm = pl.BlockSpec(memory_space=pltpu.HBM)
    return call(
        body,
        [((rows, width), bf16)] * count,
        6 * rows * width * width * count,
        1024 * 1024 * count,
        in_specs=[VMEM] * 3 + [hbm] * 3,
        out_specs=[VMEM] * count,
        scratch_shapes=[
            pltpu.VMEM((3 * count, width, width), bf16),
            pltpu.SemaphoreType.DMA((3 * count,)),
        ],
    )(dq, dk, dv, *(in_hbm(w) for w in weights))


def add_up(parts):
    total = parts[0].astype(f32)
    for part in parts[1:]:
        total = total + part.astype(f32)
    return total.astype(bf16)


def to_owner(part, k):
    return lax.ppermute(part, "mp", shifts(4, k))


def hold(x, anchor):
    return lax.optimization_barrier((x, anchor))[0]


def per_device(latents, w_query, w_key, w_value, w_out, head_gain, grad_out):
    gain = head_gain.reshape(1, -1)
    fk, v, state = key_value(latents, w_key, w_value)
    pair = swap(state)
    chip = pair_sum(state, pair)
    got = y_gather(False, chip)
    grad_held = hold(grad_out, chip)
    grads = [grad_out] + [to_owner(grad_held, k) for k in (1, 2, 3)]
    planes = plane_sums(False, chip, got)
    fq, raw_local = query_local(hold(latents, planes), w_query, fk, v)
    up = upstream_of(grads, w_out, gain)
    planes = plane_exchange(planes)
    mine = before_chip(False, planes)
    got = swap(mine)
    attn, draw, before, state = normed(mine, got, pair, fq, raw_local, up, gain)
    weights = (w_query, w_key, w_value)
    blocks = weight_blocks(2, (hold(w_query, state), w_key, w_value))
    pair = swap(state)
    chip = pair_sum(state, pair)
    got = y_gather(True, chip)
    b2, b1, b3, b0 = branch_parts(hold(attn, chip), w_out)
    planes = plane_sums(True, chip, got)
    b2, b1, b3 = (hold(b, planes) for b in (b2, b1, b3))
    branch = [b0, to_owner(b2, 2), to_owner(b1, 1), to_owner(b3, 3)]
    dq, dk_local, dv_local = local_grads(fq, fk, v, hold(draw, planes), before)
    planes = plane_exchange(planes)
    mine = before_chip(True, planes)
    got = swap(mine)
    dk, dv, l2 = first_part(mine, got, pair, fk, v, dq, dk_local, dv_local, blocks)
    l2 = to_owner(l2, 2)
    l1, l3 = other_parts((1, 3), dq, dk, dv, weights)
    l1, l3 = (to_owner(l1, 1), to_owner(l3, 3))
    (l0,) = other_parts((0,), dq, dk, dv, weights)
    return (add_up(branch), add_up([l0, l2, l1, l3]))


def solution(mesh):
    split = Mesh(mesh.devices.reshape(8, 4, 2, mesh.shape["mp"]), (*SEQ, "mp"))
    in_specs = (
        P(SEQ, None),
        P(None, "mp"),
        P(None, "mp"),
        P(None, "mp"),
        P("mp", None),
        P("mp"),
        P(SEQ, "mp"),
    )
    out_specs = (P(SEQ, "mp"), P(SEQ, "mp"))
    return jax.shard_map(
        per_device, mesh=split, in_specs=in_specs, out_specs=out_specs, check_vma=False
    )
```

```python
import jax
import jax.numpy as jnp
from jax import lax
from jax.experimental import pallas as pl
from jax.experimental.pallas import tpu as pltpu
from jax.sharding import Mesh
from jax.sharding import PartitionSpec as P


HD = 64
LANES = 128
SEQ = ("seq_0", "seq_1", "seq_2")
SWAP = [(0, 1), (1, 0)]
epsilon = 1e-06
f32, bf16 = (jnp.float32, jnp.bfloat16)
NT = (((1,), (1,)), ((), ()))
TN = (((0,), (0,)), ((), ()))
VMEM = pl.BlockSpec(memory_space=pltpu.VMEM)


def shifts(count, step):
    return [(i, (i + step) % count) for i in range(count)]


def mm(a, b, contract=(((1,), (0,)), ((), ()))):
    return lax.dot_general(a, b, contract, preferred_element_type=f32)


def in_hbm(x):
    return pltpu.with_memory_space_constraint(x, pltpu.HBM)


def shape_of(shape, kind, where=pltpu.VMEM):
    return where(shape, kind)


def call(body, outs, flops, moved, **extra):
    return pl.pallas_call(
        body,
        out_shape=[shape_of(*out) for out in outs],
        cost_estimate=pl.CostEstimate(flops=flops, bytes_accessed=moved, transcendentals=0),
        compiler_params=pltpu.CompilerParams(vmem_limit_bytes=20 * 1024 * 1024),
        **extra,
    )


def plain(body, outs, flops, moved, *args):
    return call(
        body, outs, flops, moved, in_specs=[VMEM] * len(args), out_specs=[VMEM] * len(outs)
    )(*args)


def feature_map(u):
    return jnp.where(u > 0, u + 1.0, jnp.exp(jnp.minimum(u, 0.0)))


def low_lanes(shape):
    return lax.broadcasted_iota(jnp.int32, shape, len(shape) - 1) < HD


def one_head(x, head):
    low = low_lanes(x.shape)
    keep = low if head == 0 else jnp.logical_not(low)
    return jnp.where(keep, x, jnp.zeros_like(x))


def pack(full):
    return jnp.where(low_lanes((HD, LANES)), full[:HD], full[HD:])


def unpack(rows):
    low = low_lanes((HD, LANES))
    zero = jnp.zeros_like(rows)
    return jnp.concatenate([jnp.where(low, rows, zero), jnp.where(low, zero, rows)], axis=0)


def head_ones():
    r = lax.broadcasted_iota(jnp.int32, (LANES, LANES), 0) < HD
    c = lax.broadcasted_iota(jnp.int32, (LANES, LANES), 1) < HD
    return jnp.where(r == c, 1.0, 0.0).astype(bf16)


def half_at(other, half):
    side = lax.axis_index("seq_2")
    side = 1 - side if other else side
    return pl.ds(pl.multiple_of(side * half, 16), half)


def whole_state(later, mine_ref, got_ref, pair_ref, state_ref):
    half = mine_ref.shape[0]
    last = lax.axis_index("seq_2") == (0 if later else 1)
    state_ref[half_at(False, half), :] = mine_ref[...].astype(f32)
    state_ref[half_at(True, half), :] = got_ref[...].astype(f32)
    state_ref[...] += jnp.where(last, pair_ref[...].astype(f32), 0.0)


def pair_sum(state, pair):
    half = state.shape[0] // 2

    def body(state_ref, pair_ref, chip_ref):
        own = half_at(False, half)
        chip_ref[...] = (state_ref[own, :].astype(f32) + pair_ref[own, :].astype(f32)).astype(bf16)

    return plain(body, [((half, LANES), bf16)], 1, half * 1024, state, pair)[0]


def plane_sums(later, chip, got):
    half = chip.shape[0]

    def body(chip_ref, g1, g2, g3, planes_ref):
        y = lax.axis_index("seq_1")
        y = 3 - y if later else y
        total = chip_ref[...].astype(f32)
        inside = jnp.zeros_like(total)
        for k, ref in ((1, g1), (2, g2), (3, g3)):
            piece = ref[...].astype(f32)
            total = total + piece
            inside = inside + jnp.where(y >= k, piece, 0.0)
        planes_ref[...] = jnp.broadcast_to(total.astype(bf16)[None], planes_ref.shape)
        planes_ref[pl.ds(lax.axis_index("seq_0"), 1)] = inside.astype(bf16)[None]

    outs = [((8, half, LANES), bf16, pltpu.HBM)]
    return plain(body, outs, 1, half * 4096, chip, *got)[0]


def before_chip(later, planes):
    half = planes.shape[1]

    def body(planes_ref, send_ref):
        z = lax.axis_index("seq_0")
        total = jnp.zeros((half, LANES), f32)
        for k in range(8):
            take = (z <= k) if later else (z >= k)
            total = total + jnp.where(take, planes_ref[k].astype(f32), 0.0)
        send_ref[...] = total.astype(bf16)

    return plain(body, [((half, LANES), bf16)], 1, half * 4096, planes)[0]


def plane_exchange(planes):
    return lax.all_to_all(planes, "seq_0", 0, 0, tiled=True)


def swap(x):
    return lax.ppermute(x, "seq_2", SWAP)


def y_gather(later, chip):
    got = []
    for k in (2, 1, 3):
        got.append(lax.ppermute(chip, "seq_1", shifts(4, -k if later else k)))
    return got[1], got[0], got[2]


def key_value(latents, w_key, w_value):
    rows, width = (latents.shape[0], w_key.shape[1])
    steps = 4
    depth = latents.shape[1] // steps

    def body(x_hbm, wk_hbm, wv_hbm, fk_ref, v_ref, state_ref, x_ref, w_ref, sem):
        copies = []
        for i in range(steps):
            span = pl.ds(i * depth, depth)
            copies.append(
                [
                    pltpu.make_async_copy(src, dst, sem.at[3 * i + j])
                    for j, (src, dst) in enumerate(
                        (
                            (x_hbm.at[:, span], x_ref.at[:, span]),
                            (wk_hbm.at[span, :], w_ref.at[span, pl.ds(0, width)]),
                            (wv_hbm.at[span, :], w_ref.at[span, pl.ds(width, width)]),
                        )
                    )
                ]
            )
        for group in copies:
            for copy in group:
                copy.start()
        total = None
        for i, group in enumerate(copies):
            for copy in group:
                copy.wait()
            span = slice(i * depth, (i + 1) * depth)
            part = mm(x_ref[:, span], w_ref[span, :])
            total = part if total is None else total + part
        fk_ref[...] = feature_map(total[:, :width]).astype(bf16)
        v_ref[...] = total[:, width:].astype(bf16)
        for p in range(width // LANES):
            cols = slice(p * LANES, (p + 1) * LANES)
            state_ref[p * HD : (p + 1) * HD, :] = pack(
                mm(fk_ref[:, cols], v_ref[:, cols], TN)
            ).astype(bf16)

    hbm = pl.BlockSpec(memory_space=pltpu.HBM)
    return call(
        body,
        [
            ((rows, width), bf16),
            ((rows, width), bf16),
            ((width * HD // LANES, LANES), bf16),
        ],
        4 * rows * width * latents.shape[1],
        3 * 1024 * 1024,
        in_specs=[hbm] * 3,
        out_specs=[VMEM] * 3,
        scratch_shapes=[
            pltpu.VMEM(latents.shape, bf16),
            pltpu.VMEM((latents.shape[1], 2 * width), bf16),
            pltpu.SemaphoreType.DMA((3 * steps,)),
        ],
    )(in_hbm(latents), in_hbm(w_key), in_hbm(w_value))


def tri(rows, upper):
    t = lax.broadcasted_iota(jnp.int32, (rows, rows), 0)
    s = lax.broadcasted_iota(jnp.int32, (rows, rows), 1)
    return (t <= s) if upper else (t >= s)


def masked(scores, keep):
    return jnp.where(keep, scores, 0.0).astype(bf16)


def query_local(latents, w_query, fk, v):
    rows, width = fk.shape
    steps = 2
    depth = latents.shape[1] // steps

    def body(x_hbm, wq_ref, fk_ref, v_ref, fq_ref, raw_ref, x_ref, sem):
        spans = [pl.ds(i * depth, depth) for i in range(steps)]
        copies = [
            pltpu.make_async_copy(x_hbm.at[:, span], x_ref.at[:, span], sem.at[i])
            for i, span in enumerate(spans)
        ]
        for copy in copies:
            copy.start()
        total = jnp.zeros((rows, width), f32)
        for copy, span in zip(copies, spans):
            copy.wait()
            total = total + mm(x_ref[:, span], wq_ref[span, :])
        fq_ref[...] = feature_map(total).astype(bf16)
        keep = tri(rows, False)
        for p in range(width // LANES):
            cols = slice(p * LANES, (p + 1) * LANES)
            q, k, val = (fq_ref[:, cols], fk_ref[:, cols], v_ref[:, cols])
            total = None
            for h in (0, 1):
                score = masked(mm(q, one_head(k, h), NT), keep)
                part = mm(score, one_head(val, h))
                total = part if total is None else total + part
            raw_ref[:, cols] = total.astype(bf16)

    return call(
        body,
        [((rows, width), bf16)] * 2,
        2 * rows * width * (latents.shape[1] + 4 * rows),
        3 * 1024 * 1024,
        in_specs=[pl.BlockSpec(memory_space=pltpu.HBM)] + [VMEM] * 3,
        out_specs=[VMEM] * 2,
        scratch_shapes=[pltpu.VMEM(latents.shape, bf16), pltpu.SemaphoreType.DMA((steps,))],
    )(in_hbm(latents), w_query, fk, v)


def upstream_of(grads, w_out, gain):
    rows, width = grads[0].shape

    def body(g0, g1, g2, g3, w_hbm, gain_ref, up_ref, w_ref, sem):
        m = lax.axis_index("mp")
        copies = []
        for k in range(4):
            at = pl.multiple_of(lax.rem(m + 4 - k, 4) * width, LANES)
            copies.append(
                pltpu.make_async_copy(w_hbm.at[:, pl.ds(at, width)], w_ref.at[k], sem.at[k])
            )
        for copy in copies:
            copy.start()
        total = jnp.zeros((rows, width), f32)
        for k, ref in enumerate((g0, g1, g2, g3)):
            copies[k].wait()
            total = total + mm(ref[...], w_ref[k], NT)
        up_ref[...] = (total * gain_ref[...]).astype(bf16)

    return call(
        body,
        [((rows, width), bf16)],
        8 * rows * width * width,
        3 * 1024 * 1024,
        in_specs=[VMEM] * 4 + [pl.BlockSpec(memory_space=pltpu.HBM), VMEM],
        out_specs=[VMEM],
        scratch_shapes=[pltpu.VMEM((4, width, width), bf16), pltpu.SemaphoreType.DMA((4,))],
    )(*grads, in_hbm(w_out), gain)[0]


def normed(mine, got, pair, fq, raw_local, up, gain):
    rows, width = fq.shape
    half = mine.shape[0]

    def body(
        mine_ref,
        got_ref,
        pair_ref,
        fq_ref,
        raw_ref,
        up_ref,
        gain_ref,
        attn_ref,
        draw_ref,
        before_ref,
        after_ref,
        state,
    ):
        whole_state(False, mine_ref, got_ref, pair_ref, state)
        before_ref[...] = state[...].astype(bf16)
        ones = head_ones()
        for p in range(width // LANES):
            cols = slice(p * LANES, (p + 1) * LANES)
            q = fq_ref[:, cols]
            raw = raw_ref[:, cols].astype(f32) + mm(q, unpack(before_ref[p * HD : (p + 1) * HD, :]))
            upstream = up_ref[:, cols].astype(f32)
            square = mm((raw * raw).astype(bf16), ones) * (1.0 / HD)
            cross = mm((raw * upstream).astype(bf16), ones) * (1.0 / HD)
            inv = lax.rsqrt(square + epsilon)
            unit = raw * inv
            attn_ref[:, cols] = (unit * gain_ref[:, cols]).astype(bf16)
            draw = (inv * upstream - inv * inv * unit * cross).astype(bf16)
            draw_ref[:, cols] = draw
            after_ref[p * HD : (p + 1) * HD, :] = pack(mm(q, draw, TN)).astype(bf16)

    return call(
        body,
        [
            ((rows, width), bf16),
            ((rows, width), bf16),
            ((2 * half, LANES), bf16),
            ((2 * half, LANES), bf16),
        ],
        8 * rows * width * LANES,
        2 * 1024 * 1024,
        in_specs=[VMEM] * 7,
        out_specs=[VMEM] * 4,
        scratch_shapes=[pltpu.VMEM((2 * half, LANES), f32)],
    )(mine, got, pair, fq, raw_local, up, gain)


def branch_parts(attn, w_out):
    rows, width = attn.shape

    def body(attn_ref, w_ref, *outs):
        for k, ref in zip((2, 1, 3, 0), outs):
            ref[...] = mm(attn_ref[...], w_ref[:, block_rows(k, width)]).astype(bf16)

    return plain(
        body,
        [((rows, width), bf16, pltpu.HBM)] * 4,
        8 * rows * width * width,
        2 * 1024 * 1024,
        attn,
        w_out,
    )


def local_grads(fq, fk, v, draw, before):
    rows, width = fq.shape

    def body(fq_ref, fk_ref, v_ref, draw_ref, before_ref, dq_ref, dk_ref, dv_ref):
        lower, upper = (tri(rows, False), tri(rows, True))
        for p in range(width // LANES):
            cols = slice(p * LANES, (p + 1) * LANES)
            q, k, val, dr = (fq_ref[:, cols], fk_ref[:, cols], v_ref[:, cols], draw_ref[:, cols])
            dq = mm(dr, unpack(before_ref[p * HD : (p + 1) * HD, :]), NT)
            dk, dv = (None, None)
            for h in (0, 1):
                val_h, k_h, q_h, dr_h = (one_head(a, h) for a in (val, k, q, dr))
                dq = dq + mm(masked(mm(dr, val_h, NT), lower), k_h)
                dk_h = mm(masked(mm(val_h, dr, NT), upper), q_h)
                dv_h = mm(masked(mm(k_h, q, NT), upper), dr_h)
                dk = dk_h if dk is None else dk + dk_h
                dv = dv_h if dv is None else dv + dv_h
            dq_ref[:, cols] = (dq * jnp.minimum(q.astype(f32), 1.0)).astype(bf16)
            dk_ref[:, cols] = dk.astype(bf16)
            dv_ref[:, cols] = dv.astype(bf16)

    return plain(
        body,
        [((rows, width), bf16)] * 3,
        24 * rows * rows * width,
        3 * 1024 * 1024,
        fq,
        fk,
        v,
        draw,
        before,
    )


def block_rows(k, width):
    at = lax.rem(lax.axis_index("mp") + k, 4) * width
    return pl.ds(pl.multiple_of(at, LANES), width)


def block_copies(k, sources, targets, sem, first):
    width = sources[0].shape[1]
    return [
        pltpu.make_async_copy(src.at[block_rows(k, width), :], dst, sem.at[first + i])
        for i, (src, dst) in enumerate(zip(sources, targets))
    ]


def weight_blocks(which, weights):
    width = weights[0].shape[1]
    count = 3 * len(which)

    def body(*refs):
        sources, targets, sem = (refs[:3], refs[3 : 3 + count], refs[3 + count])
        copies = []
        for i, k in enumerate(which):
            copies += block_copies(k, sources, targets[3 * i : 3 * i + 3], sem, 3 * i)
        for copy in copies:
            copy.start()
        for copy in copies:
            copy.wait()

    return call(
        body,
        [((width, width), bf16)] * count,
        1,
        1024 * 1024,
        in_specs=[pl.BlockSpec(memory_space=pltpu.HBM)] * 3,
        out_specs=[VMEM] * count,
        scratch_shapes=[pltpu.SemaphoreType.DMA((count,))],
    )(*(in_hbm(w) for w in weights))


def first_part(mine, got, pair, fk, v, dq, dk, dv, blocks):
    rows, width = fk.shape
    half = mine.shape[0]

    def body(
        mine_ref,
        got_ref,
        pair_ref,
        fk_ref,
        v_ref,
        dq_ref,
        dkl_ref,
        dvl_ref,
        wq_ref,
        wk_ref,
        wv_ref,
        dk_ref,
        dv_ref,
        upper_ref,
        lower_ref,
        state,
    ):
        whole_state(True, mine_ref, got_ref, pair_ref, state)
        for p in range(width // LANES):
            cols = slice(p * LANES, (p + 1) * LANES)
            after = unpack(state[p * HD : (p + 1) * HD, :].astype(bf16))
            k = fk_ref[:, cols]
            dk = dkl_ref[:, cols].astype(f32) + mm(v_ref[:, cols], after, NT)
            dk_ref[:, cols] = (dk * jnp.minimum(k.astype(f32), 1.0)).astype(bf16)
            dv_ref[:, cols] = (dvl_ref[:, cols].astype(f32) + mm(k, after)).astype(bf16)
        total = mm(dq_ref[...], wq_ref[...], NT)
        total = total + mm(dk_ref[...], wk_ref[...], NT)
        total = (total + mm(dv_ref[...], wv_ref[...], NT)).astype(bf16)
        upper_ref[...] = total[: rows // 2]
        lower_ref[...] = total[rows // 2 :]

    return call(
        body,
        [((rows, width), bf16)] * 2 + [((rows // 2, width), bf16)] * 2,
        6 * rows * width * width,
        2 * 1024 * 1024,
        in_specs=[VMEM] * 11,
        out_specs=[VMEM] * 4,
        scratch_shapes=[pltpu.VMEM((2 * half, LANES), f32)],
    )(mine, got, pair, fk, v, dq, dk, dv, *blocks)


def side_parts(dq, dk, dv, blocks):
    rows, width = dq.shape
    half = rows // 2

    def body(dq_ref, dk_ref, dv_ref, q1, k1, v1, q3, k3, v3, soon1, soon3, late1, late3):
        top, bottom = (slice(0, half), slice(half, rows))
        for weights, soon, late, first in (
            ((q1, k1, v1), soon1, late1, bottom),
            ((q3, k3, v3), soon3, late3, top),
        ):
            total = None
            for grad_ref, w_ref in zip((dq_ref, dk_ref, dv_ref), weights):
                part = mm(grad_ref[...], w_ref[...], NT)
                total = part if total is None else total + part
            soon[...] = total[first].astype(bf16)
            late[...] = total[top if first is bottom else bottom]

    return plain(
        body,
        [((half, width), bf16)] * 2 + [((half, width), f32)] * 2,
        12 * rows * width * width,
        2 * 1024 * 1024,
        dq,
        dk,
        dv,
        *blocks,
    )


def marker(x):
    def body(x_ref, out_ref):
        out_ref[...] = x_ref[:8, :LANES]

    return plain(body, [((8, LANES), x.dtype)], 1, 1024, x)[0]


def relayed(late1, late3, far1, far3, mark):
    half, width = far1.shape

    def body(a, b, c, d, _, out1, out3):
        out1[...] = (a[...] + c[...].astype(f32)).astype(bf16)
        out3[...] = (b[...] + d[...].astype(f32)).astype(bf16)

    outs = [((half, width), bf16)] * 2
    return plain(body, outs, 1, 1024 * 1024, late1, late3, far1, far3, mark)


def finished(own, soon3, late1, soon1, late3):
    half = soon1.shape[0]

    def body(own_ref, s3, l1, s1, l3, out_ref):
        for rows, a, b in ((slice(0, half), s3, l1), (slice(half, 2 * half), s1, l3)):
            total = own_ref[rows, :].astype(f32) + a[...].astype(f32) + b[...].astype(f32)
            out_ref[rows, :] = total.astype(bf16)

    outs = [(own.shape, bf16, pltpu.HBM)]
    return plain(body, outs, 1, 1024 * 1024, own, soon3, late1, soon1, late3)[0]


def own_part(dq, dk, dv, weights):
    rows, width = dq.shape

    def body(dq_ref, dk_ref, dv_ref, wq_hbm, wk_hbm, wv_hbm, out_ref, blocks, sem):
        copies = block_copies(0, (wq_hbm, wk_hbm, wv_hbm), [blocks.at[j] for j in range(3)], sem, 0)
        for copy in copies:
            copy.start()
        total = jnp.zeros((rows, width), f32)
        for j, grad_ref in enumerate((dq_ref, dk_ref, dv_ref)):
            copies[j].wait()
            total = total + mm(grad_ref[...], blocks[j], NT)
        out_ref[...] = total.astype(bf16)

    hbm = pl.BlockSpec(memory_space=pltpu.HBM)
    return call(
        body,
        [((rows, width), bf16)],
        6 * rows * width * width,
        1024 * 1024,
        in_specs=[VMEM] * 3 + [hbm] * 3,
        out_specs=[VMEM],
        scratch_shapes=[
            pltpu.VMEM((3, width, width), bf16),
            pltpu.SemaphoreType.DMA((3,)),
        ],
    )(dq, dk, dv, *(in_hbm(w) for w in weights))[0]


def add_up(parts):
    def body(*refs):
        total = refs[0][...].astype(f32)
        for ref in refs[1:-1]:
            total = total + ref[...].astype(f32)
        refs[-1][...] = total.astype(bf16)

    return plain(body, [(parts[0].shape, bf16, pltpu.HBM)], 1, 1024 * 1024, *map(in_hbm, parts))[0]


def to_owner(part, k):
    return lax.ppermute(part, "mp", shifts(4, k))


def hold(x, anchor):
    return lax.optimization_barrier((x, anchor))[0]


def per_device(latents, w_query, w_key, w_value, w_out, head_gain, grad_out):
    gain = head_gain.reshape(1, -1)
    fk, v, state = key_value(latents, w_key, w_value)
    pair = swap(state)
    chip = pair_sum(state, pair)
    got = y_gather(False, chip)
    grad_held = hold(grad_out, chip)
    grads = [grad_out] + [to_owner(grad_held, k) for k in (1, 2, 3)]
    planes = plane_sums(False, chip, got)
    fq, raw_local = query_local(hold(latents, planes), w_query, fk, v)
    up = upstream_of(grads, w_out, gain)
    planes = plane_exchange(planes)
    mine = before_chip(False, planes)
    got = swap(mine)
    attn, draw, before, state = normed(mine, got, pair, fq, raw_local, up, gain)
    weights = (w_query, w_key, w_value)
    blocks = weight_blocks((2,), (hold(w_query, state), w_key, w_value))
    pair = swap(state)
    chip = pair_sum(state, pair)
    got = y_gather(True, chip)
    b2, b1, b3, b0 = branch_parts(hold(attn, chip), w_out)
    planes = plane_sums(True, chip, got)
    b2, b1, b3 = (hold(b, planes) for b in (b2, b1, b3))
    branch = [b0, to_owner(b2, 2), to_owner(b1, 1), to_owner(b3, 3)]
    dq, dk_local, dv_local = local_grads(fq, fk, v, hold(draw, planes), before)
    planes = plane_exchange(planes)
    mine = before_chip(True, planes)
    got = swap(mine)
    others = weight_blocks((1, 3), (hold(w_query, mine), w_key, w_value))
    dk, dv, up2, down2 = first_part(mine, got, pair, fk, v, dq, dk_local, dv_local, blocks)
    far1, far3 = (to_owner(up2, 1), to_owner(down2, 3))
    soon1, soon3, late1, late3 = side_parts(dq, dk, dv, others)
    soon1, soon3 = (to_owner(soon1, 1), to_owner(soon3, 3))
    mark = marker(late1)
    late1, late3 = relayed(late1, late3, far1, far3, mark)
    late1, late3 = (to_owner(late1, 1), to_owner(late3, 3))
    branch = add_up(branch)
    own = own_part(dq, dk, dv, weights)
    return (branch, finished(own, soon3, late1, soon1, late3))


def solution(mesh):
    split = Mesh(mesh.devices.reshape(8, 4, 2, mesh.shape["mp"]), (*SEQ, "mp"))
    in_specs = (
        P(SEQ, None),
        P(None, "mp"),
        P(None, "mp"),
        P(None, "mp"),
        P("mp", None),
        P("mp"),
        P(SEQ, "mp"),
    )
    out_specs = (P(SEQ, "mp"), P(SEQ, "mp"))
    return jax.shard_map(
        per_device, mesh=split, in_specs=in_specs, out_specs=out_specs, check_vma=False
    )
```

```python
import jax
import jax.numpy as jnp
from jax import lax
from jax.experimental import pallas as pl
from jax.experimental.pallas import tpu as pltpu
from jax.sharding import Mesh
from jax.sharding import PartitionSpec as P


HD = 64
LANES = 128
SEQ = ("seq_0", "seq_1", "seq_2")
SWAP = [(0, 1), (1, 0)]
epsilon = 1e-06
f32, bf16 = (jnp.float32, jnp.bfloat16)
NT = (((1,), (1,)), ((), ()))
TN = (((0,), (0,)), ((), ()))
VMEM = pl.BlockSpec(memory_space=pltpu.VMEM)


def shifts(count, step):
    return [(i, (i + step) % count) for i in range(count)]


def mm(a, b, contract=(((1,), (0,)), ((), ()))):
    return lax.dot_general(a, b, contract, preferred_element_type=f32)


def in_hbm(x):
    return pltpu.with_memory_space_constraint(x, pltpu.HBM)


def shape_of(shape, kind, where=pltpu.VMEM):
    return where(shape, kind)


def call(body, outs, flops, moved, **extra):
    return pl.pallas_call(
        body,
        out_shape=[shape_of(*out) for out in outs],
        cost_estimate=pl.CostEstimate(flops=flops, bytes_accessed=moved, transcendentals=0),
        compiler_params=pltpu.CompilerParams(vmem_limit_bytes=20 * 1024 * 1024),
        **extra,
    )


def plain(body, outs, flops, moved, *args):
    return call(
        body, outs, flops, moved, in_specs=[VMEM] * len(args), out_specs=[VMEM] * len(outs)
    )(*args)


def feature_map(u):
    return jnp.where(u > 0, u + 1.0, jnp.exp(jnp.minimum(u, 0.0)))


def low_lanes(shape):
    return lax.broadcasted_iota(jnp.int32, shape, len(shape) - 1) < HD


def one_head(x, head):
    low = low_lanes(x.shape)
    keep = low if head == 0 else jnp.logical_not(low)
    return jnp.where(keep, x, jnp.zeros_like(x))


def pack(full):
    return jnp.where(low_lanes((HD, LANES)), full[:HD], full[HD:])


def unpack(rows):
    low = low_lanes((HD, LANES))
    zero = jnp.zeros_like(rows)
    return jnp.concatenate([jnp.where(low, rows, zero), jnp.where(low, zero, rows)], axis=0)


def head_ones():
    r = lax.broadcasted_iota(jnp.int32, (LANES, LANES), 0) < HD
    c = lax.broadcasted_iota(jnp.int32, (LANES, LANES), 1) < HD
    return jnp.where(r == c, 1.0, 0.0).astype(bf16)


def half_at(other, half):
    side = lax.axis_index("seq_2")
    side = 1 - side if other else side
    return pl.ds(pl.multiple_of(side * half, 16), half)


def whole_state(later, mine_ref, got_ref, pair_ref, state_ref):
    half = mine_ref.shape[0]
    last = lax.axis_index("seq_2") == (0 if later else 1)
    state_ref[half_at(False, half), :] = mine_ref[...].astype(f32)
    state_ref[half_at(True, half), :] = got_ref[...].astype(f32)
    state_ref[...] += jnp.where(last, pair_ref[...].astype(f32), 0.0)


def pair_sum(state, pair):
    half = state.shape[0] // 2

    def body(state_ref, pair_ref, chip_ref):
        own = half_at(False, half)
        chip_ref[...] = (state_ref[own, :].astype(f32) + pair_ref[own, :].astype(f32)).astype(bf16)

    return plain(body, [((half, LANES), bf16)], 1, half * 1024, state, pair)[0]


def plane_sums(later, chip, got):
    half = chip.shape[0]

    def body(chip_ref, g1, g2, g3, planes_ref):
        y = lax.axis_index("seq_1")
        y = 3 - y if later else y
        total = chip_ref[...].astype(f32)
        inside = jnp.zeros_like(total)
        for k, ref in ((1, g1), (2, g2), (3, g3)):
            piece = ref[...].astype(f32)
            total = total + piece
            inside = inside + jnp.where(y >= k, piece, 0.0)
        planes_ref[...] = jnp.broadcast_to(total.astype(bf16)[None], planes_ref.shape)
        planes_ref[pl.ds(lax.axis_index("seq_0"), 1)] = inside.astype(bf16)[None]

    outs = [((8, half, LANES), bf16, pltpu.HBM)]
    return plain(body, outs, 1, half * 4096, chip, *got)[0]


def before_chip(later, planes):
    half = planes.shape[1]

    def body(planes_ref, send_ref):
        z = lax.axis_index("seq_0")
        total = jnp.zeros((half, LANES), f32)
        for k in range(8):
            take = (z <= k) if later else (z >= k)
            total = total + jnp.where(take, planes_ref[k].astype(f32), 0.0)
        send_ref[...] = total.astype(bf16)

    return plain(body, [((half, LANES), bf16)], 1, half * 4096, planes)[0]


def plane_exchange(planes):
    return lax.all_to_all(planes, "seq_0", 0, 0, tiled=True)


def swap(x):
    return lax.ppermute(x, "seq_2", SWAP)


def y_gather(later, chip):
    got = []
    for k in (2, 1, 3):
        got.append(lax.ppermute(chip, "seq_1", shifts(4, -k if later else k)))
    return got[1], got[0], got[2]


def key_value(latents, w_key, w_value):
    rows, width = (latents.shape[0], w_key.shape[1])
    steps = 4
    depth = latents.shape[1] // steps

    def body(x_hbm, wk_hbm, wv_hbm, fk_ref, v_ref, state_ref, x_ref, w_ref, sem):
        copies = []
        for i in range(steps):
            span = pl.ds(i * depth, depth)
            copies.append(
                [
                    pltpu.make_async_copy(src, dst, sem.at[3 * i + j])
                    for j, (src, dst) in enumerate(
                        (
                            (x_hbm.at[:, span], x_ref.at[:, span]),
                            (wk_hbm.at[span, :], w_ref.at[span, pl.ds(0, width)]),
                            (wv_hbm.at[span, :], w_ref.at[span, pl.ds(width, width)]),
                        )
                    )
                ]
            )
        for group in copies:
            for copy in group:
                copy.start()
        total = None
        for i, group in enumerate(copies):
            for copy in group:
                copy.wait()
            span = slice(i * depth, (i + 1) * depth)
            part = mm(x_ref[:, span], w_ref[span, :])
            total = part if total is None else total + part
        fk_ref[...] = feature_map(total[:, :width]).astype(bf16)
        v_ref[...] = total[:, width:].astype(bf16)
        for p in range(width // LANES):
            cols = slice(p * LANES, (p + 1) * LANES)
            state_ref[p * HD : (p + 1) * HD, :] = pack(
                mm(fk_ref[:, cols], v_ref[:, cols], TN)
            ).astype(bf16)

    hbm = pl.BlockSpec(memory_space=pltpu.HBM)
    return call(
        body,
        [
            ((rows, width), bf16),
            ((rows, width), bf16),
            ((width * HD // LANES, LANES), bf16),
        ],
        4 * rows * width * latents.shape[1],
        3 * 1024 * 1024,
        in_specs=[hbm] * 3,
        out_specs=[VMEM] * 3,
        scratch_shapes=[
            pltpu.VMEM(latents.shape, bf16),
            pltpu.VMEM((latents.shape[1], 2 * width), bf16),
            pltpu.SemaphoreType.DMA((3 * steps,)),
        ],
    )(in_hbm(latents), in_hbm(w_key), in_hbm(w_value))


def tri(rows, upper):
    t = lax.broadcasted_iota(jnp.int32, (rows, rows), 0)
    s = lax.broadcasted_iota(jnp.int32, (rows, rows), 1)
    return (t <= s) if upper else (t >= s)


def masked(scores, keep):
    return jnp.where(keep, scores, 0.0).astype(bf16)


def query_local(latents, w_query, fk, v):
    rows, width = fk.shape
    steps = 2
    depth = latents.shape[1] // steps

    def body(x_hbm, wq_ref, fk_ref, v_ref, fq_ref, raw_ref, x_ref, sem):
        spans = [pl.ds(i * depth, depth) for i in range(steps)]
        copies = [
            pltpu.make_async_copy(x_hbm.at[:, span], x_ref.at[:, span], sem.at[i])
            for i, span in enumerate(spans)
        ]
        for copy in copies:
            copy.start()
        total = jnp.zeros((rows, width), f32)
        for copy, span in zip(copies, spans):
            copy.wait()
            total = total + mm(x_ref[:, span], wq_ref[span, :])
        fq_ref[...] = feature_map(total).astype(bf16)
        keep = tri(rows, False)
        for p in range(width // LANES):
            cols = slice(p * LANES, (p + 1) * LANES)
            q, k, val = (fq_ref[:, cols], fk_ref[:, cols], v_ref[:, cols])
            total = None
            for h in (0, 1):
                score = masked(mm(q, one_head(k, h), NT), keep)
                part = mm(score, one_head(val, h))
                total = part if total is None else total + part
            raw_ref[:, cols] = total.astype(bf16)

    return call(
        body,
        [((rows, width), bf16)] * 2,
        2 * rows * width * (latents.shape[1] + 4 * rows),
        3 * 1024 * 1024,
        in_specs=[pl.BlockSpec(memory_space=pltpu.HBM)] + [VMEM] * 3,
        out_specs=[VMEM] * 2,
        scratch_shapes=[pltpu.VMEM(latents.shape, bf16), pltpu.SemaphoreType.DMA((steps,))],
    )(in_hbm(latents), w_query, fk, v)


def upstream_of(grads, w_out, gain):
    rows, width = grads[0].shape

    def body(g0, g1, g2, g3, w_hbm, gain_ref, up_ref, w_ref, sem):
        m = lax.axis_index("mp")
        copies = []
        for k in range(4):
            at = pl.multiple_of(lax.rem(m + 4 - k, 4) * width, LANES)
            copies.append(
                pltpu.make_async_copy(w_hbm.at[:, pl.ds(at, width)], w_ref.at[k], sem.at[k])
            )
        for copy in copies:
            copy.start()
        total = jnp.zeros((rows, width), f32)
        for k, ref in enumerate((g0, g1, g2, g3)):
            copies[k].wait()
            total = total + mm(ref[...], w_ref[k], NT)
        up_ref[...] = (total * gain_ref[...]).astype(bf16)

    return call(
        body,
        [((rows, width), bf16)],
        8 * rows * width * width,
        3 * 1024 * 1024,
        in_specs=[VMEM] * 4 + [pl.BlockSpec(memory_space=pltpu.HBM), VMEM],
        out_specs=[VMEM],
        scratch_shapes=[pltpu.VMEM((4, width, width), bf16), pltpu.SemaphoreType.DMA((4,))],
    )(*grads, in_hbm(w_out), gain)[0]


def normed(mine, got, pair, fq, raw_local, up, gain):
    rows, width = fq.shape
    half = mine.shape[0]

    def body(
        mine_ref,
        got_ref,
        pair_ref,
        fq_ref,
        raw_ref,
        up_ref,
        gain_ref,
        attn_ref,
        draw_ref,
        before_ref,
        after_ref,
        state,
    ):
        whole_state(False, mine_ref, got_ref, pair_ref, state)
        before_ref[...] = state[...].astype(bf16)
        ones = head_ones()
        for p in range(width // LANES):
            cols = slice(p * LANES, (p + 1) * LANES)
            q = fq_ref[:, cols]
            raw = raw_ref[:, cols].astype(f32) + mm(q, unpack(before_ref[p * HD : (p + 1) * HD, :]))
            upstream = up_ref[:, cols].astype(f32)
            square = mm((raw * raw).astype(bf16), ones) * (1.0 / HD)
            cross = mm((raw * upstream).astype(bf16), ones) * (1.0 / HD)
            inv = lax.rsqrt(square + epsilon)
            unit = raw * inv
            attn_ref[:, cols] = (unit * gain_ref[:, cols]).astype(bf16)
            draw = (inv * upstream - inv * inv * unit * cross).astype(bf16)
            draw_ref[:, cols] = draw
            after_ref[p * HD : (p + 1) * HD, :] = pack(mm(q, draw, TN)).astype(bf16)

    return call(
        body,
        [
            ((rows, width), bf16),
            ((rows, width), bf16),
            ((2 * half, LANES), bf16),
            ((2 * half, LANES), bf16),
        ],
        8 * rows * width * LANES,
        2 * 1024 * 1024,
        in_specs=[VMEM] * 7,
        out_specs=[VMEM] * 4,
        scratch_shapes=[pltpu.VMEM((2 * half, LANES), f32)],
    )(mine, got, pair, fq, raw_local, up, gain)


def branch_parts(attn, w_out):
    rows, width = attn.shape

    def body(attn_ref, w_ref, *outs):
        for k, ref in zip((2, 1, 3, 0), outs):
            ref[...] = mm(attn_ref[...], w_ref[:, block_rows(k, width)]).astype(bf16)

    return plain(
        body,
        [((rows, width), bf16, pltpu.HBM)] * 4,
        8 * rows * width * width,
        2 * 1024 * 1024,
        attn,
        w_out,
    )


def local_grads(fq, fk, v, draw, before):
    rows, width = fq.shape

    def body(fq_ref, fk_ref, v_ref, draw_ref, before_ref, dq_ref, dk_ref, dv_ref):
        lower, upper = (tri(rows, False), tri(rows, True))
        for p in range(width // LANES):
            cols = slice(p * LANES, (p + 1) * LANES)
            q, k, val, dr = (fq_ref[:, cols], fk_ref[:, cols], v_ref[:, cols], draw_ref[:, cols])
            dq = mm(dr, unpack(before_ref[p * HD : (p + 1) * HD, :]), NT)
            dk, dv = (None, None)
            for h in (0, 1):
                val_h, k_h, q_h, dr_h = (one_head(a, h) for a in (val, k, q, dr))
                dq = dq + mm(masked(mm(dr, val_h, NT), lower), k_h)
                dk_h = mm(masked(mm(val_h, dr, NT), upper), q_h)
                dv_h = mm(masked(mm(k_h, q, NT), upper), dr_h)
                dk = dk_h if dk is None else dk + dk_h
                dv = dv_h if dv is None else dv + dv_h
            dq_ref[:, cols] = (dq * jnp.minimum(q.astype(f32), 1.0)).astype(bf16)
            dk_ref[:, cols] = dk.astype(bf16)
            dv_ref[:, cols] = dv.astype(bf16)

    return plain(
        body,
        [((rows, width), bf16)] * 3,
        24 * rows * rows * width,
        3 * 1024 * 1024,
        fq,
        fk,
        v,
        draw,
        before,
    )


def block_rows(k, width):
    at = lax.rem(lax.axis_index("mp") + k, 4) * width
    return pl.ds(pl.multiple_of(at, LANES), width)


def block_copies(k, sources, targets, sem, first):
    width = sources[0].shape[1]
    return [
        pltpu.make_async_copy(src.at[block_rows(k, width), :], dst, sem.at[first + i])
        for i, (src, dst) in enumerate(zip(sources, targets))
    ]


def weight_blocks(k, weights):
    width, count = (weights[0].shape[1], len(weights))

    def body(*refs):
        copies = block_copies(k, refs[:count], refs[count : 2 * count], refs[2 * count], 0)
        for copy in copies:
            copy.start()
        for copy in copies:
            copy.wait()

    return call(
        body,
        [((width, width), bf16)] * count,
        1,
        1024 * 1024,
        in_specs=[pl.BlockSpec(memory_space=pltpu.HBM)] * count,
        out_specs=[VMEM] * count,
        scratch_shapes=[pltpu.SemaphoreType.DMA((count,))],
    )(*(in_hbm(w) for w in weights))


def first_part(mine, got, pair, fk, v, dq, dk, dv, blocks):
    rows, width = fk.shape
    half = mine.shape[0]

    def body(
        mine_ref,
        got_ref,
        pair_ref,
        fk_ref,
        v_ref,
        dq_ref,
        dkl_ref,
        dvl_ref,
        wq_ref,
        wk_ref,
        wv_ref,
        dk_ref,
        dv_ref,
        part_ref,
        state,
    ):
        whole_state(True, mine_ref, got_ref, pair_ref, state)
        for p in range(width // LANES):
            cols = slice(p * LANES, (p + 1) * LANES)
            after = unpack(state[p * HD : (p + 1) * HD, :].astype(bf16))
            k = fk_ref[:, cols]
            dk = dkl_ref[:, cols].astype(f32) + mm(v_ref[:, cols], after, NT)
            dk_ref[:, cols] = (dk * jnp.minimum(k.astype(f32), 1.0)).astype(bf16)
            dv_ref[:, cols] = (dvl_ref[:, cols].astype(f32) + mm(k, after)).astype(bf16)
        total = mm(dq_ref[...], wq_ref[...], NT)
        total = total + mm(dk_ref[...], wk_ref[...], NT)
        part_ref[...] = (total + mm(dv_ref[...], wv_ref[...], NT)).astype(bf16)

    return call(
        body,
        [((rows, width), bf16)] * 3,
        6 * rows * width * width,
        2 * 1024 * 1024,
        in_specs=[VMEM] * 11,
        out_specs=[VMEM] * 3,
        scratch_shapes=[pltpu.VMEM((2 * half, LANES), f32)],
    )(mine, got, pair, fk, v, dq, dk, dv, *blocks)


def other_parts(which, dq, dk, dv, weights):
    rows, width = dq.shape
    count = len(which)

    def body(dq_ref, dk_ref, dv_ref, wq_hbm, wk_hbm, wv_hbm, *refs):
        outs, blocks, sem = (refs[:count], refs[count], refs[count + 1])
        copies = [
            block_copies(
                k, (wq_hbm, wk_hbm, wv_hbm), [blocks.at[3 * i + j] for j in range(3)], sem, 3 * i
            )
            for i, k in enumerate(which)
        ]
        for group in copies:
            for copy in group:
                copy.start()
        for i, (group, ref) in enumerate(zip(copies, outs)):
            for copy in group:
                copy.wait()
            total = None
            for j, grad_ref in enumerate((dq_ref, dk_ref, dv_ref)):
                part = mm(grad_ref[...], blocks[3 * i + j], NT)
                total = part if total is None else total + part
            ref[...] = total.astype(bf16)

    hbm = pl.BlockSpec(memory_space=pltpu.HBM)
    return call(
        body,
        [((rows, width), bf16)] * count,
        6 * rows * width * width * count,
        1024 * 1024 * count,
        in_specs=[VMEM] * 3 + [hbm] * 3,
        out_specs=[VMEM] * count,
        scratch_shapes=[
            pltpu.VMEM((3 * count, width, width), bf16),
            pltpu.SemaphoreType.DMA((3 * count,)),
        ],
    )(dq, dk, dv, *(in_hbm(w) for w in weights))


def add_up(parts):
    total = parts[0].astype(f32)
    for part in parts[1:]:
        total = total + part.astype(f32)
    return total.astype(bf16)


def to_owner(part, k):
    return lax.ppermute(part, "mp", shifts(4, k))


def hold(x, anchor):
    return lax.optimization_barrier((x, anchor))[0]


def per_device(latents, w_query, w_key, w_value, w_out, head_gain, grad_out):
    gain = head_gain.reshape(1, -1)
    grads = [grad_out] + [to_owner(grad_out, k) for k in (1, 2, 3)]
    fk, v, state = key_value(latents, w_key, w_value)
    pair = swap(state)
    chip = pair_sum(state, pair)
    got = y_gather(False, chip)
    planes = plane_sums(False, chip, got)
    fq, raw_local = query_local(hold(latents, planes), w_query, fk, v)
    up = upstream_of(grads, w_out, gain)
    planes = plane_exchange(planes)
    mine = before_chip(False, planes)
    got = swap(mine)
    blocks = weight_blocks(2, (hold(w_query, mine), w_key))
    attn, draw, before, state = normed(mine, got, pair, fq, raw_local, up, gain)
    weights = (w_query, w_key, w_value)
    blocks = blocks + weight_blocks(2, (hold(w_value, state),))
    pair = swap(state)
    chip = pair_sum(state, pair)
    got = y_gather(True, chip)
    b2, b1, b3, b0 = branch_parts(hold(attn, chip), w_out)
    planes = plane_sums(True, chip, got)
    b2, b1, b3 = (hold(b, planes) for b in (b2, b1, b3))
    branch = [b0, to_owner(b2, 2), to_owner(b1, 1), to_owner(b3, 3)]
    dq, dk_local, dv_local = local_grads(fq, fk, v, hold(draw, planes), before)
    planes = plane_exchange(planes)
    mine = before_chip(True, planes)
    got = swap(mine)
    dk, dv, l2 = first_part(mine, got, pair, fk, v, dq, dk_local, dv_local, blocks)
    l2 = to_owner(l2, 2)
    l1, l3 = other_parts((1, 3), dq, dk, dv, weights)
    l1, l3 = (to_owner(l1, 1), to_owner(l3, 3))
    (l0,) = other_parts((0,), dq, dk, dv, weights)
    return (add_up(branch), add_up([l0, l2, l1, l3]))


def solution(mesh):
    split = Mesh(mesh.devices.reshape(8, 4, 2, mesh.shape["mp"]), (*SEQ, "mp"))
    in_specs = (
        P(SEQ, None),
        P(None, "mp"),
        P(None, "mp"),
        P(None, "mp"),
        P("mp", None),
        P("mp"),
        P(SEQ, "mp"),
    )
    out_specs = (P(SEQ, "mp"), P(SEQ, "mp"))
    return jax.shard_map(
        per_device, mesh=split, in_specs=in_specs, out_specs=out_specs, check_vma=False
    )
```

```python
import jax
import jax.numpy as jnp
from jax import lax
from jax.experimental import pallas as pl
from jax.experimental.pallas import tpu as pltpu
from jax.sharding import Mesh
from jax.sharding import PartitionSpec as P


HD = 64
LANES = 128
SEQ = ("seq_0", "seq_1", "seq_2")
SWAP = [(0, 1), (1, 0)]
epsilon = 1e-06
f32, bf16 = (jnp.float32, jnp.bfloat16)
NT = (((1,), (1,)), ((), ()))
TN = (((0,), (0,)), ((), ()))
VMEM = pl.BlockSpec(memory_space=pltpu.VMEM)


def shifts(count, step):
    return [(i, (i + step) % count) for i in range(count)]


def mm(a, b, contract=(((1,), (0,)), ((), ()))):
    return lax.dot_general(a, b, contract, preferred_element_type=f32)


def in_hbm(x):
    return pltpu.with_memory_space_constraint(x, pltpu.HBM)


def shape_of(shape, kind, where=pltpu.VMEM):
    return where(shape, kind)


def call(body, outs, flops, moved, **extra):
    return pl.pallas_call(
        body,
        out_shape=[shape_of(*out) for out in outs],
        cost_estimate=pl.CostEstimate(flops=flops, bytes_accessed=moved, transcendentals=0),
        compiler_params=pltpu.CompilerParams(vmem_limit_bytes=20 * 1024 * 1024),
        **extra,
    )


def plain(body, outs, flops, moved, *args):
    return call(
        body, outs, flops, moved, in_specs=[VMEM] * len(args), out_specs=[VMEM] * len(outs)
    )(*args)


def feature_map(u):
    return jnp.where(u > 0, u + 1.0, jnp.exp(jnp.minimum(u, 0.0)))


def low_lanes(shape):
    return lax.broadcasted_iota(jnp.int32, shape, len(shape) - 1) < HD


def one_head(x, head):
    low = low_lanes(x.shape)
    keep = low if head == 0 else jnp.logical_not(low)
    return jnp.where(keep, x, jnp.zeros_like(x))


def pack(full):
    return jnp.where(low_lanes((HD, LANES)), full[:HD], full[HD:])


def unpack(rows):
    low = low_lanes((HD, LANES))
    zero = jnp.zeros_like(rows)
    return jnp.concatenate([jnp.where(low, rows, zero), jnp.where(low, zero, rows)], axis=0)


def head_ones():
    r = lax.broadcasted_iota(jnp.int32, (LANES, LANES), 0) < HD
    c = lax.broadcasted_iota(jnp.int32, (LANES, LANES), 1) < HD
    return jnp.where(r == c, 1.0, 0.0).astype(bf16)


def half_at(other, half):
    side = lax.axis_index("seq_2")
    side = 1 - side if other else side
    return pl.ds(pl.multiple_of(side * half, 16), half)


def whole_state(later, mine_ref, got_ref, pair_ref, state_ref):
    half = mine_ref.shape[0]
    last = lax.axis_index("seq_2") == (0 if later else 1)
    state_ref[half_at(False, half), :] = mine_ref[...].astype(f32)
    state_ref[half_at(True, half), :] = got_ref[...].astype(f32)
    state_ref[...] += jnp.where(last, pair_ref[...].astype(f32), 0.0)


def pair_sum(state, pair):
    half = state.shape[0] // 2

    def body(state_ref, pair_ref, chip_ref):
        own = half_at(False, half)
        chip_ref[...] = (state_ref[own, :].astype(f32) + pair_ref[own, :].astype(f32)).astype(bf16)

    return plain(body, [((half, LANES), bf16)], 1, half * 1024, state, pair)[0]


def plane_sums(later, chip, got):
    half = chip.shape[0]

    def body(chip_ref, g1, g2, g3, planes_ref):
        y = lax.axis_index("seq_1")
        y = 3 - y if later else y
        total = chip_ref[...].astype(f32)
        inside = jnp.zeros_like(total)
        for k, ref in ((1, g1), (2, g2), (3, g3)):
            piece = ref[...].astype(f32)
            total = total + piece
            inside = inside + jnp.where(y >= k, piece, 0.0)
        planes_ref[...] = jnp.broadcast_to(total.astype(bf16)[None], planes_ref.shape)
        planes_ref[pl.ds(lax.axis_index("seq_0"), 1)] = inside.astype(bf16)[None]

    outs = [((8, half, LANES), bf16, pltpu.HBM)]
    return plain(body, outs, 1, half * 4096, chip, *got)[0]


def before_chip(later, planes):
    half = planes.shape[1]

    def body(planes_ref, send_ref):
        z = lax.axis_index("seq_0")
        total = jnp.zeros((half, LANES), f32)
        for k in range(8):
            take = (z <= k) if later else (z >= k)
            total = total + jnp.where(take, planes_ref[k].astype(f32), 0.0)
        send_ref[...] = total.astype(bf16)

    return plain(body, [((half, LANES), bf16)], 1, half * 4096, planes)[0]


def plane_exchange(planes):
    return lax.all_to_all(planes, "seq_0", 0, 0, tiled=True)


def swap(x):
    return lax.ppermute(x, "seq_2", SWAP)


def y_gather(later, chip):
    got = []
    for k in (2, 1, 3):
        got.append(lax.ppermute(chip, "seq_1", shifts(4, -k if later else k)))
    return got[1], got[0], got[2]


def key_value(latents, w_key, w_value):
    rows, width = (latents.shape[0], w_key.shape[1])
    steps = 4
    depth = latents.shape[1] // steps

    def body(x_hbm, wk_hbm, wv_hbm, fk_ref, v_ref, state_ref, x_ref, w_ref, sem):
        copies = []
        for i in range(steps):
            span = pl.ds(i * depth, depth)
            copies.append(
                [
                    pltpu.make_async_copy(src, dst, sem.at[3 * i + j])
                    for j, (src, dst) in enumerate(
                        (
                            (x_hbm.at[:, span], x_ref.at[:, span]),
                            (wk_hbm.at[span, :], w_ref.at[span, pl.ds(0, width)]),
                            (wv_hbm.at[span, :], w_ref.at[span, pl.ds(width, width)]),
                        )
                    )
                ]
            )
        for group in copies:
            for copy in group:
                copy.start()
        total = None
        for i, group in enumerate(copies):
            for copy in group:
                copy.wait()
            span = slice(i * depth, (i + 1) * depth)
            part = mm(x_ref[:, span], w_ref[span, :])
            total = part if total is None else total + part
        fk_ref[...] = feature_map(total[:, :width]).astype(bf16)
        v_ref[...] = total[:, width:].astype(bf16)
        for p in range(width // LANES):
            cols = slice(p * LANES, (p + 1) * LANES)
            state_ref[p * HD : (p + 1) * HD, :] = pack(
                mm(fk_ref[:, cols], v_ref[:, cols], TN)
            ).astype(bf16)

    hbm = pl.BlockSpec(memory_space=pltpu.HBM)
    return call(
        body,
        [
            ((rows, width), bf16),
            ((rows, width), bf16),
            ((width * HD // LANES, LANES), bf16),
        ],
        4 * rows * width * latents.shape[1],
        3 * 1024 * 1024,
        in_specs=[hbm] * 3,
        out_specs=[VMEM] * 3,
        scratch_shapes=[
            pltpu.VMEM(latents.shape, bf16),
            pltpu.VMEM((latents.shape[1], 2 * width), bf16),
            pltpu.SemaphoreType.DMA((3 * steps,)),
        ],
    )(in_hbm(latents), in_hbm(w_key), in_hbm(w_value))


def tri(rows, upper):
    t = lax.broadcasted_iota(jnp.int32, (rows, rows), 0)
    s = lax.broadcasted_iota(jnp.int32, (rows, rows), 1)
    return (t <= s) if upper else (t >= s)


def masked(scores, keep):
    return jnp.where(keep, scores, 0.0).astype(bf16)


def query_local(latents, w_query, fk, v):
    rows, width = fk.shape
    steps = 2
    depth = latents.shape[1] // steps

    def body(x_hbm, wq_ref, fk_ref, v_ref, fq_ref, raw_ref, x_ref, sem):
        spans = [pl.ds(i * depth, depth) for i in range(steps)]
        copies = [
            pltpu.make_async_copy(x_hbm.at[:, span], x_ref.at[:, span], sem.at[i])
            for i, span in enumerate(spans)
        ]
        for copy in copies:
            copy.start()
        total = jnp.zeros((rows, width), f32)
        for copy, span in zip(copies, spans):
            copy.wait()
            total = total + mm(x_ref[:, span], wq_ref[span, :])
        fq_ref[...] = feature_map(total).astype(bf16)
        keep = tri(rows, False)
        for p in range(width // LANES):
            cols = slice(p * LANES, (p + 1) * LANES)
            q, k, val = (fq_ref[:, cols], fk_ref[:, cols], v_ref[:, cols])
            total = None
            for h in (0, 1):
                score = masked(mm(q, one_head(k, h), NT), keep)
                part = mm(score, one_head(val, h))
                total = part if total is None else total + part
            raw_ref[:, cols] = total.astype(bf16)

    return call(
        body,
        [((rows, width), bf16)] * 2,
        2 * rows * width * (latents.shape[1] + 4 * rows),
        3 * 1024 * 1024,
        in_specs=[pl.BlockSpec(memory_space=pltpu.HBM)] + [VMEM] * 3,
        out_specs=[VMEM] * 2,
        scratch_shapes=[pltpu.VMEM(latents.shape, bf16), pltpu.SemaphoreType.DMA((steps,))],
    )(in_hbm(latents), w_query, fk, v)


def upstream_of(grads, w_out, gain):
    rows, width = grads[0].shape

    def body(g0, g1, g2, g3, w_hbm, gain_ref, up_ref, w_ref, sem):
        m = lax.axis_index("mp")
        copies = []
        for k in range(4):
            at = pl.multiple_of(lax.rem(m + 4 - k, 4) * width, LANES)
            copies.append(
                pltpu.make_async_copy(w_hbm.at[:, pl.ds(at, width)], w_ref.at[k], sem.at[k])
            )
        for copy in copies:
            copy.start()
        total = jnp.zeros((rows, width), f32)
        for k, ref in enumerate((g0, g1, g2, g3)):
            copies[k].wait()
            total = total + mm(ref[...], w_ref[k], NT)
        up_ref[...] = (total * gain_ref[...]).astype(bf16)

    return call(
        body,
        [((rows, width), bf16)],
        8 * rows * width * width,
        3 * 1024 * 1024,
        in_specs=[VMEM] * 4 + [pl.BlockSpec(memory_space=pltpu.HBM), VMEM],
        out_specs=[VMEM],
        scratch_shapes=[pltpu.VMEM((4, width, width), bf16), pltpu.SemaphoreType.DMA((4,))],
    )(*grads, in_hbm(w_out), gain)[0]


def normed(mine, got, pair, fq, raw_local, up, gain):
    rows, width = fq.shape
    half = mine.shape[0]

    def body(
        mine_ref,
        got_ref,
        pair_ref,
        fq_ref,
        raw_ref,
        up_ref,
        gain_ref,
        attn_ref,
        draw_ref,
        before_ref,
        after_ref,
        state,
    ):
        whole_state(False, mine_ref, got_ref, pair_ref, state)
        before_ref[...] = state[...].astype(bf16)
        ones = head_ones()
        for p in range(width // LANES):
            cols = slice(p * LANES, (p + 1) * LANES)
            q = fq_ref[:, cols]
            raw = raw_ref[:, cols].astype(f32) + mm(q, unpack(before_ref[p * HD : (p + 1) * HD, :]))
            upstream = up_ref[:, cols].astype(f32)
            square = mm((raw * raw).astype(bf16), ones) * (1.0 / HD)
            cross = mm((raw * upstream).astype(bf16), ones) * (1.0 / HD)
            inv = lax.rsqrt(square + epsilon)
            unit = raw * inv
            attn_ref[:, cols] = (unit * gain_ref[:, cols]).astype(bf16)
            draw = (inv * upstream - inv * inv * unit * cross).astype(bf16)
            draw_ref[:, cols] = draw
            after_ref[p * HD : (p + 1) * HD, :] = pack(mm(q, draw, TN)).astype(bf16)

    return call(
        body,
        [
            ((rows, width), bf16),
            ((rows, width), bf16),
            ((2 * half, LANES), bf16),
            ((2 * half, LANES), bf16),
        ],
        8 * rows * width * LANES,
        2 * 1024 * 1024,
        in_specs=[VMEM] * 7,
        out_specs=[VMEM] * 4,
        scratch_shapes=[pltpu.VMEM((2 * half, LANES), f32)],
    )(mine, got, pair, fq, raw_local, up, gain)


def branch_parts(attn, w_out):
    rows, width = attn.shape

    def body(attn_ref, w_ref, *outs):
        for k, ref in zip((2, 1, 3, 0), outs):
            ref[...] = mm(attn_ref[...], w_ref[:, block_rows(k, width)]).astype(bf16)

    return plain(
        body,
        [((rows, width), bf16, pltpu.HBM)] * 4,
        8 * rows * width * width,
        2 * 1024 * 1024,
        attn,
        w_out,
    )


def local_grads(fq, fk, v, draw, before):
    rows, width = fq.shape

    def body(fq_ref, fk_ref, v_ref, draw_ref, before_ref, dq_ref, dk_ref, dv_ref):
        lower, upper = (tri(rows, False), tri(rows, True))
        for p in range(width // LANES):
            cols = slice(p * LANES, (p + 1) * LANES)
            q, k, val, dr = (fq_ref[:, cols], fk_ref[:, cols], v_ref[:, cols], draw_ref[:, cols])
            dq = mm(dr, unpack(before_ref[p * HD : (p + 1) * HD, :]), NT)
            dk, dv = (None, None)
            for h in (0, 1):
                val_h, k_h, q_h, dr_h = (one_head(a, h) for a in (val, k, q, dr))
                dq = dq + mm(masked(mm(dr, val_h, NT), lower), k_h)
                dk_h = mm(masked(mm(val_h, dr, NT), upper), q_h)
                dv_h = mm(masked(mm(k_h, q, NT), upper), dr_h)
                dk = dk_h if dk is None else dk + dk_h
                dv = dv_h if dv is None else dv + dv_h
            dq_ref[:, cols] = (dq * jnp.minimum(q.astype(f32), 1.0)).astype(bf16)
            dk_ref[:, cols] = dk.astype(bf16)
            dv_ref[:, cols] = dv.astype(bf16)

    return plain(
        body,
        [((rows, width), bf16)] * 3,
        24 * rows * rows * width,
        3 * 1024 * 1024,
        fq,
        fk,
        v,
        draw,
        before,
    )


def block_rows(k, width):
    at = lax.rem(lax.axis_index("mp") + k, 4) * width
    return pl.ds(pl.multiple_of(at, LANES), width)


def block_copies(k, sources, targets, sem, first):
    width = sources[0].shape[1]
    return [
        pltpu.make_async_copy(src.at[block_rows(k, width), :], dst, sem.at[first + i])
        for i, (src, dst) in enumerate(zip(sources, targets))
    ]


def weight_blocks(which, weights):
    width, count = (weights[0].shape[1], len(weights))
    total = count * len(which)

    def body(*refs):
        sources, targets, sem = (refs[:count], refs[count : count + total], refs[count + total])
        copies = []
        for i, k in enumerate(which):
            at = i * count
            copies += block_copies(k, sources, targets[at : at + count], sem, at)
        for copy in copies:
            copy.start()
        for copy in copies:
            copy.wait()

    return call(
        body,
        [((width, width), bf16)] * total,
        1,
        1024 * 1024,
        in_specs=[pl.BlockSpec(memory_space=pltpu.HBM)] * count,
        out_specs=[VMEM] * total,
        scratch_shapes=[pltpu.SemaphoreType.DMA((total,))],
    )(*(in_hbm(w) for w in weights))


def first_part(mine, got, pair, fk, v, dq, dk, dv, blocks):
    rows, width = fk.shape
    half = mine.shape[0]

    def body(
        mine_ref,
        got_ref,
        pair_ref,
        fk_ref,
        v_ref,
        dq_ref,
        dkl_ref,
        dvl_ref,
        wq_ref,
        wk_ref,
        wv_ref,
        dk_ref,
        dv_ref,
        part_ref,
        state,
    ):
        whole_state(True, mine_ref, got_ref, pair_ref, state)
        for p in range(width // LANES):
            cols = slice(p * LANES, (p + 1) * LANES)
            after = unpack(state[p * HD : (p + 1) * HD, :].astype(bf16))
            k = fk_ref[:, cols]
            dk = dkl_ref[:, cols].astype(f32) + mm(v_ref[:, cols], after, NT)
            dk_ref[:, cols] = (dk * jnp.minimum(k.astype(f32), 1.0)).astype(bf16)
            dv_ref[:, cols] = (dvl_ref[:, cols].astype(f32) + mm(k, after)).astype(bf16)
        total = mm(dq_ref[...], wq_ref[...], NT)
        total = total + mm(dk_ref[...], wk_ref[...], NT)
        part_ref[...] = (total + mm(dv_ref[...], wv_ref[...], NT)).astype(bf16)

    return call(
        body,
        [((rows, width), bf16)] * 3,
        6 * rows * width * width,
        2 * 1024 * 1024,
        in_specs=[VMEM] * 11,
        out_specs=[VMEM] * 3,
        scratch_shapes=[pltpu.VMEM((2 * half, LANES), f32)],
    )(mine, got, pair, fk, v, dq, dk, dv, *blocks)


def other_parts(dq, dk, dv, *blocks):
    rows, width = dq.shape

    def body(dq_ref, dk_ref, dv_ref, *refs):
        for i, out_ref in enumerate(refs[len(blocks) :]):
            total = None
            for j, grad_ref in enumerate((dq_ref, dk_ref, dv_ref)):
                part = mm(grad_ref[...], refs[3 * i + j][...], NT)
                total = part if total is None else total + part
            out_ref[...] = total.astype(bf16)

    count = len(blocks) // 3
    return plain(
        body,
        [((rows, width), bf16)] * count,
        6 * rows * width * width * count,
        1024 * 1024 * count,
        dq,
        dk,
        dv,
        *blocks,
    )


def own_part(dq, dk, dv, weights):
    rows, width = dq.shape

    def body(dq_ref, dk_ref, dv_ref, wq_hbm, wk_hbm, wv_hbm, out_ref, blocks, sem):
        copies = block_copies(0, (wq_hbm, wk_hbm, wv_hbm), [blocks.at[j] for j in range(3)], sem, 0)
        for copy in copies:
            copy.start()
        total = jnp.zeros((rows, width), f32)
        for j, grad_ref in enumerate((dq_ref, dk_ref, dv_ref)):
            copies[j].wait()
            total = total + mm(grad_ref[...], blocks[j], NT)
        out_ref[...] = total.astype(bf16)

    hbm = pl.BlockSpec(memory_space=pltpu.HBM)
    return call(
        body,
        [((rows, width), bf16)],
        6 * rows * width * width,
        1024 * 1024,
        in_specs=[VMEM] * 3 + [hbm] * 3,
        out_specs=[VMEM],
        scratch_shapes=[
            pltpu.VMEM((3, width, width), bf16),
            pltpu.SemaphoreType.DMA((3,)),
        ],
    )(dq, dk, dv, *(in_hbm(w) for w in weights))[0]


def add_up(parts):
    total = parts[0].astype(f32)
    for part in parts[1:]:
        total = total + part.astype(f32)
    return total.astype(bf16)


def to_owner(part, k):
    return lax.ppermute(part, "mp", shifts(4, k))


def hold(x, anchor):
    return lax.optimization_barrier((x, anchor))[0]


def per_device(latents, w_query, w_key, w_value, w_out, head_gain, grad_out):
    gain = head_gain.reshape(1, -1)
    fk, v, state = key_value(latents, w_key, w_value)
    pair = swap(state)
    grad1 = to_owner(hold(grad_out, state), 1)
    chip = pair_sum(state, pair)
    got = y_gather(False, chip)
    grad_held = hold(grad_out, chip)
    grads = [grad_out, grad1] + [to_owner(grad_held, k) for k in (2, 3)]
    planes = plane_sums(False, chip, got)
    fq, raw_local = query_local(hold(latents, planes), w_query, fk, v)
    up = upstream_of(grads, w_out, gain)
    planes = plane_exchange(planes)
    mine = before_chip(False, planes)
    got = swap(mine)
    blocks = weight_blocks((2,), (hold(w_query, mine), w_key))
    attn, draw, before, state = normed(mine, got, pair, fq, raw_local, up, gain)
    weights = (w_query, w_key, w_value)
    blocks = blocks + weight_blocks((2,), (hold(w_value, state),))
    pair = swap(state)
    chip = pair_sum(state, pair)
    got = y_gather(True, chip)
    b2, b1, b3, b0 = branch_parts(hold(attn, chip), w_out)
    planes = plane_sums(True, chip, got)
    b2, b1, b3 = (hold(b, planes) for b in (b2, b1, b3))
    branch = [b0, to_owner(b2, 2), to_owner(b1, 1), to_owner(b3, 3)]
    dq, dk_local, dv_local = local_grads(fq, fk, v, hold(draw, planes), before)
    planes = plane_exchange(planes)
    mine = before_chip(True, planes)
    got = swap(mine)
    others = weight_blocks((1, 3), (hold(w_query, mine), w_key, w_value))
    dk, dv, l2 = first_part(mine, got, pair, fk, v, dq, dk_local, dv_local, blocks)
    l2 = to_owner(l2, 2)
    l1, l3 = other_parts(dq, dk, dv, *others)
    l1, l3 = (to_owner(l1, 1), to_owner(l3, 3))
    l0 = own_part(dq, dk, dv, weights)
    return (add_up(branch), add_up([l0, l2, l1, l3]))


def solution(mesh):
    split = Mesh(mesh.devices.reshape(8, 4, 2, mesh.shape["mp"]), (*SEQ, "mp"))
    in_specs = (
        P(SEQ, None),
        P(None, "mp"),
        P(None, "mp"),
        P(None, "mp"),
        P("mp", None),
        P("mp"),
        P(SEQ, "mp"),
    )
    out_specs = (P(SEQ, "mp"), P(SEQ, "mp"))
    return jax.shard_map(
        per_device, mesh=split, in_specs=in_specs, out_specs=out_specs, check_vma=False
    )
```

```python
import jax
import jax.numpy as jnp
from jax import lax
from jax.experimental import pallas as pl
from jax.experimental.pallas import tpu as pltpu
from jax.sharding import Mesh
from jax.sharding import PartitionSpec as P


HD = 64
LANES = 128
SEQ = ("seq_0", "seq_1", "seq_2")
SWAP = [(0, 1), (1, 0)]
epsilon = 1e-06
f32, bf16 = (jnp.float32, jnp.bfloat16)
NT = (((1,), (1,)), ((), ()))
TN = (((0,), (0,)), ((), ()))
VMEM = pl.BlockSpec(memory_space=pltpu.VMEM)


def shifts(count, step):
    return [(i, (i + step) % count) for i in range(count)]


def mm(a, b, contract=(((1,), (0,)), ((), ()))):
    return lax.dot_general(a, b, contract, preferred_element_type=f32)


def in_hbm(x):
    return pltpu.with_memory_space_constraint(x, pltpu.HBM)


def shape_of(shape, kind, where=pltpu.VMEM):
    return where(shape, kind)


def call(body, outs, flops, moved, **extra):
    return pl.pallas_call(
        body,
        out_shape=[shape_of(*out) for out in outs],
        cost_estimate=pl.CostEstimate(flops=flops, bytes_accessed=moved, transcendentals=0),
        compiler_params=pltpu.CompilerParams(vmem_limit_bytes=20 * 1024 * 1024),
        **extra,
    )


def plain(body, outs, flops, moved, *args):
    return call(
        body, outs, flops, moved, in_specs=[VMEM] * len(args), out_specs=[VMEM] * len(outs)
    )(*args)


def feature_map(u):
    return jnp.where(u > 0, u + 1.0, jnp.exp(jnp.minimum(u, 0.0)))


def low_lanes(shape):
    return lax.broadcasted_iota(jnp.int32, shape, len(shape) - 1) < HD


def one_head(x, head):
    low = low_lanes(x.shape)
    keep = low if head == 0 else jnp.logical_not(low)
    return jnp.where(keep, x, jnp.zeros_like(x))


def pack(full):
    return jnp.where(low_lanes((HD, LANES)), full[:HD], full[HD:])


def unpack(rows):
    low = low_lanes((HD, LANES))
    zero = jnp.zeros_like(rows)
    return jnp.concatenate([jnp.where(low, rows, zero), jnp.where(low, zero, rows)], axis=0)


def head_ones():
    r = lax.broadcasted_iota(jnp.int32, (LANES, LANES), 0) < HD
    c = lax.broadcasted_iota(jnp.int32, (LANES, LANES), 1) < HD
    return jnp.where(r == c, 1.0, 0.0).astype(bf16)


def half_at(other, half):
    side = lax.axis_index("seq_2")
    side = 1 - side if other else side
    return pl.ds(pl.multiple_of(side * half, 16), half)


def whole_state(later, mine_ref, got_ref, pair_ref, state_ref):
    half = mine_ref.shape[0]
    last = lax.axis_index("seq_2") == (0 if later else 1)
    state_ref[half_at(False, half), :] = mine_ref[...].astype(f32)
    state_ref[half_at(True, half), :] = got_ref[...].astype(f32)
    state_ref[...] += jnp.where(last, pair_ref[...].astype(f32), 0.0)


def pair_sum(state, pair):
    half = state.shape[0] // 2

    def body(state_ref, pair_ref, chip_ref):
        own = half_at(False, half)
        chip_ref[...] = (state_ref[own, :].astype(f32) + pair_ref[own, :].astype(f32)).astype(bf16)

    return plain(body, [((half, LANES), bf16)], 1, half * 1024, state, pair)[0]


def plane_sums(later, chip, got):
    half = chip.shape[0]

    def body(chip_ref, g1, g2, g3, planes_ref):
        y = lax.axis_index("seq_1")
        y = 3 - y if later else y
        total = chip_ref[...].astype(f32)
        inside = jnp.zeros_like(total)
        for k, ref in ((1, g1), (2, g2), (3, g3)):
            piece = ref[...].astype(f32)
            total = total + piece
            inside = inside + jnp.where(y >= k, piece, 0.0)
        planes_ref[...] = jnp.broadcast_to(total.astype(bf16)[None], planes_ref.shape)
        planes_ref[pl.ds(lax.axis_index("seq_0"), 1)] = inside.astype(bf16)[None]

    outs = [((8, half, LANES), bf16, pltpu.HBM)]
    return plain(body, outs, 1, half * 4096, chip, *got)[0]


def before_chip(later, planes):
    half = planes.shape[1]

    def body(planes_ref, send_ref):
        z = lax.axis_index("seq_0")
        total = jnp.zeros((half, LANES), f32)
        for k in range(8):
            take = (z <= k) if later else (z >= k)
            total = total + jnp.where(take, planes_ref[k].astype(f32), 0.0)
        send_ref[...] = total.astype(bf16)

    return plain(body, [((half, LANES), bf16)], 1, half * 4096, planes)[0]


def plane_exchange(planes):
    return lax.all_to_all(planes, "seq_0", 0, 0, tiled=True)


def swap(x):
    return lax.ppermute(x, "seq_2", SWAP)


def y_gather(later, chip):
    got = []
    for k in (2, 1, 3):
        got.append(lax.ppermute(chip, "seq_1", shifts(4, -k if later else k)))
    return got[1], got[0], got[2]


def key_value(latents, w_key, w_value):
    rows, width = (latents.shape[0], w_key.shape[1])
    depths = [latents.shape[1] // 12 * part for part in (4, 4, 3, 1)]
    steps = len(depths)

    def body(x_hbm, wk_hbm, wv_hbm, fk_ref, v_ref, state_ref, x_ref, w_ref, sem):
        copies = []
        for i in range(steps):
            span = pl.ds(sum(depths[:i]), depths[i])
            copies.append(
                [
                    pltpu.make_async_copy(src, dst, sem.at[3 * i + j])
                    for j, (src, dst) in enumerate(
                        (
                            (x_hbm.at[:, span], x_ref.at[:, span]),
                            (wk_hbm.at[span, :], w_ref.at[span, pl.ds(0, width)]),
                            (wv_hbm.at[span, :], w_ref.at[span, pl.ds(width, width)]),
                        )
                    )
                ]
            )
        for group in copies:
            for copy in group:
                copy.start()
        total = None
        for i, group in enumerate(copies):
            for copy in group:
                copy.wait()
            span = slice(sum(depths[:i]), sum(depths[: i + 1]))
            part = mm(x_ref[:, span], w_ref[span, :])
            total = part if total is None else total + part
        fk_ref[...] = feature_map(total[:, :width]).astype(bf16)
        v_ref[...] = total[:, width:].astype(bf16)
        for p in range(width // LANES):
            cols = slice(p * LANES, (p + 1) * LANES)
            state_ref[p * HD : (p + 1) * HD, :] = pack(
                mm(fk_ref[:, cols], v_ref[:, cols], TN)
            ).astype(bf16)

    hbm = pl.BlockSpec(memory_space=pltpu.HBM)
    return call(
        body,
        [
            ((rows, width), bf16),
            ((rows, width), bf16),
            ((width * HD // LANES, LANES), bf16),
        ],
        4 * rows * width * latents.shape[1],
        3 * 1024 * 1024,
        in_specs=[hbm] * 3,
        out_specs=[VMEM] * 3,
        scratch_shapes=[
            pltpu.VMEM(latents.shape, bf16),
            pltpu.VMEM((latents.shape[1], 2 * width), bf16),
            pltpu.SemaphoreType.DMA((3 * steps,)),
        ],
    )(in_hbm(latents), in_hbm(w_key), in_hbm(w_value))


def tri(rows, upper):
    t = lax.broadcasted_iota(jnp.int32, (rows, rows), 0)
    s = lax.broadcasted_iota(jnp.int32, (rows, rows), 1)
    return (t <= s) if upper else (t >= s)


def masked(scores, keep):
    return jnp.where(keep, scores, 0.0).astype(bf16)


def query_local(latents, w_query, fk, v):
    rows, width = fk.shape
    steps = 2
    depth = latents.shape[1] // steps

    def body(x_hbm, wq_ref, fk_ref, v_ref, fq_ref, raw_ref, x_ref, sem):
        spans = [pl.ds(i * depth, depth) for i in range(steps)]
        copies = [
            pltpu.make_async_copy(x_hbm.at[:, span], x_ref.at[:, span], sem.at[i])
            for i, span in enumerate(spans)
        ]
        for copy in copies:
            copy.start()
        total = jnp.zeros((rows, width), f32)
        for copy, span in zip(copies, spans):
            copy.wait()
            total = total + mm(x_ref[:, span], wq_ref[span, :])
        fq_ref[...] = feature_map(total).astype(bf16)
        keep = tri(rows, False)
        for p in range(width // LANES):
            cols = slice(p * LANES, (p + 1) * LANES)
            q, k, val = (fq_ref[:, cols], fk_ref[:, cols], v_ref[:, cols])
            total = None
            for h in (0, 1):
                score = masked(mm(q, one_head(k, h), NT), keep)
                part = mm(score, one_head(val, h))
                total = part if total is None else total + part
            raw_ref[:, cols] = total.astype(bf16)

    return call(
        body,
        [((rows, width), bf16)] * 2,
        2 * rows * width * (latents.shape[1] + 4 * rows),
        3 * 1024 * 1024,
        in_specs=[pl.BlockSpec(memory_space=pltpu.HBM)] + [VMEM] * 3,
        out_specs=[VMEM] * 2,
        scratch_shapes=[pltpu.VMEM(latents.shape, bf16), pltpu.SemaphoreType.DMA((steps,))],
    )(in_hbm(latents), w_query, fk, v)


def upstream_of(grads, w_out, gain):
    rows, width = grads[0].shape

    def body(g0, g1, g2, g3, w_hbm, gain_ref, up_ref, w_ref, sem):
        m = lax.axis_index("mp")
        copies = []
        for k in range(4):
            at = pl.multiple_of(lax.rem(m + 4 - k, 4) * width, LANES)
            copies.append(
                pltpu.make_async_copy(w_hbm.at[:, pl.ds(at, width)], w_ref.at[k], sem.at[k])
            )
        for copy in copies:
            copy.start()
        total = jnp.zeros((rows, width), f32)
        for k, ref in enumerate((g0, g1, g2, g3)):
            copies[k].wait()
            total = total + mm(ref[...], w_ref[k], NT)
        up_ref[...] = (total * gain_ref[...]).astype(bf16)

    return call(
        body,
        [((rows, width), bf16)],
        8 * rows * width * width,
        3 * 1024 * 1024,
        in_specs=[VMEM] * 4 + [pl.BlockSpec(memory_space=pltpu.HBM), VMEM],
        out_specs=[VMEM],
        scratch_shapes=[pltpu.VMEM((4, width, width), bf16), pltpu.SemaphoreType.DMA((4,))],
    )(*grads, in_hbm(w_out), gain)[0]


def normed(mine, got, pair, fq, raw_local, up, gain):
    rows, width = fq.shape
    half = mine.shape[0]

    def body(
        mine_ref,
        got_ref,
        pair_ref,
        fq_ref,
        raw_ref,
        up_ref,
        gain_ref,
        attn_ref,
        draw_ref,
        before_ref,
        after_ref,
        state,
    ):
        whole_state(False, mine_ref, got_ref, pair_ref, state)
        before_ref[...] = state[...].astype(bf16)
        ones = head_ones()
        for p in range(width // LANES):
            cols = slice(p * LANES, (p + 1) * LANES)
            q = fq_ref[:, cols]
            raw = raw_ref[:, cols].astype(f32) + mm(q, unpack(before_ref[p * HD : (p + 1) * HD, :]))
            upstream = up_ref[:, cols].astype(f32)
            square = mm((raw * raw).astype(bf16), ones) * (1.0 / HD)
            cross = mm((raw * upstream).astype(bf16), ones) * (1.0 / HD)
            inv = lax.rsqrt(square + epsilon)
            unit = raw * inv
            attn_ref[:, cols] = (unit * gain_ref[:, cols]).astype(bf16)
            draw = (inv * upstream - inv * inv * unit * cross).astype(bf16)
            draw_ref[:, cols] = draw
            after_ref[p * HD : (p + 1) * HD, :] = pack(mm(q, draw, TN)).astype(bf16)

    return call(
        body,
        [
            ((rows, width), bf16),
            ((rows, width), bf16),
            ((2 * half, LANES), bf16),
            ((2 * half, LANES), bf16),
        ],
        8 * rows * width * LANES,
        2 * 1024 * 1024,
        in_specs=[VMEM] * 7,
        out_specs=[VMEM] * 4,
        scratch_shapes=[pltpu.VMEM((2 * half, LANES), f32)],
    )(mine, got, pair, fq, raw_local, up, gain)


def branch_parts(attn, w_out):
    rows, width = attn.shape

    def body(attn_ref, w_ref, *outs):
        for k, ref in zip((2, 1, 3, 0), outs):
            ref[...] = mm(attn_ref[...], w_ref[:, block_rows(k, width)]).astype(bf16)

    return plain(
        body,
        [((rows, width), bf16, pltpu.HBM)] * 4,
        8 * rows * width * width,
        2 * 1024 * 1024,
        attn,
        w_out,
    )


def local_grads(fq, fk, v, draw, before):
    rows, width = fq.shape

    def body(fq_ref, fk_ref, v_ref, draw_ref, before_ref, dq_ref, dk_ref, dv_ref):
        lower, upper = (tri(rows, False), tri(rows, True))
        for p in range(width // LANES):
            cols = slice(p * LANES, (p + 1) * LANES)
            q, k, val, dr = (fq_ref[:, cols], fk_ref[:, cols], v_ref[:, cols], draw_ref[:, cols])
            dq = mm(dr, unpack(before_ref[p * HD : (p + 1) * HD, :]), NT)
            dk, dv = (None, None)
            for h in (0, 1):
                val_h, k_h, q_h, dr_h = (one_head(a, h) for a in (val, k, q, dr))
                dq = dq + mm(masked(mm(dr, val_h, NT), lower), k_h)
                dk_h = mm(masked(mm(val_h, dr, NT), upper), q_h)
                dv_h = mm(masked(mm(k_h, q, NT), upper), dr_h)
                dk = dk_h if dk is None else dk + dk_h
                dv = dv_h if dv is None else dv + dv_h
            dq_ref[:, cols] = (dq * jnp.minimum(q.astype(f32), 1.0)).astype(bf16)
            dk_ref[:, cols] = dk.astype(bf16)
            dv_ref[:, cols] = dv.astype(bf16)

    return plain(
        body,
        [((rows, width), bf16)] * 3,
        24 * rows * rows * width,
        3 * 1024 * 1024,
        fq,
        fk,
        v,
        draw,
        before,
    )


def block_rows(k, width):
    at = lax.rem(lax.axis_index("mp") + k, 4) * width
    return pl.ds(pl.multiple_of(at, LANES), width)


def block_copies(k, sources, targets, sem, first):
    width = sources[0].shape[1]
    return [
        pltpu.make_async_copy(src.at[block_rows(k, width), :], dst, sem.at[first + i])
        for i, (src, dst) in enumerate(zip(sources, targets))
    ]


def weight_blocks(k, weights):
    width = weights[0].shape[1]

    def body(*refs):
        copies = block_copies(k, refs[:3], refs[3:6], refs[6], 0)
        for copy in copies:
            copy.start()
        for copy in copies:
            copy.wait()

    return call(
        body,
        [((width, width), bf16)] * 3,
        1,
        1024 * 1024,
        in_specs=[pl.BlockSpec(memory_space=pltpu.HBM)] * 3,
        out_specs=[VMEM] * 3,
        scratch_shapes=[pltpu.SemaphoreType.DMA((3,))],
    )(*(in_hbm(w) for w in weights))


def first_part(mine, got, pair, fk, v, dq, dk, dv, blocks):
    rows, width = fk.shape
    half = mine.shape[0]

    def body(
        mine_ref,
        got_ref,
        pair_ref,
        fk_ref,
        v_ref,
        dq_ref,
        dkl_ref,
        dvl_ref,
        wq_ref,
        wk_ref,
        wv_ref,
        dk_ref,
        dv_ref,
        part_ref,
        state,
    ):
        whole_state(True, mine_ref, got_ref, pair_ref, state)
        for p in range(width // LANES):
            cols = slice(p * LANES, (p + 1) * LANES)
            after = unpack(state[p * HD : (p + 1) * HD, :].astype(bf16))
            k = fk_ref[:, cols]
            dk = dkl_ref[:, cols].astype(f32) + mm(v_ref[:, cols], after, NT)
            dk_ref[:, cols] = (dk * jnp.minimum(k.astype(f32), 1.0)).astype(bf16)
            dv_ref[:, cols] = (dvl_ref[:, cols].astype(f32) + mm(k, after)).astype(bf16)
        total = mm(dq_ref[...], wq_ref[...], NT)
        total = total + mm(dk_ref[...], wk_ref[...], NT)
        part_ref[...] = (total + mm(dv_ref[...], wv_ref[...], NT)).astype(bf16)

    return call(
        body,
        [((rows, width), bf16)] * 3,
        6 * rows * width * width,
        2 * 1024 * 1024,
        in_specs=[VMEM] * 11,
        out_specs=[VMEM] * 3,
        scratch_shapes=[pltpu.VMEM((2 * half, LANES), f32)],
    )(mine, got, pair, fk, v, dq, dk, dv, *blocks)


def other_parts(which, dq, dk, dv, weights):
    rows, width = dq.shape
    count = len(which)

    def body(dq_ref, dk_ref, dv_ref, wq_hbm, wk_hbm, wv_hbm, *refs):
        outs, blocks, sem = (refs[:count], refs[count], refs[count + 1])
        copies = [
            block_copies(
                k, (wq_hbm, wk_hbm, wv_hbm), [blocks.at[3 * i + j] for j in range(3)], sem, 3 * i
            )
            for i, k in enumerate(which)
        ]
        for group in copies:
            for copy in group:
                copy.start()
        for i, (group, ref) in enumerate(zip(copies, outs)):
            for copy in group:
                copy.wait()
            total = None
            for j, grad_ref in enumerate((dq_ref, dk_ref, dv_ref)):
                part = mm(grad_ref[...], blocks[3 * i + j], NT)
                total = part if total is None else total + part
            ref[...] = total.astype(bf16)

    hbm = pl.BlockSpec(memory_space=pltpu.HBM)
    return call(
        body,
        [((rows, width), bf16)] * count,
        6 * rows * width * width * count,
        1024 * 1024 * count,
        in_specs=[VMEM] * 3 + [hbm] * 3,
        out_specs=[VMEM] * count,
        scratch_shapes=[
            pltpu.VMEM((3 * count, width, width), bf16),
            pltpu.SemaphoreType.DMA((3 * count,)),
        ],
    )(dq, dk, dv, *(in_hbm(w) for w in weights))


def add_up(parts):
    total = parts[0].astype(f32)
    for part in parts[1:]:
        total = total + part.astype(f32)
    return total.astype(bf16)


def to_owner(part, k):
    return lax.ppermute(part, "mp", shifts(4, k))


def hold(x, anchor):
    return lax.optimization_barrier((x, anchor))[0]


def per_device(latents, w_query, w_key, w_value, w_out, head_gain, grad_out):
    gain = head_gain.reshape(1, -1)
    fk, v, state = key_value(latents, w_key, w_value)
    pair = swap(state)
    grad1 = to_owner(hold(grad_out, state), 1)
    chip = pair_sum(state, pair)
    got = y_gather(False, chip)
    grad_held = hold(grad_out, chip)
    grads = [grad_out, grad1] + [to_owner(grad_held, k) for k in (2, 3)]
    planes = plane_sums(False, chip, got)
    fq, raw_local = query_local(hold(latents, planes), w_query, fk, v)
    up = upstream_of(grads, w_out, gain)
    planes = plane_exchange(planes)
    mine = before_chip(False, planes)
    got = swap(mine)
    attn, draw, before, state = normed(mine, got, pair, fq, raw_local, up, gain)
    weights = (w_query, w_key, w_value)
    blocks = weight_blocks(2, (hold(w_query, state), w_key, w_value))
    pair = swap(state)
    chip = pair_sum(state, pair)
    got = y_gather(True, chip)
    b2, b1, b3, b0 = branch_parts(hold(attn, chip), w_out)
    planes = plane_sums(True, chip, got)
    b2, b1, b3 = (hold(b, planes) for b in (b2, b1, b3))
    branch = [b0, to_owner(b2, 2), to_owner(b1, 1), to_owner(b3, 3)]
    dq, dk_local, dv_local = local_grads(fq, fk, v, hold(draw, planes), before)
    planes = plane_exchange(planes)
    mine = before_chip(True, planes)
    got = swap(mine)
    dk, dv, l2 = first_part(mine, got, pair, fk, v, dq, dk_local, dv_local, blocks)
    l2 = to_owner(l2, 2)
    l1, l3 = other_parts((1, 3), dq, dk, dv, weights)
    l1, l3 = (to_owner(l1, 1), to_owner(l3, 3))
    (l0,) = other_parts((0,), dq, dk, dv, weights)
    return (add_up(branch), add_up([l0, l2, l1, l3]))


def solution(mesh):
    split = Mesh(mesh.devices.reshape(8, 4, 2, mesh.shape["mp"]), (*SEQ, "mp"))
    in_specs = (
        P(SEQ, None),
        P(None, "mp"),
        P(None, "mp"),
        P(None, "mp"),
        P("mp", None),
        P("mp"),
        P(SEQ, "mp"),
    )
    out_specs = (P(SEQ, "mp"), P(SEQ, "mp"))
    return jax.shard_map(
        per_device, mesh=split, in_specs=in_specs, out_specs=out_specs, check_vma=False
    )
```

```python
import jax
import jax.numpy as jnp
from jax import lax
from jax.experimental import pallas as pl
from jax.experimental.pallas import tpu as pltpu
from jax.sharding import Mesh
from jax.sharding import PartitionSpec as P


HD = 64
LANES = 128
SEQ = ("seq_0", "seq_1", "seq_2")
SWAP = [(0, 1), (1, 0)]
epsilon = 1e-06
f32, bf16 = (jnp.float32, jnp.bfloat16)
NT = (((1,), (1,)), ((), ()))
TN = (((0,), (0,)), ((), ()))
VMEM = pl.BlockSpec(memory_space=pltpu.VMEM)


def shifts(count, step):
    return [(i, (i + step) % count) for i in range(count)]


def mm(a, b, contract=(((1,), (0,)), ((), ()))):
    return lax.dot_general(a, b, contract, preferred_element_type=f32)


def in_hbm(x):
    return pltpu.with_memory_space_constraint(x, pltpu.HBM)


def shape_of(shape, kind, where=pltpu.VMEM):
    return where(shape, kind)


def call(body, outs, flops, moved, **extra):
    return pl.pallas_call(
        body,
        out_shape=[shape_of(*out) for out in outs],
        cost_estimate=pl.CostEstimate(flops=flops, bytes_accessed=moved, transcendentals=0),
        compiler_params=pltpu.CompilerParams(vmem_limit_bytes=20 * 1024 * 1024),
        **extra,
    )


def plain(body, outs, flops, moved, *args):
    return call(
        body, outs, flops, moved, in_specs=[VMEM] * len(args), out_specs=[VMEM] * len(outs)
    )(*args)


def feature_map(u):
    return jnp.where(u > 0, u + 1.0, jnp.exp(jnp.minimum(u, 0.0)))


def low_lanes(shape):
    return lax.broadcasted_iota(jnp.int32, shape, len(shape) - 1) < HD


def one_head(x, head):
    low = low_lanes(x.shape)
    keep = low if head == 0 else jnp.logical_not(low)
    return jnp.where(keep, x, jnp.zeros_like(x))


def pack(full):
    return jnp.where(low_lanes((HD, LANES)), full[:HD], full[HD:])


def unpack(rows):
    low = low_lanes((HD, LANES))
    zero = jnp.zeros_like(rows)
    return jnp.concatenate([jnp.where(low, rows, zero), jnp.where(low, zero, rows)], axis=0)


def head_ones():
    r = lax.broadcasted_iota(jnp.int32, (LANES, LANES), 0) < HD
    c = lax.broadcasted_iota(jnp.int32, (LANES, LANES), 1) < HD
    return jnp.where(r == c, 1.0, 0.0).astype(bf16)


def half_at(other, half):
    side = lax.axis_index("seq_2")
    side = 1 - side if other else side
    return pl.ds(pl.multiple_of(side * half, 16), half)


def whole_state(later, mine_ref, got_ref, pair_ref, state_ref):
    half = mine_ref.shape[0]
    last = lax.axis_index("seq_2") == (0 if later else 1)
    state_ref[half_at(False, half), :] = mine_ref[...].astype(f32)
    state_ref[half_at(True, half), :] = got_ref[...].astype(f32)
    state_ref[...] += jnp.where(last, pair_ref[...].astype(f32), 0.0)


def pair_sum(state, pair):
    half = state.shape[0] // 2

    def body(state_ref, pair_ref, chip_ref):
        own = half_at(False, half)
        chip_ref[...] = (state_ref[own, :].astype(f32) + pair_ref[own, :].astype(f32)).astype(bf16)

    return plain(body, [((half, LANES), bf16)], 1, half * 1024, state, pair)[0]


def plane_sums(later, chip, got):
    half = chip.shape[0]

    def body(chip_ref, g1, g2, g3, planes_ref):
        y = lax.axis_index("seq_1")
        y = 3 - y if later else y
        total = chip_ref[...].astype(f32)
        inside = jnp.zeros_like(total)
        for k, ref in ((1, g1), (2, g2), (3, g3)):
            piece = ref[...].astype(f32)
            total = total + piece
            inside = inside + jnp.where(y >= k, piece, 0.0)
        planes_ref[...] = jnp.broadcast_to(total.astype(bf16)[None], planes_ref.shape)
        planes_ref[pl.ds(lax.axis_index("seq_0"), 1)] = inside.astype(bf16)[None]

    outs = [((8, half, LANES), bf16, pltpu.HBM)]
    return plain(body, outs, 1, half * 4096, chip, *got)[0]


def before_chip(later, planes):
    half = planes.shape[1]

    def body(planes_ref, send_ref):
        z = lax.axis_index("seq_0")
        total = jnp.zeros((half, LANES), f32)
        for k in range(8):
            take = (z <= k) if later else (z >= k)
            total = total + jnp.where(take, planes_ref[k].astype(f32), 0.0)
        send_ref[...] = total.astype(bf16)

    return plain(body, [((half, LANES), bf16)], 1, half * 4096, planes)[0]


def plane_exchange(planes):
    return lax.all_to_all(planes, "seq_0", 0, 0, tiled=True)


def swap(x):
    return lax.ppermute(x, "seq_2", SWAP)


def y_gather(later, chip):
    got = []
    for k in (2, 1, 3):
        got.append(lax.ppermute(chip, "seq_1", shifts(4, -k if later else k)))
    return got[1], got[0], got[2]


def key_value(latents, w_key, w_value):
    rows, width = (latents.shape[0], w_key.shape[1])
    depths = [latents.shape[1] // 12 * part for part in (4, 4, 3, 1)]
    steps = len(depths)

    def body(x_hbm, wk_hbm, wv_hbm, fk_ref, v_ref, state_ref, x_ref, w_ref, sem):
        copies = []
        for i in range(steps):
            span = pl.ds(sum(depths[:i]), depths[i])
            copies.append(
                [
                    pltpu.make_async_copy(src, dst, sem.at[3 * i + j])
                    for j, (src, dst) in enumerate(
                        (
                            (x_hbm.at[:, span], x_ref.at[:, span]),
                            (wk_hbm.at[span, :], w_ref.at[span, pl.ds(0, width)]),
                            (wv_hbm.at[span, :], w_ref.at[span, pl.ds(width, width)]),
                        )
                    )
                ]
            )
        for group in copies:
            for copy in group:
                copy.start()
        total = None
        for i, group in enumerate(copies):
            for copy in group:
                copy.wait()
            span = slice(sum(depths[:i]), sum(depths[: i + 1]))
            part = mm(x_ref[:, span], w_ref[span, :])
            total = part if total is None else total + part
        fk_ref[...] = feature_map(total[:, :width]).astype(bf16)
        v_ref[...] = total[:, width:].astype(bf16)
        for p in range(width // LANES):
            cols = slice(p * LANES, (p + 1) * LANES)
            state_ref[p * HD : (p + 1) * HD, :] = pack(
                mm(fk_ref[:, cols], v_ref[:, cols], TN)
            ).astype(bf16)

    hbm = pl.BlockSpec(memory_space=pltpu.HBM)
    return call(
        body,
        [
            ((rows, width), bf16),
            ((rows, width), bf16),
            ((width * HD // LANES, LANES), bf16),
        ],
        4 * rows * width * latents.shape[1],
        3 * 1024 * 1024,
        in_specs=[hbm] * 3,
        out_specs=[VMEM] * 3,
        scratch_shapes=[
            pltpu.VMEM(latents.shape, bf16),
            pltpu.VMEM((latents.shape[1], 2 * width), bf16),
            pltpu.SemaphoreType.DMA((3 * steps,)),
        ],
    )(in_hbm(latents), in_hbm(w_key), in_hbm(w_value))


def tri(rows, upper):
    t = lax.broadcasted_iota(jnp.int32, (rows, rows), 0)
    s = lax.broadcasted_iota(jnp.int32, (rows, rows), 1)
    return (t <= s) if upper else (t >= s)


def masked(scores, keep):
    return jnp.where(keep, scores, 0.0).astype(bf16)


def query_local(latents, w_query, fk, v):
    rows, width = fk.shape
    steps = 2
    depth = latents.shape[1] // steps

    def body(x_hbm, wq_ref, fk_ref, v_ref, fq_ref, raw_ref, x_ref, sem):
        spans = [pl.ds(i * depth, depth) for i in range(steps)]
        copies = [
            pltpu.make_async_copy(x_hbm.at[:, span], x_ref.at[:, span], sem.at[i])
            for i, span in enumerate(spans)
        ]
        for copy in copies:
            copy.start()
        total = jnp.zeros((rows, width), f32)
        for copy, span in zip(copies, spans):
            copy.wait()
            total = total + mm(x_ref[:, span], wq_ref[span, :])
        fq_ref[...] = feature_map(total).astype(bf16)
        keep = tri(rows, False)
        for p in range(width // LANES):
            cols = slice(p * LANES, (p + 1) * LANES)
            q, k, val = (fq_ref[:, cols], fk_ref[:, cols], v_ref[:, cols])
            total = None
            for h in (0, 1):
                score = masked(mm(q, one_head(k, h), NT), keep)
                part = mm(score, one_head(val, h))
                total = part if total is None else total + part
            raw_ref[:, cols] = total.astype(bf16)

    return call(
        body,
        [((rows, width), bf16)] * 2,
        2 * rows * width * (latents.shape[1] + 4 * rows),
        3 * 1024 * 1024,
        in_specs=[pl.BlockSpec(memory_space=pltpu.HBM)] + [VMEM] * 3,
        out_specs=[VMEM] * 2,
        scratch_shapes=[pltpu.VMEM(latents.shape, bf16), pltpu.SemaphoreType.DMA((steps,))],
    )(in_hbm(latents), w_query, fk, v)


def upstream_of(grads, w_out, gain):
    rows, width = grads[0].shape

    def body(g0, g1, g2, g3, w_hbm, gain_ref, up_ref, w_ref, sem):
        m = lax.axis_index("mp")
        copies = []
        for k in range(4):
            at = pl.multiple_of(lax.rem(m + 4 - k, 4) * width, LANES)
            copies.append(
                pltpu.make_async_copy(w_hbm.at[:, pl.ds(at, width)], w_ref.at[k], sem.at[k])
            )
        for copy in copies:
            copy.start()
        total = jnp.zeros((rows, width), f32)
        for k, ref in enumerate((g0, g1, g2, g3)):
            copies[k].wait()
            total = total + mm(ref[...], w_ref[k], NT)
        up_ref[...] = (total * gain_ref[...]).astype(bf16)

    return call(
        body,
        [((rows, width), bf16)],
        8 * rows * width * width,
        3 * 1024 * 1024,
        in_specs=[VMEM] * 4 + [pl.BlockSpec(memory_space=pltpu.HBM), VMEM],
        out_specs=[VMEM],
        scratch_shapes=[pltpu.VMEM((4, width, width), bf16), pltpu.SemaphoreType.DMA((4,))],
    )(*grads, in_hbm(w_out), gain)[0]


def normed(mine, got, pair, fq, raw_local, up, gain):
    rows, width = fq.shape
    half = mine.shape[0]

    def body(
        mine_ref,
        got_ref,
        pair_ref,
        fq_ref,
        raw_ref,
        up_ref,
        gain_ref,
        attn_ref,
        draw_ref,
        before_ref,
        after_ref,
        state,
    ):
        whole_state(False, mine_ref, got_ref, pair_ref, state)
        before_ref[...] = state[...].astype(bf16)
        ones = head_ones()
        for p in range(width // LANES):
            cols = slice(p * LANES, (p + 1) * LANES)
            q = fq_ref[:, cols]
            raw = raw_ref[:, cols].astype(f32) + mm(q, unpack(before_ref[p * HD : (p + 1) * HD, :]))
            upstream = up_ref[:, cols].astype(f32)
            square = mm((raw * raw).astype(bf16), ones) * (1.0 / HD)
            cross = mm((raw * upstream).astype(bf16), ones) * (1.0 / HD)
            inv = lax.rsqrt(square + epsilon)
            unit = raw * inv
            attn_ref[:, cols] = (unit * gain_ref[:, cols]).astype(bf16)
            draw = (inv * upstream - inv * inv * unit * cross).astype(bf16)
            draw_ref[:, cols] = draw
            after_ref[p * HD : (p + 1) * HD, :] = pack(mm(q, draw, TN)).astype(bf16)

    return call(
        body,
        [
            ((rows, width), bf16),
            ((rows, width), bf16),
            ((2 * half, LANES), bf16),
            ((2 * half, LANES), bf16),
        ],
        8 * rows * width * LANES,
        2 * 1024 * 1024,
        in_specs=[VMEM] * 7,
        out_specs=[VMEM] * 4,
        scratch_shapes=[pltpu.VMEM((2 * half, LANES), f32)],
    )(mine, got, pair, fq, raw_local, up, gain)


def branch_parts(attn, w_out, weights):
    rows, width = attn.shape

    def body(attn_ref, w_ref, wq_hbm, wk_hbm, wv_hbm, *refs):
        outs, blocks, sem = (refs[:4], refs[4:7], refs[7])
        copies = block_copies(2, (wq_hbm, wk_hbm, wv_hbm), blocks, sem, 0)
        for copy in copies:
            copy.start()
        for k, ref in zip((2, 1, 3, 0), outs):
            ref[...] = mm(attn_ref[...], w_ref[:, block_rows(k, width)]).astype(bf16)
        for copy in copies:
            copy.wait()

    hbm = pl.BlockSpec(memory_space=pltpu.HBM)
    return call(
        body,
        [((rows, width), bf16, pltpu.HBM)] * 4 + [((width, width), bf16)] * 3,
        8 * rows * width * width,
        3 * 1024 * 1024,
        in_specs=[VMEM] * 2 + [hbm] * 3,
        out_specs=[VMEM] * 7,
        scratch_shapes=[pltpu.SemaphoreType.DMA((3,))],
    )(attn, w_out, *(in_hbm(w) for w in weights))


def local_values(fq, fk, draw):
    rows, width = fq.shape

    def body(fq_ref, fk_ref, draw_ref, dv_ref):
        upper = tri(rows, True)
        for p in range(width // LANES):
            cols = slice(p * LANES, (p + 1) * LANES)
            q, k, dr = (fq_ref[:, cols], fk_ref[:, cols], draw_ref[:, cols])
            dv = None
            for h in (0, 1):
                part = mm(masked(mm(one_head(k, h), q, NT), upper), one_head(dr, h))
                dv = part if dv is None else dv + part
            dv_ref[:, cols] = dv.astype(bf16)

    outs = [((rows, width), bf16)]
    return plain(body, outs, 8 * rows * rows * width, 1024 * 1024, fq, fk, draw)[0]


def local_grads(fq, fk, v, draw, before):
    rows, width = fq.shape

    def body(fq_ref, fk_ref, v_ref, draw_ref, before_ref, dq_ref, dk_ref):
        lower, upper = (tri(rows, False), tri(rows, True))
        for p in range(width // LANES):
            cols = slice(p * LANES, (p + 1) * LANES)
            q, k, val, dr = (fq_ref[:, cols], fk_ref[:, cols], v_ref[:, cols], draw_ref[:, cols])
            dq = mm(dr, unpack(before_ref[p * HD : (p + 1) * HD, :]), NT)
            dk = None
            for h in (0, 1):
                val_h, k_h, q_h = (one_head(a, h) for a in (val, k, q))
                dq = dq + mm(masked(mm(dr, val_h, NT), lower), k_h)
                dk_h = mm(masked(mm(val_h, dr, NT), upper), q_h)
                dk = dk_h if dk is None else dk + dk_h
            dq_ref[:, cols] = (dq * jnp.minimum(q.astype(f32), 1.0)).astype(bf16)
            dk_ref[:, cols] = dk.astype(bf16)

    return plain(
        body,
        [((rows, width), bf16)] * 2,
        16 * rows * rows * width,
        2 * 1024 * 1024,
        fq,
        fk,
        v,
        draw,
        before,
    )


def block_rows(k, width):
    at = lax.rem(lax.axis_index("mp") + k, 4) * width
    return pl.ds(pl.multiple_of(at, LANES), width)


def block_copies(k, sources, targets, sem, first):
    width = sources[0].shape[1]
    return [
        pltpu.make_async_copy(src.at[block_rows(k, width), :], dst, sem.at[first + i])
        for i, (src, dst) in enumerate(zip(sources, targets))
    ]


def first_part(mine, got, pair, fk, v, dq, dk, dv, blocks):
    rows, width = fk.shape
    half = mine.shape[0]

    def body(
        mine_ref,
        got_ref,
        pair_ref,
        fk_ref,
        v_ref,
        dq_ref,
        dkl_ref,
        dvl_ref,
        wq_ref,
        wk_ref,
        wv_ref,
        dk_ref,
        dv_ref,
        part_ref,
        state,
    ):
        whole_state(True, mine_ref, got_ref, pair_ref, state)
        for p in range(width // LANES):
            cols = slice(p * LANES, (p + 1) * LANES)
            after = unpack(state[p * HD : (p + 1) * HD, :].astype(bf16))
            k = fk_ref[:, cols]
            dk = dkl_ref[:, cols].astype(f32) + mm(v_ref[:, cols], after, NT)
            dk_ref[:, cols] = (dk * jnp.minimum(k.astype(f32), 1.0)).astype(bf16)
            dv_ref[:, cols] = (dvl_ref[:, cols].astype(f32) + mm(k, after)).astype(bf16)
        total = mm(dq_ref[...], wq_ref[...], NT)
        total = total + mm(dk_ref[...], wk_ref[...], NT)
        part_ref[...] = (total + mm(dv_ref[...], wv_ref[...], NT)).astype(bf16)

    return call(
        body,
        [((rows, width), bf16)] * 3,
        6 * rows * width * width,
        2 * 1024 * 1024,
        in_specs=[VMEM] * 11,
        out_specs=[VMEM] * 3,
        scratch_shapes=[pltpu.VMEM((2 * half, LANES), f32)],
    )(mine, got, pair, fk, v, dq, dk, dv, *blocks)


def other_parts(which, dq, dk, dv, weights):
    rows, width = dq.shape
    count = len(which)

    def body(dq_ref, dk_ref, dv_ref, wq_hbm, wk_hbm, wv_hbm, *refs):
        outs, blocks, sem = (refs[:count], refs[count], refs[count + 1])
        copies = [
            block_copies(
                k, (wq_hbm, wk_hbm, wv_hbm), [blocks.at[3 * i + j] for j in range(3)], sem, 3 * i
            )
            for i, k in enumerate(which)
        ]
        for group in copies:
            for copy in group:
                copy.start()
        for i, (group, ref) in enumerate(zip(copies, outs)):
            for copy in group:
                copy.wait()
            total = None
            for j, grad_ref in enumerate((dq_ref, dk_ref, dv_ref)):
                part = mm(grad_ref[...], blocks[3 * i + j], NT)
                total = part if total is None else total + part
            ref[...] = total.astype(bf16)

    hbm = pl.BlockSpec(memory_space=pltpu.HBM)
    return call(
        body,
        [((rows, width), bf16)] * count,
        6 * rows * width * width * count,
        1024 * 1024 * count,
        in_specs=[VMEM] * 3 + [hbm] * 3,
        out_specs=[VMEM] * count,
        scratch_shapes=[
            pltpu.VMEM((3 * count, width, width), bf16),
            pltpu.SemaphoreType.DMA((3 * count,)),
        ],
    )(dq, dk, dv, *(in_hbm(w) for w in weights))


def add_up(parts):
    total = parts[0].astype(f32)
    for part in parts[1:]:
        total = total + part.astype(f32)
    return total.astype(bf16)


def to_owner(part, k):
    return lax.ppermute(part, "mp", shifts(4, k))


def hold(x, anchor):
    return lax.optimization_barrier((x, anchor))[0]


def per_device(latents, w_query, w_key, w_value, w_out, head_gain, grad_out):
    gain = head_gain.reshape(1, -1)
    fk, v, state = key_value(latents, w_key, w_value)
    pair = swap(state)
    grad1 = to_owner(hold(grad_out, state), 1)
    chip = pair_sum(state, pair)
    got = y_gather(False, chip)
    grad_held = hold(grad_out, chip)
    grads = [grad_out, grad1] + [to_owner(grad_held, k) for k in (2, 3)]
    planes = plane_sums(False, chip, got)
    fq, raw_local = query_local(hold(latents, planes), w_query, fk, v)
    up = upstream_of(grads, w_out, gain)
    planes = plane_exchange(planes)
    mine = before_chip(False, planes)
    got = swap(mine)
    attn, draw, before, state = normed(mine, got, pair, fq, raw_local, up, gain)
    weights = (w_query, w_key, w_value)
    pair = swap(state)
    dv_local = local_values(fq, fk, draw)
    chip = pair_sum(state, pair)
    got = y_gather(True, chip)
    b2, b1, b3, b0, *blocks = branch_parts(hold(attn, chip), w_out, weights)
    planes = plane_sums(True, chip, got)
    b2, b1, b3 = (hold(b, planes) for b in (b2, b1, b3))
    branch = [b0, to_owner(b2, 2), to_owner(b1, 1), to_owner(b3, 3)]
    dq, dk_local = local_grads(fq, fk, v, hold(draw, planes), before)
    planes = plane_exchange(planes)
    mine = before_chip(True, planes)
    got = swap(mine)
    dk, dv, l2 = first_part(mine, got, pair, fk, v, dq, dk_local, dv_local, blocks)
    l2 = to_owner(l2, 2)
    l1, l3 = other_parts((1, 3), dq, dk, dv, weights)
    l1, l3 = (to_owner(l1, 1), to_owner(l3, 3))
    (l0,) = other_parts((0,), dq, dk, dv, weights)
    return (add_up(branch), add_up([l0, l2, l1, l3]))


def solution(mesh):
    split = Mesh(mesh.devices.reshape(8, 4, 2, mesh.shape["mp"]), (*SEQ, "mp"))
    in_specs = (
        P(SEQ, None),
        P(None, "mp"),
        P(None, "mp"),
        P(None, "mp"),
        P("mp", None),
        P("mp"),
        P(SEQ, "mp"),
    )
    out_specs = (P(SEQ, "mp"), P(SEQ, "mp"))
    return jax.shard_map(
        per_device, mesh=split, in_specs=in_specs, out_specs=out_specs, check_vma=False
    )
```

```python
import jax
import jax.numpy as jnp
from jax import lax
from jax.experimental import pallas as pl
from jax.experimental.pallas import tpu as pltpu
from jax.sharding import Mesh
from jax.sharding import PartitionSpec as P


HD = 64
LANES = 128
SEQ = ("seq_0", "seq_1", "seq_2")
SWAP = [(0, 1), (1, 0)]
epsilon = 1e-06
f32, bf16 = (jnp.float32, jnp.bfloat16)
NT = (((1,), (1,)), ((), ()))
TN = (((0,), (0,)), ((), ()))
VMEM = pl.BlockSpec(memory_space=pltpu.VMEM)


def shifts(count, step):
    return [(i, (i + step) % count) for i in range(count)]


def mm(a, b, contract=(((1,), (0,)), ((), ()))):
    return lax.dot_general(a, b, contract, preferred_element_type=f32)


def in_hbm(x):
    return pltpu.with_memory_space_constraint(x, pltpu.HBM)


def shape_of(shape, kind, where=pltpu.VMEM):
    return where(shape, kind)


def call(body, outs, flops, moved, **extra):
    return pl.pallas_call(
        body,
        out_shape=[shape_of(*out) for out in outs],
        cost_estimate=pl.CostEstimate(flops=flops, bytes_accessed=moved, transcendentals=0),
        compiler_params=pltpu.CompilerParams(vmem_limit_bytes=20 * 1024 * 1024),
        **extra,
    )


def plain(body, outs, flops, moved, *args):
    return call(
        body, outs, flops, moved, in_specs=[VMEM] * len(args), out_specs=[VMEM] * len(outs)
    )(*args)


def feature_map(u):
    return jnp.where(u > 0, u + 1.0, jnp.exp(jnp.minimum(u, 0.0)))


def low_lanes(shape):
    return lax.broadcasted_iota(jnp.int32, shape, len(shape) - 1) < HD


def one_head(x, head):
    low = low_lanes(x.shape)
    keep = low if head == 0 else jnp.logical_not(low)
    return jnp.where(keep, x, jnp.zeros_like(x))


def pack(full):
    return jnp.where(low_lanes((HD, LANES)), full[:HD], full[HD:])


def unpack(rows):
    low = low_lanes((HD, LANES))
    zero = jnp.zeros_like(rows)
    return jnp.concatenate([jnp.where(low, rows, zero), jnp.where(low, zero, rows)], axis=0)


def head_ones():
    r = lax.broadcasted_iota(jnp.int32, (LANES, LANES), 0) < HD
    c = lax.broadcasted_iota(jnp.int32, (LANES, LANES), 1) < HD
    return jnp.where(r == c, 1.0, 0.0).astype(bf16)


def half_at(other, half):
    side = lax.axis_index("seq_2")
    side = 1 - side if other else side
    return pl.ds(pl.multiple_of(side * half, 16), half)


def whole_state(later, mine_ref, got_ref, pair_ref, state_ref):
    half = mine_ref.shape[0]
    last = lax.axis_index("seq_2") == (0 if later else 1)
    state_ref[half_at(False, half), :] = mine_ref[...].astype(f32)
    state_ref[half_at(True, half), :] = got_ref[...].astype(f32)
    state_ref[...] += jnp.where(last, pair_ref[...].astype(f32), 0.0)


def pair_sum(state, pair):
    half = state.shape[0] // 2

    def body(state_ref, pair_ref, chip_ref):
        own = half_at(False, half)
        chip_ref[...] = (state_ref[own, :].astype(f32) + pair_ref[own, :].astype(f32)).astype(bf16)

    return plain(body, [((half, LANES), bf16)], 1, half * 1024, state, pair)[0]


def plane_sums(later, chip, got):
    half = chip.shape[0]

    def body(chip_ref, g1, g2, g3, planes_ref):
        y = lax.axis_index("seq_1")
        y = 3 - y if later else y
        total = chip_ref[...].astype(f32)
        inside = jnp.zeros_like(total)
        for k, ref in ((1, g1), (2, g2), (3, g3)):
            piece = ref[...].astype(f32)
            total = total + piece
            inside = inside + jnp.where(y >= k, piece, 0.0)
        planes_ref[...] = jnp.broadcast_to(total.astype(bf16)[None], planes_ref.shape)
        planes_ref[pl.ds(lax.axis_index("seq_0"), 1)] = inside.astype(bf16)[None]

    outs = [((8, half, LANES), bf16, pltpu.HBM)]
    return plain(body, outs, 1, half * 4096, chip, *got)[0]


def before_chip(later, planes):
    half = planes.shape[1]

    def body(planes_ref, send_ref):
        z = lax.axis_index("seq_0")
        total = jnp.zeros((half, LANES), f32)
        for k in range(8):
            take = (z <= k) if later else (z >= k)
            total = total + jnp.where(take, planes_ref[k].astype(f32), 0.0)
        send_ref[...] = total.astype(bf16)

    return plain(body, [((half, LANES), bf16)], 1, half * 4096, planes)[0]


def plane_exchange(planes):
    return lax.all_to_all(planes, "seq_0", 0, 0, tiled=True)


def swap(x):
    return lax.ppermute(x, "seq_2", SWAP)


def y_gather(later, chip):
    got = []
    for k in (2, 1, 3):
        got.append(lax.ppermute(chip, "seq_1", shifts(4, -k if later else k)))
    return got[1], got[0], got[2]


def key_value(latents, w_key, w_value):
    rows, width = (latents.shape[0], w_key.shape[1])
    depths = [latents.shape[1] // 12 * part for part in (4, 4, 3, 1)]
    steps = len(depths)

    def body(x_hbm, wk_hbm, wv_hbm, fk_ref, v_ref, state_ref, x_ref, w_ref, sem):
        copies = []
        for i in range(steps):
            span = pl.ds(sum(depths[:i]), depths[i])
            copies.append(
                [
                    pltpu.make_async_copy(src, dst, sem.at[3 * i + j])
                    for j, (src, dst) in enumerate(
                        (
                            (x_hbm.at[:, span], x_ref.at[:, span]),
                            (wk_hbm.at[span, :], w_ref.at[span, pl.ds(0, width)]),
                            (wv_hbm.at[span, :], w_ref.at[span, pl.ds(width, width)]),
                        )
                    )
                ]
            )
        for group in copies:
            for copy in group:
                copy.start()
        total = None
        for i, group in enumerate(copies):
            for copy in group:
                copy.wait()
            span = slice(sum(depths[:i]), sum(depths[: i + 1]))
            part = mm(x_ref[:, span], w_ref[span, :])
            total = part if total is None else total + part
        fk_ref[...] = feature_map(total[:, :width]).astype(bf16)
        v_ref[...] = total[:, width:].astype(bf16)
        for p in range(width // LANES):
            cols = slice(p * LANES, (p + 1) * LANES)
            state_ref[p * HD : (p + 1) * HD, :] = pack(
                mm(fk_ref[:, cols], v_ref[:, cols], TN)
            ).astype(bf16)

    hbm = pl.BlockSpec(memory_space=pltpu.HBM)
    return call(
        body,
        [
            ((rows, width), bf16),
            ((rows, width), bf16),
            ((width * HD // LANES, LANES), bf16),
        ],
        4 * rows * width * latents.shape[1],
        3 * 1024 * 1024,
        in_specs=[hbm] * 3,
        out_specs=[VMEM] * 3,
        scratch_shapes=[
            pltpu.VMEM(latents.shape, bf16),
            pltpu.VMEM((latents.shape[1], 2 * width), bf16),
            pltpu.SemaphoreType.DMA((3 * steps,)),
        ],
    )(in_hbm(latents), in_hbm(w_key), in_hbm(w_value))


def tri(rows, upper):
    t = lax.broadcasted_iota(jnp.int32, (rows, rows), 0)
    s = lax.broadcasted_iota(jnp.int32, (rows, rows), 1)
    return (t <= s) if upper else (t >= s)


def masked(scores, keep):
    return jnp.where(keep, scores, 0.0).astype(bf16)


def query_local(latents, w_query, fk, v):
    rows, width = fk.shape
    steps = 2
    depth = latents.shape[1] // steps

    def body(x_hbm, wq_ref, fk_ref, v_ref, fq_ref, raw_ref, x_ref, sem):
        spans = [pl.ds(i * depth, depth) for i in range(steps)]
        copies = [
            pltpu.make_async_copy(x_hbm.at[:, span], x_ref.at[:, span], sem.at[i])
            for i, span in enumerate(spans)
        ]
        for copy in copies:
            copy.start()
        total = jnp.zeros((rows, width), f32)
        for copy, span in zip(copies, spans):
            copy.wait()
            total = total + mm(x_ref[:, span], wq_ref[span, :])
        fq_ref[...] = feature_map(total).astype(bf16)
        keep = tri(rows, False)
        for p in range(width // LANES):
            cols = slice(p * LANES, (p + 1) * LANES)
            q, k, val = (fq_ref[:, cols], fk_ref[:, cols], v_ref[:, cols])
            total = None
            for h in (0, 1):
                score = masked(mm(q, one_head(k, h), NT), keep)
                part = mm(score, one_head(val, h))
                total = part if total is None else total + part
            raw_ref[:, cols] = total.astype(bf16)

    return call(
        body,
        [((rows, width), bf16)] * 2,
        2 * rows * width * (latents.shape[1] + 4 * rows),
        3 * 1024 * 1024,
        in_specs=[pl.BlockSpec(memory_space=pltpu.HBM)] + [VMEM] * 3,
        out_specs=[VMEM] * 2,
        scratch_shapes=[pltpu.VMEM(latents.shape, bf16), pltpu.SemaphoreType.DMA((steps,))],
    )(in_hbm(latents), w_query, fk, v)


def upstream_of(grads, w_out, gain):
    rows, width = grads[0].shape

    def body(g0, g1, g2, g3, w_hbm, gain_ref, up_ref, w_ref, sem):
        m = lax.axis_index("mp")
        copies = []
        for k in range(4):
            at = pl.multiple_of(lax.rem(m + 4 - k, 4) * width, LANES)
            copies.append(
                pltpu.make_async_copy(w_hbm.at[:, pl.ds(at, width)], w_ref.at[k], sem.at[k])
            )
        for copy in copies:
            copy.start()
        total = jnp.zeros((rows, width), f32)
        for k, ref in enumerate((g0, g1, g2, g3)):
            copies[k].wait()
            total = total + mm(ref[...], w_ref[k], NT)
        up_ref[...] = (total * gain_ref[...]).astype(bf16)

    return call(
        body,
        [((rows, width), bf16)],
        8 * rows * width * width,
        3 * 1024 * 1024,
        in_specs=[VMEM] * 4 + [pl.BlockSpec(memory_space=pltpu.HBM), VMEM],
        out_specs=[VMEM],
        scratch_shapes=[pltpu.VMEM((4, width, width), bf16), pltpu.SemaphoreType.DMA((4,))],
    )(*grads, in_hbm(w_out), gain)[0]


def normed(mine, got, pair, fq, raw_local, up, gain):
    rows, width = fq.shape
    half = mine.shape[0]

    def body(
        mine_ref,
        got_ref,
        pair_ref,
        fq_ref,
        raw_ref,
        up_ref,
        gain_ref,
        attn_ref,
        draw_ref,
        before_ref,
        after_ref,
        state,
    ):
        whole_state(False, mine_ref, got_ref, pair_ref, state)
        before_ref[...] = state[...].astype(bf16)
        ones = head_ones()
        for p in range(width // LANES):
            cols = slice(p * LANES, (p + 1) * LANES)
            q = fq_ref[:, cols]
            raw = raw_ref[:, cols].astype(f32) + mm(q, unpack(before_ref[p * HD : (p + 1) * HD, :]))
            upstream = up_ref[:, cols].astype(f32)
            square = mm((raw * raw).astype(bf16), ones) * (1.0 / HD)
            cross = mm((raw * upstream).astype(bf16), ones) * (1.0 / HD)
            inv = lax.rsqrt(square + epsilon)
            unit = raw * inv
            attn_ref[:, cols] = (unit * gain_ref[:, cols]).astype(bf16)
            draw = (inv * upstream - inv * inv * unit * cross).astype(bf16)
            draw_ref[:, cols] = draw
            after_ref[p * HD : (p + 1) * HD, :] = pack(mm(q, draw, TN)).astype(bf16)

    return call(
        body,
        [
            ((rows, width), bf16),
            ((rows, width), bf16),
            ((2 * half, LANES), bf16),
            ((2 * half, LANES), bf16),
        ],
        8 * rows * width * LANES,
        2 * 1024 * 1024,
        in_specs=[VMEM] * 7,
        out_specs=[VMEM] * 4,
        scratch_shapes=[pltpu.VMEM((2 * half, LANES), f32)],
    )(mine, got, pair, fq, raw_local, up, gain)


def branch_parts(attn, w_out):
    rows, width = attn.shape

    def body(attn_ref, w_ref, *outs):
        for k, ref in zip((2, 1, 3, 0), outs):
            ref[...] = mm(attn_ref[...], w_ref[:, block_rows(k, width)]).astype(bf16)

    return plain(
        body,
        [((rows, width), bf16, pltpu.HBM)] * 4,
        8 * rows * width * width,
        2 * 1024 * 1024,
        attn,
        w_out,
    )


def local_values(fq, fk, draw):
    rows, width = fq.shape

    def body(fq_ref, fk_ref, draw_ref, dv_ref):
        upper = tri(rows, True)
        for p in range(width // LANES):
            cols = slice(p * LANES, (p + 1) * LANES)
            q, k, dr = (fq_ref[:, cols], fk_ref[:, cols], draw_ref[:, cols])
            dv = None
            for h in (0, 1):
                part = mm(masked(mm(one_head(k, h), q, NT), upper), one_head(dr, h))
                dv = part if dv is None else dv + part
            dv_ref[:, cols] = dv.astype(bf16)

    outs = [((rows, width), bf16)]
    return plain(body, outs, 8 * rows * rows * width, 1024 * 1024, fq, fk, draw)[0]


def local_grads(fq, fk, v, draw, before):
    rows, width = fq.shape

    def body(fq_ref, fk_ref, v_ref, draw_ref, before_ref, dq_ref, dk_ref):
        lower, upper = (tri(rows, False), tri(rows, True))
        for p in range(width // LANES):
            cols = slice(p * LANES, (p + 1) * LANES)
            q, k, val, dr = (fq_ref[:, cols], fk_ref[:, cols], v_ref[:, cols], draw_ref[:, cols])
            dq = mm(dr, unpack(before_ref[p * HD : (p + 1) * HD, :]), NT)
            dk = None
            for h in (0, 1):
                val_h, k_h, q_h = (one_head(a, h) for a in (val, k, q))
                dq = dq + mm(masked(mm(dr, val_h, NT), lower), k_h)
                dk_h = mm(masked(mm(val_h, dr, NT), upper), q_h)
                dk = dk_h if dk is None else dk + dk_h
            dq_ref[:, cols] = (dq * jnp.minimum(q.astype(f32), 1.0)).astype(bf16)
            dk_ref[:, cols] = dk.astype(bf16)

    return plain(
        body,
        [((rows, width), bf16)] * 2,
        16 * rows * rows * width,
        2 * 1024 * 1024,
        fq,
        fk,
        v,
        draw,
        before,
    )


def block_rows(k, width):
    at = lax.rem(lax.axis_index("mp") + k, 4) * width
    return pl.ds(pl.multiple_of(at, LANES), width)


def block_copies(k, sources, targets, sem, first):
    width = sources[0].shape[1]
    return [
        pltpu.make_async_copy(src.at[block_rows(k, width), :], dst, sem.at[first + i])
        for i, (src, dst) in enumerate(zip(sources, targets))
    ]


def weight_blocks(which, weights):
    width = weights[0].shape[1]
    count = 3 * len(which)

    def body(*refs):
        sources, targets, sem = (refs[:3], refs[3 : 3 + count], refs[3 + count])
        copies = []
        for i, k in enumerate(which):
            copies += block_copies(k, sources, targets[3 * i : 3 * i + 3], sem, 3 * i)
        for copy in copies:
            copy.start()
        for copy in copies:
            copy.wait()

    return call(
        body,
        [((width, width), bf16)] * count,
        1,
        1024 * 1024,
        in_specs=[pl.BlockSpec(memory_space=pltpu.HBM)] * 3,
        out_specs=[VMEM] * count,
        scratch_shapes=[pltpu.SemaphoreType.DMA((count,))],
    )(*(in_hbm(w) for w in weights))


def first_part(mine, got, pair, fk, v, dq, dk, dv, blocks):
    rows, width = fk.shape
    half = mine.shape[0]

    def body(
        mine_ref,
        got_ref,
        pair_ref,
        fk_ref,
        v_ref,
        dq_ref,
        dkl_ref,
        dvl_ref,
        wq_ref,
        wk_ref,
        wv_ref,
        dk_ref,
        dv_ref,
        upper_ref,
        lower_ref,
        state,
    ):
        whole_state(True, mine_ref, got_ref, pair_ref, state)
        for p in range(width // LANES):
            cols = slice(p * LANES, (p + 1) * LANES)
            after = unpack(state[p * HD : (p + 1) * HD, :].astype(bf16))
            k = fk_ref[:, cols]
            dk = dkl_ref[:, cols].astype(f32) + mm(v_ref[:, cols], after, NT)
            dk_ref[:, cols] = (dk * jnp.minimum(k.astype(f32), 1.0)).astype(bf16)
            dv_ref[:, cols] = (dvl_ref[:, cols].astype(f32) + mm(k, after)).astype(bf16)
        total = mm(dq_ref[...], wq_ref[...], NT)
        total = total + mm(dk_ref[...], wk_ref[...], NT)
        total = (total + mm(dv_ref[...], wv_ref[...], NT)).astype(bf16)
        upper_ref[...] = total[: rows // 2]
        lower_ref[...] = total[rows // 2 :]

    return call(
        body,
        [((rows, width), bf16)] * 2 + [((rows // 2, width), bf16)] * 2,
        6 * rows * width * width,
        2 * 1024 * 1024,
        in_specs=[VMEM] * 11,
        out_specs=[VMEM] * 4,
        scratch_shapes=[pltpu.VMEM((2 * half, LANES), f32)],
    )(mine, got, pair, fk, v, dq, dk, dv, *blocks)


def side_parts(dq, dk, dv, blocks):
    rows, width = dq.shape
    half = rows // 2

    def body(dq_ref, dk_ref, dv_ref, q1, k1, v1, q3, k3, v3, soon1, soon3, late1, late3):
        top, bottom = (slice(0, half), slice(half, rows))
        for weights, soon, late, first in (
            ((q1, k1, v1), soon1, late1, bottom),
            ((q3, k3, v3), soon3, late3, top),
        ):
            total = None
            for grad_ref, w_ref in zip((dq_ref, dk_ref, dv_ref), weights):
                part = mm(grad_ref[...], w_ref[...], NT)
                total = part if total is None else total + part
            soon[...] = total[first].astype(bf16)
            late[...] = total[top if first is bottom else bottom]

    return plain(
        body,
        [((half, width), bf16)] * 2 + [((half, width), f32)] * 2,
        12 * rows * width * width,
        2 * 1024 * 1024,
        dq,
        dk,
        dv,
        *blocks,
    )


def marker(x):
    def body(x_ref, out_ref):
        out_ref[...] = x_ref[:8, :LANES]

    return plain(body, [((8, LANES), x.dtype)], 1, 1024, x)[0]


def relayed(late1, late3, far1, far3, mark):
    half, width = far1.shape

    def body(a, b, c, d, _, out1, out3):
        out1[...] = (a[...] + c[...].astype(f32)).astype(bf16)
        out3[...] = (b[...] + d[...].astype(f32)).astype(bf16)

    outs = [((half, width), bf16)] * 2
    return plain(body, outs, 1, 1024 * 1024, late1, late3, far1, far3, mark)


def finished(own, soon3, late1, soon1, late3):
    half = soon1.shape[0]

    def body(own_ref, s3, l1, s1, l3, out_ref):
        for rows, a, b in ((slice(0, half), s3, l1), (slice(half, 2 * half), s1, l3)):
            total = own_ref[rows, :].astype(f32) + a[...].astype(f32) + b[...].astype(f32)
            out_ref[rows, :] = total.astype(bf16)

    outs = [(own.shape, bf16, pltpu.HBM)]
    return plain(body, outs, 1, 1024 * 1024, own, soon3, late1, soon1, late3)[0]


def own_part(dq, dk, dv, weights):
    rows, width = dq.shape

    def body(dq_ref, dk_ref, dv_ref, wq_hbm, wk_hbm, wv_hbm, out_ref, blocks, sem):
        copies = block_copies(0, (wq_hbm, wk_hbm, wv_hbm), [blocks.at[j] for j in range(3)], sem, 0)
        for copy in copies:
            copy.start()
        total = jnp.zeros((rows, width), f32)
        for j, grad_ref in enumerate((dq_ref, dk_ref, dv_ref)):
            copies[j].wait()
            total = total + mm(grad_ref[...], blocks[j], NT)
        out_ref[...] = total.astype(bf16)

    hbm = pl.BlockSpec(memory_space=pltpu.HBM)
    return call(
        body,
        [((rows, width), bf16)],
        6 * rows * width * width,
        1024 * 1024,
        in_specs=[VMEM] * 3 + [hbm] * 3,
        out_specs=[VMEM],
        scratch_shapes=[
            pltpu.VMEM((3, width, width), bf16),
            pltpu.SemaphoreType.DMA((3,)),
        ],
    )(dq, dk, dv, *(in_hbm(w) for w in weights))[0]


def add_up(parts):
    total = parts[0].astype(f32)
    for part in parts[1:]:
        total = total + part.astype(f32)
    return total.astype(bf16)


def to_owner(part, k):
    return lax.ppermute(part, "mp", shifts(4, k))


def hold(x, anchor):
    return lax.optimization_barrier((x, anchor))[0]


def per_device(latents, w_query, w_key, w_value, w_out, head_gain, grad_out):
    gain = head_gain.reshape(1, -1)
    fk, v, state = key_value(latents, w_key, w_value)
    pair = swap(state)
    grad1 = to_owner(hold(grad_out, state), 1)
    chip = pair_sum(state, pair)
    got = y_gather(False, chip)
    grad_held = hold(grad_out, chip)
    grads = [grad_out, grad1] + [to_owner(grad_held, k) for k in (2, 3)]
    planes = plane_sums(False, chip, got)
    fq, raw_local = query_local(hold(latents, planes), w_query, fk, v)
    up = upstream_of(grads, w_out, gain)
    planes = plane_exchange(planes)
    mine = before_chip(False, planes)
    got = swap(mine)
    weights = (w_query, w_key, w_value)
    blocks = weight_blocks((2,), (hold(w_query, mine), w_key, w_value))
    attn, draw, before, state = normed(mine, got, pair, fq, raw_local, up, gain)
    pair = swap(state)
    dv_local = local_values(fq, fk, draw)
    chip = pair_sum(state, pair)
    got = y_gather(True, chip)
    b2, b1, b3, b0 = branch_parts(hold(attn, chip), w_out)
    planes = plane_sums(True, chip, got)
    b2, b1, b3 = (hold(b, planes) for b in (b2, b1, b3))
    branch = [b0, to_owner(b2, 2), to_owner(b1, 1), to_owner(b3, 3)]
    dq, dk_local = local_grads(fq, fk, v, hold(draw, planes), before)
    planes = plane_exchange(planes)
    mine = before_chip(True, planes)
    got = swap(mine)
    others = weight_blocks((1, 3), (hold(w_query, mine), w_key, w_value))
    dk, dv, up2, down2 = first_part(mine, got, pair, fk, v, dq, dk_local, dv_local, blocks)
    far1, far3 = (to_owner(up2, 1), to_owner(down2, 3))
    soon1, soon3, late1, late3 = side_parts(dq, dk, dv, others)
    soon1, soon3 = (to_owner(soon1, 1), to_owner(soon3, 3))
    mark = marker(late1)
    late1, late3 = relayed(late1, late3, far1, far3, mark)
    late1, late3 = (to_owner(late1, 1), to_owner(late3, 3))
    own = own_part(dq, dk, dv, weights)
    return (add_up(branch), finished(own, soon3, late1, soon1, late3))


def solution(mesh):
    split = Mesh(mesh.devices.reshape(8, 4, 2, mesh.shape["mp"]), (*SEQ, "mp"))
    in_specs = (
        P(SEQ, None),
        P(None, "mp"),
        P(None, "mp"),
        P(None, "mp"),
        P("mp", None),
        P("mp"),
        P(SEQ, "mp"),
    )
    out_specs = (P(SEQ, "mp"), P(SEQ, "mp"))
    return jax.shard_map(
        per_device, mesh=split, in_specs=in_specs, out_specs=out_specs, check_vma=False
    )
```

```python
import jax
import jax.numpy as jnp
from jax import lax
from jax.experimental import pallas as pl
from jax.experimental.pallas import tpu as pltpu
from jax.sharding import Mesh
from jax.sharding import PartitionSpec as P


HD = 64
LANES = 128
SEQ = ("seq_0", "seq_1", "seq_2")
SWAP = [(0, 1), (1, 0)]
epsilon = 1e-06
f32, bf16 = (jnp.float32, jnp.bfloat16)
NT = (((1,), (1,)), ((), ()))
TN = (((0,), (0,)), ((), ()))
VMEM = pl.BlockSpec(memory_space=pltpu.VMEM)


def shifts(count, step):
    return [(i, (i + step) % count) for i in range(count)]


def mm(a, b, contract=(((1,), (0,)), ((), ()))):
    return lax.dot_general(a, b, contract, preferred_element_type=f32)


def in_hbm(x):
    return pltpu.with_memory_space_constraint(x, pltpu.HBM)


def shape_of(shape, kind, where=pltpu.VMEM):
    return where(shape, kind)


def call(body, outs, flops, moved, **extra):
    return pl.pallas_call(
        body,
        out_shape=[shape_of(*out) for out in outs],
        cost_estimate=pl.CostEstimate(flops=flops, bytes_accessed=moved, transcendentals=0),
        compiler_params=pltpu.CompilerParams(vmem_limit_bytes=20 * 1024 * 1024),
        **extra,
    )


def plain(body, outs, flops, moved, *args):
    return call(
        body, outs, flops, moved, in_specs=[VMEM] * len(args), out_specs=[VMEM] * len(outs)
    )(*args)


def feature_map(u):
    return jnp.where(u > 0, u + 1.0, jnp.exp(jnp.minimum(u, 0.0)))


def low_lanes(shape):
    return lax.broadcasted_iota(jnp.int32, shape, len(shape) - 1) < HD


def one_head(x, head):
    low = low_lanes(x.shape)
    keep = low if head == 0 else jnp.logical_not(low)
    return jnp.where(keep, x, jnp.zeros_like(x))


def pack(full):
    return jnp.where(low_lanes((HD, LANES)), full[:HD], full[HD:])


def unpack(rows):
    low = low_lanes((HD, LANES))
    zero = jnp.zeros_like(rows)
    return jnp.concatenate([jnp.where(low, rows, zero), jnp.where(low, zero, rows)], axis=0)


def head_ones():
    r = lax.broadcasted_iota(jnp.int32, (LANES, LANES), 0) < HD
    c = lax.broadcasted_iota(jnp.int32, (LANES, LANES), 1) < HD
    return jnp.where(r == c, 1.0, 0.0).astype(bf16)


def half_at(other, half):
    side = lax.axis_index("seq_2")
    side = 1 - side if other else side
    return pl.ds(pl.multiple_of(side * half, 16), half)


def whole_state(later, mine_ref, got_ref, pair_ref, state_ref):
    half = mine_ref.shape[0]
    last = lax.axis_index("seq_2") == (0 if later else 1)
    state_ref[half_at(False, half), :] = mine_ref[...].astype(f32)
    state_ref[half_at(True, half), :] = got_ref[...].astype(f32)
    state_ref[...] += jnp.where(last, pair_ref[...].astype(f32), 0.0)


def pair_sum(state, pair):
    half = state.shape[0] // 2

    def body(state_ref, pair_ref, chip_ref):
        own = half_at(False, half)
        chip_ref[...] = (state_ref[own, :].astype(f32) + pair_ref[own, :].astype(f32)).astype(bf16)

    return plain(body, [((half, LANES), bf16)], 1, half * 1024, state, pair)[0]


def plane_sums(later, chip, got):
    half = chip.shape[0]

    def body(chip_ref, g1, g2, g3, planes_ref):
        y = lax.axis_index("seq_1")
        y = 3 - y if later else y
        total = chip_ref[...].astype(f32)
        inside = jnp.zeros_like(total)
        for k, ref in ((1, g1), (2, g2), (3, g3)):
            piece = ref[...].astype(f32)
            total = total + piece
            inside = inside + jnp.where(y >= k, piece, 0.0)
        planes_ref[...] = jnp.broadcast_to(total.astype(bf16)[None], planes_ref.shape)
        planes_ref[pl.ds(lax.axis_index("seq_0"), 1)] = inside.astype(bf16)[None]

    outs = [((8, half, LANES), bf16, pltpu.HBM)]
    return plain(body, outs, 1, half * 4096, chip, *got)[0]


def before_chip(later, planes):
    half = planes.shape[1]

    def body(planes_ref, send_ref):
        z = lax.axis_index("seq_0")
        total = jnp.zeros((half, LANES), f32)
        for k in range(8):
            take = (z <= k) if later else (z >= k)
            total = total + jnp.where(take, planes_ref[k].astype(f32), 0.0)
        send_ref[...] = total.astype(bf16)

    return plain(body, [((half, LANES), bf16)], 1, half * 4096, planes)[0]


def plane_exchange(planes):
    return lax.all_to_all(planes, "seq_0", 0, 0, tiled=True)


def swap(x):
    return lax.ppermute(x, "seq_2", SWAP)


def y_gather(later, chip):
    got = []
    for k in (2, 1, 3):
        got.append(lax.ppermute(chip, "seq_1", shifts(4, -k if later else k)))
    return got[1], got[0], got[2]


def key_value(latents, w_key, w_value):
    rows, width = (latents.shape[0], w_key.shape[1])
    depths = [latents.shape[1] // 12 * part for part in (4, 4, 3, 1)]
    steps = len(depths)

    def body(x_hbm, wk_hbm, wv_hbm, fk_ref, v_ref, state_ref, x_ref, w_ref, sem):
        copies = []
        for i in range(steps):
            span = pl.ds(sum(depths[:i]), depths[i])
            copies.append(
                [
                    pltpu.make_async_copy(src, dst, sem.at[3 * i + j])
                    for j, (src, dst) in enumerate(
                        (
                            (x_hbm.at[:, span], x_ref.at[:, span]),
                            (wk_hbm.at[span, :], w_ref.at[span, pl.ds(0, width)]),
                            (wv_hbm.at[span, :], w_ref.at[span, pl.ds(width, width)]),
                        )
                    )
                ]
            )
        for group in copies:
            for copy in group:
                copy.start()
        total = None
        for i, group in enumerate(copies):
            for copy in group:
                copy.wait()
            span = slice(sum(depths[:i]), sum(depths[: i + 1]))
            part = mm(x_ref[:, span], w_ref[span, :])
            total = part if total is None else total + part
        fk_ref[...] = feature_map(total[:, :width]).astype(bf16)
        v_ref[...] = total[:, width:].astype(bf16)
        for p in range(width // LANES):
            cols = slice(p * LANES, (p + 1) * LANES)
            state_ref[p * HD : (p + 1) * HD, :] = pack(
                mm(fk_ref[:, cols], v_ref[:, cols], TN)
            ).astype(bf16)

    hbm = pl.BlockSpec(memory_space=pltpu.HBM)
    return call(
        body,
        [
            ((rows, width), bf16),
            ((rows, width), bf16),
            ((width * HD // LANES, LANES), bf16),
        ],
        4 * rows * width * latents.shape[1],
        3 * 1024 * 1024,
        in_specs=[hbm] * 3,
        out_specs=[VMEM] * 3,
        scratch_shapes=[
            pltpu.VMEM(latents.shape, bf16),
            pltpu.VMEM((latents.shape[1], 2 * width), bf16),
            pltpu.SemaphoreType.DMA((3 * steps,)),
        ],
    )(in_hbm(latents), in_hbm(w_key), in_hbm(w_value))


def tri(rows, upper):
    t = lax.broadcasted_iota(jnp.int32, (rows, rows), 0)
    s = lax.broadcasted_iota(jnp.int32, (rows, rows), 1)
    return (t <= s) if upper else (t >= s)


def masked(scores, keep):
    return jnp.where(keep, scores, 0.0).astype(bf16)


def query_local(latents, w_query, fk, v):
    rows, width = fk.shape
    steps = 2
    depth = latents.shape[1] // steps

    def body(x_hbm, wq_ref, fk_ref, v_ref, fq_ref, raw_ref, x_ref, sem):
        spans = [pl.ds(i * depth, depth) for i in range(steps)]
        copies = [
            pltpu.make_async_copy(x_hbm.at[:, span], x_ref.at[:, span], sem.at[i])
            for i, span in enumerate(spans)
        ]
        for copy in copies:
            copy.start()
        total = jnp.zeros((rows, width), f32)
        for copy, span in zip(copies, spans):
            copy.wait()
            total = total + mm(x_ref[:, span], wq_ref[span, :])
        fq_ref[...] = feature_map(total).astype(bf16)
        keep = tri(rows, False)
        for p in range(width // LANES):
            cols = slice(p * LANES, (p + 1) * LANES)
            q, k, val = (fq_ref[:, cols], fk_ref[:, cols], v_ref[:, cols])
            total = None
            for h in (0, 1):
                score = masked(mm(q, one_head(k, h), NT), keep)
                part = mm(score, one_head(val, h))
                total = part if total is None else total + part
            raw_ref[:, cols] = total.astype(bf16)

    return call(
        body,
        [((rows, width), bf16)] * 2,
        2 * rows * width * (latents.shape[1] + 4 * rows),
        3 * 1024 * 1024,
        in_specs=[pl.BlockSpec(memory_space=pltpu.HBM)] + [VMEM] * 3,
        out_specs=[VMEM] * 2,
        scratch_shapes=[pltpu.VMEM(latents.shape, bf16), pltpu.SemaphoreType.DMA((steps,))],
    )(in_hbm(latents), w_query, fk, v)


def upstream_of(grads, w_out, gain):
    rows, width = grads[0].shape

    def body(g0, g1, g2, g3, w_hbm, gain_ref, up_ref, w_ref, sem):
        m = lax.axis_index("mp")
        copies = []
        for k in range(4):
            at = pl.multiple_of(lax.rem(m + 4 - k, 4) * width, LANES)
            copies.append(
                pltpu.make_async_copy(w_hbm.at[:, pl.ds(at, width)], w_ref.at[k], sem.at[k])
            )
        for copy in copies:
            copy.start()
        total = jnp.zeros((rows, width), f32)
        for k, ref in enumerate((g0, g1, g2, g3)):
            copies[k].wait()
            total = total + mm(ref[...], w_ref[k], NT)
        up_ref[...] = (total * gain_ref[...]).astype(bf16)

    return call(
        body,
        [((rows, width), bf16)],
        8 * rows * width * width,
        3 * 1024 * 1024,
        in_specs=[VMEM] * 4 + [pl.BlockSpec(memory_space=pltpu.HBM), VMEM],
        out_specs=[VMEM],
        scratch_shapes=[pltpu.VMEM((4, width, width), bf16), pltpu.SemaphoreType.DMA((4,))],
    )(*grads, in_hbm(w_out), gain)[0]


def normed(mine, got, pair, fq, raw_local, up, gain):
    rows, width = fq.shape
    half = mine.shape[0]

    def body(
        mine_ref,
        got_ref,
        pair_ref,
        fq_ref,
        raw_ref,
        up_ref,
        gain_ref,
        attn_ref,
        draw_ref,
        before_ref,
        after_ref,
        state,
    ):
        whole_state(False, mine_ref, got_ref, pair_ref, state)
        before_ref[...] = state[...].astype(bf16)
        ones = head_ones()
        for p in range(width // LANES):
            cols = slice(p * LANES, (p + 1) * LANES)
            q = fq_ref[:, cols]
            raw = raw_ref[:, cols].astype(f32) + mm(q, unpack(before_ref[p * HD : (p + 1) * HD, :]))
            upstream = up_ref[:, cols].astype(f32)
            square = mm((raw * raw).astype(bf16), ones) * (1.0 / HD)
            cross = mm((raw * upstream).astype(bf16), ones) * (1.0 / HD)
            inv = lax.rsqrt(square + epsilon)
            unit = raw * inv
            attn_ref[:, cols] = (unit * gain_ref[:, cols]).astype(bf16)
            draw = (inv * upstream - inv * inv * unit * cross).astype(bf16)
            draw_ref[:, cols] = draw
            after_ref[p * HD : (p + 1) * HD, :] = pack(mm(q, draw, TN)).astype(bf16)

    return call(
        body,
        [
            ((rows, width), bf16),
            ((rows, width), bf16),
            ((2 * half, LANES), bf16),
            ((2 * half, LANES), bf16),
        ],
        8 * rows * width * LANES,
        2 * 1024 * 1024,
        in_specs=[VMEM] * 7,
        out_specs=[VMEM] * 4,
        scratch_shapes=[pltpu.VMEM((2 * half, LANES), f32)],
    )(mine, got, pair, fq, raw_local, up, gain)


def branch_parts(attn, w_out):
    rows, width = attn.shape

    def body(attn_ref, w_ref, *outs):
        for k, ref in zip((2, 1, 3, 0), outs):
            ref[...] = mm(attn_ref[...], w_ref[:, block_rows(k, width)]).astype(bf16)

    return plain(
        body,
        [((rows, width), bf16, pltpu.HBM)] * 4,
        8 * rows * width * width,
        2 * 1024 * 1024,
        attn,
        w_out,
    )


def local_values(fq, fk, draw):
    rows, width = fq.shape

    def body(fq_ref, fk_ref, draw_ref, dv_ref):
        upper = tri(rows, True)
        for p in range(width // LANES):
            cols = slice(p * LANES, (p + 1) * LANES)
            q, k, dr = (fq_ref[:, cols], fk_ref[:, cols], draw_ref[:, cols])
            dv = None
            for h in (0, 1):
                part = mm(masked(mm(one_head(k, h), q, NT), upper), one_head(dr, h))
                dv = part if dv is None else dv + part
            dv_ref[:, cols] = dv.astype(bf16)

    outs = [((rows, width), bf16)]
    return plain(body, outs, 8 * rows * rows * width, 1024 * 1024, fq, fk, draw)[0]


def local_grads(fq, fk, v, draw, before):
    rows, width = fq.shape

    def body(fq_ref, fk_ref, v_ref, draw_ref, before_ref, dq_ref, dk_ref):
        lower, upper = (tri(rows, False), tri(rows, True))
        for p in range(width // LANES):
            cols = slice(p * LANES, (p + 1) * LANES)
            q, k, val, dr = (fq_ref[:, cols], fk_ref[:, cols], v_ref[:, cols], draw_ref[:, cols])
            dq = mm(dr, unpack(before_ref[p * HD : (p + 1) * HD, :]), NT)
            dk = None
            for h in (0, 1):
                val_h, k_h, q_h = (one_head(a, h) for a in (val, k, q))
                dq = dq + mm(masked(mm(dr, val_h, NT), lower), k_h)
                dk_h = mm(masked(mm(val_h, dr, NT), upper), q_h)
                dk = dk_h if dk is None else dk + dk_h
            dq_ref[:, cols] = (dq * jnp.minimum(q.astype(f32), 1.0)).astype(bf16)
            dk_ref[:, cols] = dk.astype(bf16)

    return plain(
        body,
        [((rows, width), bf16)] * 2,
        16 * rows * rows * width,
        2 * 1024 * 1024,
        fq,
        fk,
        v,
        draw,
        before,
    )


def block_rows(k, width):
    at = lax.rem(lax.axis_index("mp") + k, 4) * width
    return pl.ds(pl.multiple_of(at, LANES), width)


def block_copies(k, sources, targets, sem, first):
    width = sources[0].shape[1]
    return [
        pltpu.make_async_copy(src.at[block_rows(k, width), :], dst, sem.at[first + i])
        for i, (src, dst) in enumerate(zip(sources, targets))
    ]


def weight_blocks(k, weights):
    width = weights[0].shape[1]

    def body(*refs):
        copies = block_copies(k, refs[:3], refs[3:6], refs[6], 0)
        for copy in copies:
            copy.start()
        for copy in copies:
            copy.wait()

    return call(
        body,
        [((width, width), bf16)] * 3,
        1,
        1024 * 1024,
        in_specs=[pl.BlockSpec(memory_space=pltpu.HBM)] * 3,
        out_specs=[VMEM] * 3,
        scratch_shapes=[pltpu.SemaphoreType.DMA((3,))],
    )(*(in_hbm(w) for w in weights))


def first_part(mine, got, pair, fk, v, dq, dk, dv, blocks):
    rows, width = fk.shape
    half = mine.shape[0]

    def body(
        mine_ref,
        got_ref,
        pair_ref,
        fk_ref,
        v_ref,
        dq_ref,
        dkl_ref,
        dvl_ref,
        wq_ref,
        wk_ref,
        wv_ref,
        dk_ref,
        dv_ref,
        part_ref,
        state,
    ):
        whole_state(True, mine_ref, got_ref, pair_ref, state)
        for p in range(width // LANES):
            cols = slice(p * LANES, (p + 1) * LANES)
            after = unpack(state[p * HD : (p + 1) * HD, :].astype(bf16))
            k = fk_ref[:, cols]
            dk = dkl_ref[:, cols].astype(f32) + mm(v_ref[:, cols], after, NT)
            dk_ref[:, cols] = (dk * jnp.minimum(k.astype(f32), 1.0)).astype(bf16)
            dv_ref[:, cols] = (dvl_ref[:, cols].astype(f32) + mm(k, after)).astype(bf16)
        total = mm(dq_ref[...], wq_ref[...], NT)
        total = total + mm(dk_ref[...], wk_ref[...], NT)
        part_ref[...] = (total + mm(dv_ref[...], wv_ref[...], NT)).astype(bf16)

    return call(
        body,
        [((rows, width), bf16)] * 3,
        6 * rows * width * width,
        2 * 1024 * 1024,
        in_specs=[VMEM] * 11,
        out_specs=[VMEM] * 3,
        scratch_shapes=[pltpu.VMEM((2 * half, LANES), f32)],
    )(mine, got, pair, fk, v, dq, dk, dv, *blocks)


def other_parts(which, dq, dk, dv, weights):
    rows, width = dq.shape
    count = len(which)

    def body(dq_ref, dk_ref, dv_ref, wq_hbm, wk_hbm, wv_hbm, *refs):
        outs, blocks, sem = (refs[:count], refs[count], refs[count + 1])
        copies = [
            block_copies(
                k, (wq_hbm, wk_hbm, wv_hbm), [blocks.at[3 * i + j] for j in range(3)], sem, 3 * i
            )
            for i, k in enumerate(which)
        ]
        for group in copies:
            for copy in group:
                copy.start()
        for i, (group, ref) in enumerate(zip(copies, outs)):
            for copy in group:
                copy.wait()
            total = None
            for j, grad_ref in enumerate((dq_ref, dk_ref, dv_ref)):
                part = mm(grad_ref[...], blocks[3 * i + j], NT)
                total = part if total is None else total + part
            ref[...] = total.astype(bf16)

    hbm = pl.BlockSpec(memory_space=pltpu.HBM)
    return call(
        body,
        [((rows, width), bf16)] * count,
        6 * rows * width * width * count,
        1024 * 1024 * count,
        in_specs=[VMEM] * 3 + [hbm] * 3,
        out_specs=[VMEM] * count,
        scratch_shapes=[
            pltpu.VMEM((3 * count, width, width), bf16),
            pltpu.SemaphoreType.DMA((3 * count,)),
        ],
    )(dq, dk, dv, *(in_hbm(w) for w in weights))


def add_up(parts):
    total = parts[0].astype(f32)
    for part in parts[1:]:
        total = total + part.astype(f32)
    return total.astype(bf16)


def to_owner(part, k):
    return lax.ppermute(part, "mp", shifts(4, k))


def hold(x, anchor):
    return lax.optimization_barrier((x, anchor))[0]


def per_device(latents, w_query, w_key, w_value, w_out, head_gain, grad_out):
    gain = head_gain.reshape(1, -1)
    fk, v, state = key_value(latents, w_key, w_value)
    pair = swap(state)
    grad1 = to_owner(hold(grad_out, state), 1)
    chip = pair_sum(state, pair)
    got = y_gather(False, chip)
    grad_held = hold(grad_out, chip)
    grads = [grad_out, grad1] + [to_owner(grad_held, k) for k in (2, 3)]
    planes = plane_sums(False, chip, got)
    fq, raw_local = query_local(hold(latents, planes), w_query, fk, v)
    up = upstream_of(grads, w_out, gain)
    planes = plane_exchange(planes)
    mine = before_chip(False, planes)
    got = swap(mine)
    weights = (w_query, w_key, w_value)
    blocks = weight_blocks(2, (hold(w_query, mine), w_key, w_value))
    attn, draw, before, state = normed(mine, got, pair, fq, raw_local, up, gain)
    pair = swap(state)
    dv_local = local_values(fq, fk, draw)
    chip = pair_sum(state, pair)
    got = y_gather(True, chip)
    b2, b1, b3, b0 = branch_parts(hold(attn, chip), w_out)
    planes = plane_sums(True, chip, got)
    b2, b1, b3 = (hold(b, planes) for b in (b2, b1, b3))
    branch = [b0, to_owner(b2, 2), to_owner(b1, 1), to_owner(b3, 3)]
    dq, dk_local = local_grads(fq, fk, v, hold(draw, planes), before)
    planes = plane_exchange(planes)
    mine = before_chip(True, planes)
    got = swap(mine)
    dk, dv, l2 = first_part(mine, got, pair, fk, v, dq, dk_local, dv_local, blocks)
    l2 = to_owner(l2, 2)
    l1, l3 = other_parts((1, 3), dq, dk, dv, weights)
    l1, l3 = (to_owner(l1, 1), to_owner(l3, 3))
    (l0,) = other_parts((0,), dq, dk, dv, weights)
    return (add_up(branch), add_up([l0, l2, l1, l3]))


def solution(mesh):
    split = Mesh(mesh.devices.reshape(8, 4, 2, mesh.shape["mp"]), (*SEQ, "mp"))
    in_specs = (
        P(SEQ, None),
        P(None, "mp"),
        P(None, "mp"),
        P(None, "mp"),
        P("mp", None),
        P("mp"),
        P(SEQ, "mp"),
    )
    out_specs = (P(SEQ, "mp"), P(SEQ, "mp"))
    return jax.shard_map(
        per_device, mesh=split, in_specs=in_specs, out_specs=out_specs, check_vma=False
    )
```
